32 devices in a mesh: tile: 4 (over y, x), slab: 8 (over z, core).
Axes of the slice: x: 2, y: 2, z: 4, core: 2. Of those that a mesh axis runs over, the one named last changes fastest.
Arguments:
- raw_stack: bfloat16 [32, 120, 2048], P('slab', None, 'tile'), may hold values from -48 to 48
- shear_offsets: int32 [32], P('slab'), may hold values from 0 to 8
- intersection_widths: int32 [3], replicated, may hold values from 32 to 128
Outputs:
- difference: bfloat16 [128, 32, 2048], P('slab', None, 'tile')
- level_one: bfloat16 [64, 16, 1024], P('slab', None, 'tile')
- level_two: bfloat16 [32, 8, 512], P('slab', None, 'tile')
The draws below stay inside these ranges and needn't reach their ends.
All inputs are finite; a program needn't handle non-finite values.
Results may differ from the reference program's by a relative error of at most 0.003.
Values may be sent and summed in bfloat16 or wider, within the bound.
No kernel may reach another device: no remote copies, remote signals or barrier semaphores. Data moves between devices by JAX's collectives and lax.ppermute only.
A program may use at most 64 MiB of HBM per device.

```python
import math
import jax
import jax.numpy as jnp
from jax import lax

TILE_COLS = 512
STRIP = 6
RADIUS = 4
TILES = 4
SCANS = 32
ROWS = 128
SHEAR_MAX = 8
CAMERA = 120
N_TILE = 4


def draw_shear_offsets(key, part):
    flags = (jnp.arange(SCANS - 1, dtype=jnp.int32) < SHEAR_MAX).astype(jnp.int32)
    mixed = jax.random.permutation(key, flags)
    rising = jnp.cumsum(mixed).astype(jnp.int32)
    return jnp.concatenate([jnp.zeros((1,), jnp.int32), rising])


def block_levels(own_key, extent, split, least, high):
    gain, own = 1.0, jax.random.fold_in(own_key, 6)
    for position, shards_of in split:
        heights = jnp.exp(jax.random.uniform(jax.random.fold_in(own, position), (shards_of,), jnp.float32, least / len(split), high / len(split)))
        gain = gain * jnp.repeat(heights, extent[position] // shards_of).reshape([-1 if axis == position else 1 for axis in range(len(extent))])
    return gain


def bell_draw(rng, dims, width, reach, split=(), kind=jnp.bfloat16):
    drawn = jax.random.normal(rng, dims, jnp.float32) * width
    if len(split) > 0:
        drawn = block_levels(rng, dims, split, -0.22, 0.18) * drawn
    return jnp.clip(drawn, min=-reach, max=reach).astype(kind)


def setup_inputs(seed: int = 0) -> dict:
    seeds = jax.random.split(jax.random.key(seed), 4)
    raw_stack = bell_draw(seeds[0], (SCANS, CAMERA, TILES * TILE_COLS), 8.0, 48.0, ((0, 8), (2, 4)))
    shear_offsets = draw_shear_offsets(jax.random.fold_in(seeds[3], 71), 0)
    intersection_widths = jax.random.randint(seeds[2], (TILES - 1,), TILE_COLS // 16, TILE_COLS // 4 + 1).astype(jnp.int32)
    return dict(raw_stack=raw_stack, shear_offsets=shear_offsets, intersection_widths=intersection_widths)


def gauss_taps(sigma_value, reach_cells):
    entries = [math.exp(-(offset * offset) / (2.0 * sigma_value * sigma_value)) for offset in range(-reach_cells, reach_cells + 1)]
    weight_sum = sum(entries)
    return [entry_value / weight_sum for entry_value in entries]


def binomial_taps():
    return [1.0 / 16.0, 4.0 / 16.0, 6.0 / 16.0, 4.0 / 16.0, 1.0 / 16.0]


def smooth(source, weights, direction, begin_at, length_out, stride):
    result = weights[0] * lax.slice_in_dim(source, begin_at, begin_at + (length_out - 1) * stride + 1, stride, direction)
    for offset in range(1, len(weights)):
        lowest = begin_at + offset
        window = lax.slice_in_dim(source, lowest, lowest + (length_out - 1) * stride + 1, stride, direction)
        result = result + weights[offset] * window
    return result


def pad_scans(source, width_cells):
    return jnp.pad(source, ((0, 0), (width_cells, width_cells), (0, 0)))


def deskew(planes_block, shifts, shear_top, total_rows, margin):
    padded = jnp.pad(planes_block, ((0, 0), (shear_top + margin, shear_top + margin), (0, 0)))

    def place_plane(plane, shift_value):
        return lax.dynamic_slice_in_dim(plane, (shear_top - shift_value).astype(jnp.int32), total_rows + 2 * margin, 0)

    return jax.vmap(place_plane, out_axes=1)(padded, shifts)


def analyse(float_field, row_depth, row_count, lead_rows, coarse_count, tile_index, tile_count, row_keep):
    scan_count = float_field.shape[1]
    columns = float_field.shape[2] - 2 * STRIP

    def gaussian(sigma_value):
        weights = gauss_taps(sigma_value, RADIUS)
        along_rows = smooth(float_field, weights, 0, row_depth - RADIUS, row_count, 1)
        along_scans = smooth(pad_scans(along_rows, RADIUS), weights, 1, 0, scan_count, 1)
        return smooth(along_scans, weights, 2, STRIP - RADIUS, columns, 1)

    difference = (gaussian(1.0) - gaussian(1.6)).astype(jnp.bfloat16)
    binomial = binomial_taps()
    rows_blur = smooth(float_field, binomial, 0, row_depth - lead_rows - 2, coarse_count, 2)
    scans_blur = smooth(pad_scans(rows_blur, 2), binomial, 1, 0, scan_count // 2, 2)
    cols_blur = smooth(scans_blur, binomial, 2, STRIP - 6, columns // 2 + 4, 2)
    col_pos = jnp.arange(columns // 2 + 4, dtype=jnp.int32) * 2 - 4
    col_keep = ((col_pos >= 0) | (tile_index > 0)) & ((col_pos < columns) | (tile_index < tile_count - 1))
    keep_mask = row_keep[:, None, None] & col_keep[None, None, :]
    level_ext = jnp.where(keep_mask, cols_blur, 0.0).astype(jnp.bfloat16)
    return difference, level_ext


def level_two_of(coarse, row_count, columns):
    binomial = binomial_taps()
    coarse_float = coarse.astype(jnp.float32)
    scan_half = coarse_float.shape[1]
    rows_blur = smooth(coarse_float, binomial, 0, 0, row_count, 2)
    scans_blur = smooth(pad_scans(rows_blur, 2), binomial, 1, 0, scan_half // 2, 2)
    return smooth(scans_blur, binomial, 2, 0, columns // 4, 2).astype(jnp.bfloat16)


def reference(raw_stack, shear_offsets, intersection_widths):
    all_cols = N_TILE * TILE_COLS

    def one_tile(tile_index):
        own_start = tile_index * TILE_COLS
        left_width = intersection_widths[jnp.maximum(tile_index - 1, 0)]
        right_width = intersection_widths[jnp.minimum(tile_index, N_TILE - 2)]
        own_cols = lax.dynamic_slice_in_dim(raw_stack, own_start.astype(jnp.int32), TILE_COLS, 2)
        left_start = jnp.maximum(own_start - left_width - STRIP, 0).astype(jnp.int32)
        right_start = jnp.minimum(own_start + TILE_COLS + right_width, all_cols - STRIP).astype(jnp.int32)
        left_cols = lax.dynamic_slice_in_dim(raw_stack, left_start, STRIP, 2)
        right_cols = lax.dynamic_slice_in_dim(raw_stack, right_start, STRIP, 2)
        left_cols = jnp.where(tile_index > 0, left_cols, jnp.zeros_like(left_cols))
        right_cols = jnp.where(tile_index < N_TILE - 1, right_cols, jnp.zeros_like(right_cols))
        joined = jnp.concatenate([left_cols, own_cols, right_cols], axis=2)
        volume = deskew(joined, shear_offsets, SHEAR_MAX, ROWS, 0)
        float_field = jnp.pad(volume.astype(jnp.float32), ((STRIP, STRIP), (0, 0), (0, 0)))
        row_keep = jnp.ones((ROWS // 2,), dtype=bool)
        difference, level_ext = analyse(float_field, STRIP, ROWS, 0, ROWS // 2, tile_index, N_TILE, row_keep)
        level_one = level_ext[:, :, 2:2 + TILE_COLS // 2]
        coarse = jnp.pad(level_ext, ((2, 2), (0, 0), (0, 0)))
        level_two = level_two_of(coarse, ROWS // 4, TILE_COLS)
        return difference, level_one, level_two

    stacked = lax.map(one_tile, jnp.arange(N_TILE, dtype=jnp.int32))

    def lay_out(blocks):
        moved = jnp.moveaxis(blocks, 0, 2)
        return moved.reshape(moved.shape[0], moved.shape[1], moved.shape[2] * moved.shape[3])

    return (lay_out(stacked[0]), lay_out(stacked[1]), lay_out(stacked[2]))
```

```python
import functools
import math

import jax
import jax.numpy as jnp
import ml_dtypes
import numpy as np
from jax import lax
from jax.experimental import pallas as pl
from jax.experimental.pallas import tpu as pltpu
from jax.sharding import PartitionSpec as P

SLAB_ROWS = 16
STRIP = 6
RADIUS = 4
LOW = 6
HIGH = 4
PAIR = 2 * SLAB_ROWS + LOW + HIGH
NEED = SLAB_ROWS + LOW + HIGH
LEVEL = 11
LANE = 128
F32 = jnp.float32
BF16 = jnp.bfloat16


def gauss_taps(sigma_value):
    entries = [math.exp(-(j * j) / (2.0 * sigma_value * sigma_value)) for j in range(-RADIUS, RADIUS + 1)]
    weight_sum = sum(entries)
    return np.array([entry / weight_sum for entry in entries], np.float64)


BINOMIAL = np.array([1.0, 4.0, 6.0, 4.0, 1.0], np.float64) / 16.0


def band(weights, source, target):
    reach = len(weights) // 2
    offset = source[None, :] - target[:, None] + reach
    inside = (offset >= 0) & (offset < len(weights))
    return np.where(inside, weights[np.clip(offset, 0, len(weights) - 1)], 0.0)


def two_parts(table):
    high = table.astype(ml_dtypes.bfloat16)
    return high, (table - high.astype(np.float64)).astype(ml_dtypes.bfloat16)


def row_scan_table(row_band, scan_band, groups):
    rows_out, rows_in = row_band.shape
    scans_out = scan_band.shape[0]
    scans = scan_band.reshape(scans_out, groups, 4)
    table = np.einsum("yr,sgp->ysgrp", row_band, scans)
    table = table.reshape(rows_out * scans_out, groups, rows_in * 4)
    table = np.pad(table, ((0, 0), (0, 0), (0, LANE - rows_in * 4)))
    return table.reshape(rows_out * scans_out, groups * LANE)


def tables(scans, columns):
    row_in = np.arange(NEED) - LOW
    own = np.arange(SLAB_ROWS)
    near = np.arange(16) - 4
    block = np.arange(8)
    rowscan, column = [], []
    half = columns // 2
    window = np.arange(half + 2 * LANE) - LANE
    for sigma in (1.0, 1.6):
        taps = gauss_taps(sigma)
        rowscan += list(two_parts(row_scan_table(band(taps, row_in, own), band(taps, near, block), 4)))
        column += list(two_parts(band(taps, window, np.arange(half)).T))
    level_rows = 2 * np.arange(LEVEL) - 4
    level_scans = 2 * np.arange(scans // 2)
    level = row_scan_table(
        band(BINOMIAL, row_in, level_rows), band(BINOMIAL, np.arange(scans), level_scans), scans // 4
    )
    edge_tile = np.where(np.arange(LANE) < LANE // 2, columns, -LANE) + np.arange(LANE)
    places = np.concatenate([edge_tile, np.arange(columns)])
    edges = np.array([-4, -2, columns, columns + 2])
    targets = np.concatenate([2 * np.arange(columns // 2), edges])
    level_column = np.pad(band(BINOMIAL, places, targets).T, ((0, 0), (0, LANE - 4)))
    two = np.einsum(
        "yr,sp->ysrp",
        band(BINOMIAL, np.arange(LEVEL) - 2, 2 * np.arange(4)),
        band(BINOMIAL, np.arange(scans // 2), 2 * np.arange(scans // 4)),
    ).reshape(scans, LEVEL * scans // 2)
    two_column = np.pad(
        band(BINOMIAL, np.floor_divide(targets, 2), 2 * np.arange(columns // 4)).T, ((0, LANE - 4), (0, 0))
    )
    small = ml_dtypes.bfloat16
    return dict(
        rowscan=np.concatenate(rowscan, 0),
        level=level.astype(small),
        column=np.stack(column),
        level_column=level_column.astype(small),
        two=two.astype(small),
        two_column=two_column.astype(small),
    )


def dot(left, right):
    return jnp.dot(left, right, preferred_element_type=F32)


def dot_rows(left, right):
    return lax.dot_general(left, right, (((1,), (1,)), ((), ())), preferred_element_type=F32)


def place_table(shear_ref, group, slots, camera):
    slot = lax.broadcasted_iota(jnp.int32, (slots, 1), 0)
    plane, row = slot & 3, slot >> 2
    shift = jnp.where(plane == 0, shear_ref[0], jnp.where(plane == 1, shear_ref[1], jnp.where(plane == 2, shear_ref[2], shear_ref[3])))
    source = group * (2 * SLAB_ROWS) - LOW + row - shift
    inside = (source >= 0) & (source < camera) & (row < PAIR)
    wanted = jnp.where(inside, plane * camera + source, -1)
    lane = lax.broadcasted_iota(jnp.int32, (slots, 4 * camera), 1)
    return jnp.where(lane == wanted, 1.0, 0.0).astype(BF16)


def pack_first(raw_ref, shear_ref, width_ref, right_ref, left_ref, *out_refs):
    camera = raw_ref.shape[0] // 4
    columns = raw_ref.shape[1]
    tile = lax.axis_index("tile")
    tiles = lax.axis_size("tile")
    mine = lax.axis_index("slab") >> 1
    lane = lax.broadcasted_iota(jnp.int32, (8, columns), 1)
    line = lax.broadcasted_iota(jnp.int32, (8, columns), 0)
    right_width = width_ref[jnp.minimum(tile, tiles - 2)]
    left_width = width_ref[jnp.maximum(tile - 1, 0)]
    toward_right = jnp.where((lane == columns - right_width - 8 + line) & (line >= 2), 1.0, 0.0).astype(BF16)
    toward_left = jnp.where((lane == left_width + line) & (line < 6), 1.0, 0.0).astype(BF16)
    right_ref[...] = dot_rows(toward_right, raw_ref[...]).astype(BF16)
    left_ref[...] = dot_rows(toward_left, raw_ref[...]).astype(BF16)
    for step, out_ref in enumerate(out_refs):
        table = place_table(shear_ref, mine ^ step, PAIR * 4, camera)
        out_ref[...] = dot(table, raw_ref[:, : columns // 2]).astype(BF16)


def pack_second(raw_ref, shear_ref, from_left_ref, from_right_ref, *out_refs):
    camera = raw_ref.shape[0] // 4
    columns = raw_ref.shape[1]
    mine = lax.axis_index("slab") >> 1
    for step, out_ref in enumerate(out_refs):
        table = place_table(shear_ref, mine ^ step, columns // 2, camera)
        out_ref[: PAIR * 4, :] = dot(table[: PAIR * 4], raw_ref[:, columns // 2 :]).astype(BF16)
        strips = jnp.concatenate([from_right_ref[...].astype(F32), from_left_ref[...].astype(F32)], 0)
        out_ref[PAIR * 4 :, :] = dot_rows(strips.astype(BF16), table).astype(BF16)


def collect(in_refs, volume, scans):
    slab = lax.axis_index("slab")
    core = slab & 1
    lanes = volume.shape[-1]
    groups = scans // 4
    volume[0] = jnp.zeros((LANE, lanes), BF16)
    volume[groups + 1] = jnp.zeros((LANE, lanes), BF16)
    for index, in_ref in enumerate(in_refs):
        group = (slab ^ index) + 1
        start = pl.multiple_of(core * (SLAB_ROWS * 4), SLAB_ROWS * 4)
        volume[group, : NEED * 4, :] = in_ref[pl.ds(start, NEED * 4), :]
        volume[group, NEED * 4 :, :] = jnp.zeros((LANE - NEED * 4, lanes), BF16)


def split(value):
    high = value.astype(BF16)
    return high, (value - high.astype(F32)).astype(BF16)


def row_scan(rowscan_ref, operand, product, scans, store):
    rows = 8 * SLAB_ROWS
    for block in range(scans // 8):
        both = product(rowscan_ref[...], operand(block))
        for sigma in range(2):
            total = both[2 * sigma * rows : (2 * sigma + 1) * rows] + both[(2 * sigma + 1) * rows : (2 * sigma + 2) * rows]
            high, low = split(total)
            store(2 * sigma, block * rows, high)
            store(2 * sigma + 1, block * rows, low)


def first_half(count, scans, rowscan_ref, level_ref, *refs):
    in_refs, (wide_ref, coarse_ref), volume = refs[:count], refs[count : count + 2], refs[count + 2]
    collect(in_refs, volume, scans)
    lanes = volume.shape[-1]

    def store(part, start, value):
        wide_ref[part, start : start + value.shape[0], :] = value

    row_scan(rowscan_ref, lambda block: volume[2 * block : 2 * block + 4].reshape(4 * LANE, lanes), dot, scans, store)
    groups = scans // 4
    coarse_ref[...] = dot(level_ref[...], volume[1 : groups + 1].reshape(groups * LANE, lanes))


def second_half(count, scans, *refs):
    rowscan_ref, level_ref, column_ref, level_column_ref, two_ref, two_column_ref, wide_ref, coarse_ref = refs[:8]
    in_refs = refs[8 : 8 + count]
    difference_ref, one_ref, second_ref, volume, edge, wide, rim = refs[8 + count :]
    slab = lax.axis_index("slab")
    slabs = lax.axis_size("slab")
    tile = lax.axis_index("tile")
    tiles = lax.axis_size("tile")
    core = slab & 1
    groups = scans // 4
    lanes = volume.shape[-1]
    collect(in_refs, volume, scans)
    edge[...] = jnp.zeros(edge.shape, BF16)
    for index, in_ref in enumerate(in_refs):
        place = pl.multiple_of(((slab ^ index) + 1) * LANE, LANE)
        strips = in_ref[PAIR * 4 :, :].astype(F32)
        strips = jnp.where(core == 0, strips[:, :LANE], strips[:, SLAB_ROWS * 4 : SLAB_ROWS * 4 + LANE]).astype(BF16)
        edge[0:8, pl.ds(place, LANE)] = strips[:8]
        edge[LANE - 8 :, pl.ds(place, LANE)] = strips[8:]

    def store(part, start, value):
        wide[part, start : start + value.shape[0], :] = value

    def store_rim(part, start, value):
        rim[part, start : start + value.shape[0], :] = value

    row_scan(rowscan_ref, lambda block: volume[2 * block : 2 * block + 4].reshape(4 * LANE, lanes), dot, scans, store)
    row_scan(rowscan_ref, lambda block: edge[:, 2 * block * LANE : (2 * block + 4) * LANE], dot_rows, scans, store_rim)

    for half in range(2):
        total = None
        for sigma in range(2):
            parts = []
            for part in (2 * sigma, 2 * sigma + 1):
                if half == 0:
                    parts.append(jnp.concatenate([rim[part], wide_ref[part], wide[part][:, :LANE]], 1))
                else:
                    parts.append(jnp.concatenate([wide_ref[part][:, lanes - LANE :], wide[part], rim[part]], 1))
            smooth = dot(parts[0], column_ref[2 * sigma]) + dot(parts[1], column_ref[2 * sigma]) + dot(parts[0], column_ref[2 * sigma + 1])
            total = smooth if total is None else total - smooth
        total = total.reshape(scans // 8, SLAB_ROWS, 8, lanes)
        for pair in range(scans // 16):
            joined = jnp.concatenate([total[2 * pair], total[2 * pair + 1]], 1)
            difference_ref[:, 16 * pair : 16 * pair + 16, half * lanes : (half + 1) * lanes] = joined.astype(BF16)

    coarse = jnp.concatenate(
        [
            dot_rows(level_ref[...], edge[:, LANE : (groups + 1) * LANE]),
            coarse_ref[...],
            dot(level_ref[...], volume[1 : groups + 1].reshape(groups * LANE, lanes)),
        ],
        1,
    )
    high, low = split(coarse)
    level = dot(high, level_column_ref[...]) + dot(low, level_column_ref[...])
    shape = (LEVEL, scans // 2, level.shape[-1])
    level = level.reshape(shape)
    row = slab * (SLAB_ROWS // 2) - 2 + lax.broadcasted_iota(jnp.int32, shape, 0)
    lane = lax.broadcasted_iota(jnp.int32, shape, 2) - lanes
    keep = (row >= 0) & (row < slabs * (SLAB_ROWS // 2))
    keep = keep & ((lane < 0) | (lane >= 2) | (tile > 0)) & ((lane < 2) | (tile < tiles - 1))
    level = jnp.where(keep, level, 0.0)
    ready = level.astype(BF16)
    one_ref[...] = ready[2:10, :, :lanes]
    blurred = dot(two_ref[...], ready.reshape(LEVEL * scans // 2, level.shape[-1]))
    high, low = split(blurred)
    second = dot(high, two_column_ref[...]) + dot(low, two_column_ref[...])
    second_ref[...] = second.reshape(second_ref.shape).astype(BF16)


VECTOR = pl.BlockSpec(memory_space=pltpu.VMEM)
SCALAR = pl.BlockSpec(memory_space=pltpu.SMEM)
PARAMS = pltpu.CompilerParams(vmem_limit_bytes=48 * 1024 * 1024)


def exchange(chunks, slabs):
    order = sorted(range(1, len(chunks)), key=lambda step: (-(step & -step), step))
    held = {0: chunks[0]}
    for step in order:
        held[step] = lax.ppermute(chunks[step], "slab", [(i, i ^ (2 * step)) for i in range(slabs)])
    swap = [(i, i ^ 1) for i in range(slabs)]
    result = []
    for step in range(len(chunks)):
        result += [held[step], lax.ppermute(held[step], "slab", swap)]
    return result


def shifted(block, distance):
    devices = range(lax.axis_size("tile"))
    route = [(i - distance, i) for i in devices if i - distance in devices]
    return lax.ppermute(block, "tile", route)


def body(raw_stack, shear_offsets, intersection_widths):
    slabs = lax.axis_size("slab")
    planes, camera, columns = raw_stack.shape
    scans = planes * slabs
    half = columns // 2
    pairs = slabs // 2
    raw = raw_stack.reshape(planes * camera, columns)
    table = {name: jnp.asarray(value) for name, value in tables(scans, columns).items()}
    strip = jax.ShapeDtypeStruct((8, planes * camera), BF16)
    first = jax.ShapeDtypeStruct((PAIR * planes, half), BF16)
    toward_right, toward_left, *chunks = pl.pallas_call(
        pack_first,
        out_shape=[strip, strip] + [first] * pairs,
        in_specs=[VECTOR, SCALAR, SCALAR],
        out_specs=[VECTOR] * (2 + pairs),
        compiler_params=PARAMS,
        name="pack_first",
    )(raw, shear_offsets, intersection_widths)
    from_left = shifted(toward_right, 1)
    from_right = shifted(toward_left, -1)
    got_first = exchange(chunks, slabs)
    second = jax.ShapeDtypeStruct((PAIR * planes + 16, half), BF16)
    chunks = pl.pallas_call(
        pack_second,
        out_shape=[second] * pairs,
        in_specs=[VECTOR, SCALAR, VECTOR, VECTOR],
        out_specs=[VECTOR] * pairs,
        compiler_params=PARAMS,
        name="pack_second",
    )(raw, shear_offsets, from_left, from_right)
    got_second = exchange(chunks, slabs)
    wide = jax.ShapeDtypeStruct((4, scans * SLAB_ROWS, half), BF16)
    coarse = jax.ShapeDtypeStruct((LEVEL * scans // 2, half), F32)
    volume = pltpu.VMEM((slabs + 2, LANE, half), BF16)
    wide_first, coarse_first = pl.pallas_call(
        functools.partial(first_half, slabs, scans),
        out_shape=[wide, coarse],
        in_specs=[VECTOR] * (2 + slabs),
        out_specs=[VECTOR] * 2,
        scratch_shapes=[volume],
        compiler_params=PARAMS,
        name="first_half",
    )(table["rowscan"], table["level"], *got_first)
    return pl.pallas_call(
        functools.partial(second_half, slabs, scans),
        out_shape=[
            jax.ShapeDtypeStruct((SLAB_ROWS, scans, columns), BF16),
            jax.ShapeDtypeStruct((SLAB_ROWS // 2, scans // 2, columns // 2), BF16),
            jax.ShapeDtypeStruct((SLAB_ROWS // 4, scans // 4, columns // 4), BF16),
        ],
        in_specs=[VECTOR] * (8 + slabs),
        out_specs=[VECTOR] * 3,
        scratch_shapes=[
            volume,
            pltpu.VMEM((LANE, (slabs + 2) * LANE), BF16),
            pltpu.VMEM((4, scans * SLAB_ROWS, half), BF16),
            pltpu.VMEM((4, scans * SLAB_ROWS, LANE), BF16),
        ],
        compiler_params=PARAMS,
        name="second_half",
    )(
        table["rowscan"],
        table["level"],
        table["column"],
        table["level_column"],
        table["two"],
        table["two_column"],
        wide_first,
        coarse_first,
        *got_second,
    )


def solution(mesh):
    placed = (P("slab", None, "tile"), P("slab"), P())
    return jax.shard_map(
        body,
        mesh=mesh,
        in_specs=placed,
        out_specs=(P("slab", None, "tile"), P("slab", None, "tile"), P("slab", None, "tile")),
        check_vma=False,
    )
```

```python
import functools
import math

import jax
import jax.numpy as jnp
import ml_dtypes
import numpy as np
from jax import lax
from jax.experimental import pallas as pl
from jax.experimental.pallas import tpu as pltpu
from jax.sharding import PartitionSpec as P

SLAB_ROWS = 16
STRIP = 6
RADIUS = 4
LOW = 6
HIGH = 4
PAIR = 2 * SLAB_ROWS + LOW + HIGH
NEED = SLAB_ROWS + LOW + HIGH
LEVEL = 11
LANE = 128
F32 = jnp.float32
BF16 = jnp.bfloat16


def gauss_taps(sigma_value):
    entries = [math.exp(-(j * j) / (2.0 * sigma_value * sigma_value)) for j in range(-RADIUS, RADIUS + 1)]
    weight_sum = sum(entries)
    return np.array([entry / weight_sum for entry in entries], np.float64)


BINOMIAL = np.array([1.0, 4.0, 6.0, 4.0, 1.0], np.float64) / 16.0


def band(weights, source, target):
    reach = len(weights) // 2
    offset = source[None, :] - target[:, None] + reach
    inside = (offset >= 0) & (offset < len(weights))
    return np.where(inside, weights[np.clip(offset, 0, len(weights) - 1)], 0.0)


def two_parts(table):
    high = table.astype(ml_dtypes.bfloat16)
    return [high, (table - high.astype(np.float64)).astype(ml_dtypes.bfloat16)]


def row_scan_table(row_band, scan_band, groups):
    rows_out, rows_in = row_band.shape
    scans_out = scan_band.shape[0]
    scans = scan_band.reshape(scans_out, groups, 4)
    table = np.einsum("yr,sgp->ysgrp", row_band, scans)
    table = table.reshape(rows_out * scans_out, groups, rows_in * 4)
    table = np.pad(table, ((0, 0), (0, 0), (0, LANE - rows_in * 4)))
    return table.reshape(rows_out * scans_out, groups * LANE)


def tables(scans, columns):
    row_in = np.arange(NEED) - LOW
    own = np.arange(SLAB_ROWS)
    near = np.arange(16) - 4
    block = np.arange(8)
    cut = columns - LANE
    rim = np.where(np.arange(LANE) < LANE // 2, columns, -LANE) + np.arange(LANE)
    last = np.concatenate([np.arange(cut, columns), rim])
    touched = np.concatenate([np.arange(cut, columns), np.arange(LANE // 2), np.arange(cut - LANE // 2, cut)])
    rowscan, column_first, column_last = [], [], []
    for sigma, sign in ((1.0, 1.0), (1.6, -1.0)):
        taps = gauss_taps(sigma)
        rowscan += two_parts(row_scan_table(band(taps, row_in, own), band(taps, near, block), 4))
        column_first += two_parts(sign * band(taps, np.arange(4 * LANE) - LANE, np.arange(2 * LANE)).T)
        column_last += two_parts(sign * band(taps, last, touched).T)
    level_rows = 2 * np.arange(LEVEL) - 4
    level_scans = 2 * np.arange(scans // 2)
    level = row_scan_table(
        band(BINOMIAL, row_in, level_rows), band(BINOMIAL, np.arange(scans), level_scans), scans // 4
    )
    edges = np.array([-4, -2, columns, columns + 2])
    targets = np.concatenate([2 * np.arange(columns // 2), edges])
    two = np.einsum(
        "yr,sp->ysrp",
        band(BINOMIAL, np.arange(LEVEL) - 2, 2 * np.arange(4)),
        band(BINOMIAL, np.arange(scans // 2), 2 * np.arange(scans // 4)),
    ).reshape(scans, LEVEL * scans // 2)
    fill = ((0, 0), (0, LANE - 4))
    small = ml_dtypes.bfloat16
    return dict(
        rowscan=np.concatenate(rowscan, 0),
        level=level.astype(small),
        column_first=np.stack(column_first),
        column_last=np.stack(column_last),
        level_first=np.pad(band(BINOMIAL, np.arange(cut), targets).T, fill).astype(small),
        level_last=np.pad(band(BINOMIAL, last, targets).T, fill).astype(small),
        two=two.astype(small),
        two_column=np.pad(band(BINOMIAL, targets // 2, 2 * np.arange(columns // 4)), fill).T.astype(small),
    )


def dot(left, right):
    return jnp.dot(left, right, preferred_element_type=F32)


def dot_rows(left, right):
    return lax.dot_general(left, right, (((1,), (1,)), ((), ())), preferred_element_type=F32)


def place_table(shift, group, camera):
    slots = shift.shape[0]
    slot = lax.broadcasted_iota(jnp.int32, (slots, 1), 0)
    plane, row = slot & 3, slot >> 2
    source = group * (2 * SLAB_ROWS) - LOW + row - shift
    inside = (source >= 0) & (source < camera) & (row < PAIR)
    wanted = jnp.where(inside, plane * camera + source, -1)
    lane = lax.broadcasted_iota(jnp.int32, (slots, 4 * camera), 1)
    return jnp.where(lane == wanted, 1.0, 0.0).astype(BF16)


def pack_first(raw_ref, shear_ref, width_ref, right_ref, left_ref, kept_ref, shift_ref, *refs):
    out_refs, (shears, widths, raw_sem, shear_sem, width_sem) = refs[:-5], refs[-5:]
    load_raw = pltpu.make_async_copy(raw_ref, kept_ref, raw_sem)
    load_shear = pltpu.make_async_copy(shear_ref, shears, shear_sem)
    load_width = pltpu.make_async_copy(width_ref, widths, width_sem)
    load_raw.start()
    load_shear.start()
    load_width.start()
    camera = raw_ref.shape[0] // 4
    columns = raw_ref.shape[1]
    tile = lax.axis_index("tile")
    tiles = lax.axis_size("tile")
    mine = lax.axis_index("slab") >> 1
    lane = lax.broadcasted_iota(jnp.int32, (8, columns), 1)
    line = lax.broadcasted_iota(jnp.int32, (8, columns), 0)
    load_shear.wait()
    load_width.wait()
    right_width = widths[jnp.minimum(tile, tiles - 2)]
    left_width = widths[jnp.maximum(tile - 1, 0)]
    toward_right = jnp.where((lane == columns - right_width - 8 + line) & (line >= 2), 1.0, 0.0).astype(BF16)
    toward_left = jnp.where((lane == left_width + line) & (line < 6), 1.0, 0.0).astype(BF16)
    plane = lax.broadcasted_iota(jnp.int32, shift_ref.shape, 0) & 3
    shift_ref[...] = jnp.where(plane < 2, jnp.where(plane == 0, shears[0], shears[1]), jnp.where(plane == 2, shears[2], shears[3]))
    load_raw.wait()
    for step, out_ref in enumerate(out_refs):
        table = place_table(shift_ref[: PAIR * 4, :1], mine ^ step, camera)
        out_ref[...] = dot(table, kept_ref[:, : columns - LANE]).astype(BF16)
    right_ref[...] = dot_rows(toward_right, kept_ref[...]).astype(BF16)
    left_ref[...] = dot_rows(toward_left, kept_ref[...]).astype(BF16)


def stage(order_ref, *refs):
    sems, refs = refs[-1], refs[:-1]
    count = len(refs) // 2
    loads = [pltpu.make_async_copy(refs[index], refs[count + index], sems.at[index]) for index in range(count)]
    for load in loads:
        load.start()
    for load in loads:
        load.wait()


def pack_second(raw_ref, shift_ref, from_left_ref, from_right_ref, order_ref, *out_refs):
    camera = raw_ref.shape[0] // 4
    columns = raw_ref.shape[1]
    mine = lax.axis_index("slab") >> 1
    tile = lax.axis_index("tile")
    right = jnp.where(tile < lax.axis_size("tile") - 1, from_right_ref[...].astype(F32), 0.0)
    left = jnp.where(tile > 0, from_left_ref[...].astype(F32), 0.0)
    strips = jnp.concatenate([right, left], 0).astype(BF16)
    for step, out_ref in enumerate(out_refs):
        table = place_table(shift_ref[:, :1], mine ^ step, camera)
        out_ref[: PAIR * 4, :] = dot(table[: PAIR * 4], raw_ref[:, columns - LANE :]).astype(BF16)
        placed = dot_rows(strips, table).astype(BF16)
        out_ref[PAIR * 4 : PAIR * 4 + 16, :] = placed[:, :LANE]
        out_ref[PAIR * 4 + 16 :, :] = placed[:, LANE:]


def collect(in_refs, volume, scans):
    slab = lax.axis_index("slab")
    core = slab & 1
    lanes = in_refs[0].shape[-1]
    groups = scans // 4
    outside = jnp.zeros((LANE,) + volume.shape[2:], BF16)
    volume[0] = outside
    volume[groups + 1] = outside
    for index, in_ref in enumerate(in_refs):
        group = (slab ^ index) + 1
        start = pl.multiple_of(core * (SLAB_ROWS * 4), SLAB_ROWS * 4)
        volume[group, : NEED * 4, :lanes] = in_ref[pl.ds(start, NEED * 4), :]
        volume[group, NEED * 4 :, :lanes] = jnp.zeros((LANE - NEED * 4, lanes), BF16)


def split(value):
    high = value.astype(BF16)
    return high, (value - high.astype(F32)).astype(BF16)


def row_scan(rowscan_ref, volume, block, wide):
    rows = 8 * SLAB_ROWS
    both = dot(rowscan_ref[...], volume[2 * block : 2 * block + 4].reshape(4 * LANE, volume.shape[-1]))
    for sigma in range(2):
        total = both[2 * sigma * rows : (2 * sigma + 1) * rows] + both[(2 * sigma + 1) * rows : (2 * sigma + 2) * rows]
        high, low = split(total)
        wide[2 * sigma, block * rows : (block + 1) * rows, :] = high
        wide[2 * sigma + 1, block * rows : (block + 1) * rows, :] = low


def across(wide, rows, lanes, column_ref, taken):
    total = None
    for sigma in range(2):
        high, low = wide[2 * sigma, rows, lanes], wide[2 * sigma + 1, rows, lanes]
        part = dot(high, column_ref[2 * sigma, taken]) + dot(low, column_ref[2 * sigma, taken])
        part = part + dot(high, column_ref[2 * sigma + 1, taken])
        total = part if total is None else total + part
    return total


def level_part(level_ref, level_column_ref, volume, scans):
    groups = scans // 4
    high, low = split(dot(level_ref[...], volume[1 : groups + 1].reshape(groups * LANE, volume.shape[-1])))
    return dot(high, level_column_ref[...]) + dot(low, level_column_ref[...])


def first_half(count, scans, rowscan_ref, level_ref, column_ref, level_column_ref, *refs):
    in_refs, (partial_ref, coarse_ref, volume, wide) = refs[:count], refs[count:]
    collect(in_refs, volume, scans)
    for block in range(scans // 8):
        row_scan(rowscan_ref, volume, block, wide)
    cut = wide.shape[-1]
    for start in range(0, partial_ref.shape[1], 2 * LANE):
        low, high = max(start - LANE, 0), min(start + 3 * LANE, cut)
        taken = slice(low - start + LANE, high - start + LANE)
        partial_ref[:, start : start + 2 * LANE] = across(wide, slice(None), slice(low, high), column_ref, taken)
    coarse_ref[...] = level_part(level_ref, level_column_ref, volume, scans)


def second_half(count, scans, rowscan_ref, level_ref, column_ref, level_column_ref, two_ref, two_column_ref, *refs):
    partial_ref, coarse_ref, *in_refs = refs[: 2 + count]
    difference_ref, one_ref, second_ref, volume, strips, wide, held, sems = refs[2 + count :]
    slab = lax.axis_index("slab")
    slabs = lax.axis_size("slab")
    tile = lax.axis_index("tile")
    tiles = lax.axis_size("tile")
    core = slab & 1
    groups = scans // 4
    columns = partial_ref.shape[1]
    cut = columns - LANE
    collect(in_refs, volume, scans)
    for index, in_ref in enumerate(in_refs):
        place = pl.multiple_of((slab ^ index) * LANE, LANE)
        both = jnp.concatenate([in_ref[PAIR * 4 : PAIR * 4 + 16, :], in_ref[PAIR * 4 + 16 :, :]], 1).astype(F32)
        both = jnp.where(core == 0, both[:, :LANE], both[:, SLAB_ROWS * 4 : SLAB_ROWS * 4 + LANE])
        strips[:, pl.ds(place, LANE)] = both.astype(BF16)
    line = lax.broadcasted_iota(jnp.int32, (16, LANE), 0)
    lane = lax.broadcasted_iota(jnp.int32, (16, LANE), 1)
    spread = jnp.where(lane == jnp.where(line < 8, line, line + LANE - 16), 1.0, 0.0).astype(BF16)
    rim = lax.dot_general(strips[...], spread, (((0,), (0,)), ((), ())), preferred_element_type=F32)
    volume[1 : groups + 1, :, LANE:] = rim.astype(BF16).reshape(groups, LANE, LANE)

    level = coarse_ref[...] + level_part(level_ref, level_column_ref, volume, scans)
    half = columns // 2
    shape = (LEVEL, scans // 2, level.shape[-1])
    level = level.reshape(shape)
    row = slab * (SLAB_ROWS // 2) - 2 + lax.broadcasted_iota(jnp.int32, shape, 0)
    place = lax.broadcasted_iota(jnp.int32, shape, 2) - half
    keep = (row >= 0) & (row < slabs * (SLAB_ROWS // 2))
    keep = keep & ((place < 0) | (place >= 2) | (tile > 0)) & ((place < 2) | (tile < tiles - 1))
    ready = jnp.where(keep, level, 0.0).astype(BF16)
    one_ref[...] = ready[2:10, :, :half]
    high, low = split(dot(two_ref[...], ready.reshape(LEVEL * scans // 2, level.shape[-1])))
    second = dot(high, two_column_ref[...]) + dot(low, two_column_ref[...])
    second_ref[...] = second.reshape(second_ref.shape).astype(BF16)

    copies = []
    rows = 8 * SLAB_ROWS
    left = lax.broadcasted_iota(jnp.int32, (2 * rows, LANE), 1) < LANE // 2
    for pair in range(scans // 16):
        for block in (2 * pair, 2 * pair + 1):
            row_scan(rowscan_ref, volume, block, wide)
        here = slice(2 * pair * rows, 2 * (pair + 1) * rows)
        late = across(wide, here, slice(None), column_ref, slice(None))
        ends = late[:, LANE:]
        for start in range(0, columns, LANE):
            total = partial_ref[here, start : start + LANE]
            if start == cut:
                total = total + late[:, :LANE]
            if start == 0:
                total = total + jnp.where(left, ends, 0.0)
            if start == cut - LANE:
                total = total + jnp.where(left, 0.0, ends)
            total = total.reshape(2, SLAB_ROWS, 8, LANE)
            joined = jnp.concatenate([total[0], total[1]], 1)
            held[:, 16 * pair : 16 * pair + 16, start : start + LANE] = joined.astype(BF16)
        copy = pltpu.make_async_copy(
            held.at[:, 16 * pair : 16 * pair + 16, :], difference_ref.at[:, 16 * pair : 16 * pair + 16, :], sems.at[pair]
        )
        copy.start()
        copies.append(copy)
    for copy in copies:
        copy.wait()


VECTOR = pl.BlockSpec(memory_space=pltpu.VMEM)
ANYWHERE = pl.BlockSpec(memory_space=pl.ANY)
OUTSIDE = pl.BlockSpec(memory_space=pltpu.HBM)
PARAMS = pltpu.CompilerParams(vmem_limit_bytes=20 * 1024 * 1024)


def along(chunks, slabs):
    held = {}
    for step in sorted(range(1, len(chunks)), key=lambda step: (-(step & -step), step)):
        held[step] = lax.ppermute(chunks[step], "slab", [(i, i ^ (2 * step)) for i in range(slabs)])
    return held


def within(held, slabs):
    result = []
    for step in range(len(held)):
        result += [held[step], lax.ppermute(held[step], "slab", [(i, i ^ 1) for i in range(slabs)])]
    return result


def shifted(block, distance):
    count = lax.axis_size("tile")
    return lax.ppermute(block, "tile", [(i, (i + distance) % count) for i in range(count)])


def body(raw_stack, shear_offsets, intersection_widths):
    slabs = lax.axis_size("slab")
    planes, camera, columns = raw_stack.shape
    scans = planes * slabs
    cut = columns - LANE
    pairs = slabs // 2
    table = {name: jnp.asarray(value) for name, value in tables(scans, columns).items()}
    outside = [raw_stack.reshape(planes * camera, columns), shear_offsets, intersection_widths]
    outside = [pltpu.with_memory_space_constraint(each, pltpu.HBM) for each in outside]
    strip = jax.ShapeDtypeStruct((8, planes * camera), BF16)
    first = jax.ShapeDtypeStruct((PAIR * planes, cut), BF16)
    toward_right, toward_left, raw, shift, *chunks = pl.pallas_call(
        pack_first,
        out_shape=[strip, strip, jax.ShapeDtypeStruct((planes * camera, columns), BF16), jax.ShapeDtypeStruct((2 * LANE, LANE), jnp.int32)]
        + [first] * pairs,
        in_specs=[OUTSIDE] * 3,
        out_specs=[VECTOR] * (4 + pairs),
        scratch_shapes=[pltpu.SMEM(shear_offsets.shape, jnp.int32), pltpu.SMEM(intersection_widths.shape, jnp.int32)]
        + [pltpu.SemaphoreType.DMA] * 3,
        compiler_params=PARAMS,
        name="pack_first",
    )(*outside)
    first_held = along(chunks, slabs)
    from_left = shifted(toward_right, 1)
    from_right = shifted(toward_left, -1)
    own = chunks[0]
    second = jax.ShapeDtypeStruct((PAIR * planes + 32, LANE), BF16)
    names = list(table)
    staged = pl.pallas_call(
        stage,
        out_shape=[jax.ShapeDtypeStruct(table[name].shape, BF16) for name in names],
        in_specs=[ANYWHERE] + [OUTSIDE] * len(names),
        out_specs=[VECTOR] * len(names),
        scratch_shapes=[pltpu.SemaphoreType.DMA((len(names),))],
        compiler_params=PARAMS,
        name="stage",
    )(toward_left, *[pltpu.with_memory_space_constraint(table[name], pltpu.HBM) for name in names])
    table = dict(zip(names, staged))
    chunks = pl.pallas_call(
        pack_second,
        out_shape=[second] * pairs,
        in_specs=[VECTOR] * 4 + [ANYWHERE],
        out_specs=[VECTOR] * pairs,
        compiler_params=PARAMS,
        name="pack_second",
    )(raw, shift, from_left, from_right, table["two"])
    second_held = along(chunks, slabs)
    first_held[0] = own
    first_held = lax.optimization_barrier((first_held, chunks))[0]
    got_first = within(first_held, slabs)
    partial, coarse = pl.pallas_call(
        functools.partial(first_half, slabs, scans),
        out_shape=[
            jax.ShapeDtypeStruct((scans * SLAB_ROWS, columns), F32),
            jax.ShapeDtypeStruct((LEVEL * scans // 2, columns // 2 + LANE), F32),
        ],
        in_specs=[VECTOR] * (4 + slabs),
        out_specs=[VECTOR] * 2,
        scratch_shapes=[
            pltpu.VMEM((slabs + 2, LANE, cut), BF16),
            pltpu.VMEM((4, scans * SLAB_ROWS, cut), BF16),
        ],
        compiler_params=PARAMS,
        name="first_half",
    )(table["rowscan"], table["level"], table["column_first"], table["level_first"], *got_first)
    second_held[0] = chunks[0]
    second_held, partial = lax.optimization_barrier((second_held, partial))
    got_second = within(second_held, slabs)
    return pl.pallas_call(
        functools.partial(second_half, slabs, scans),
        out_shape=[
            jax.ShapeDtypeStruct((SLAB_ROWS, scans, columns), BF16),
            jax.ShapeDtypeStruct((SLAB_ROWS // 2, scans // 2, columns // 2), BF16),
            jax.ShapeDtypeStruct((SLAB_ROWS // 4, scans // 4, columns // 4), BF16),
        ],
        in_specs=[VECTOR] * (8 + slabs),
        out_specs=[OUTSIDE, VECTOR, VECTOR],
        scratch_shapes=[
            pltpu.VMEM((slabs + 2, LANE, 2 * LANE), BF16),
            pltpu.VMEM((16, slabs * LANE), BF16),
            pltpu.VMEM((4, scans * SLAB_ROWS, 2 * LANE), BF16),
            pltpu.VMEM((SLAB_ROWS, scans, columns), BF16),
            pltpu.SemaphoreType.DMA((scans // 16,)),
        ],
        compiler_params=PARAMS,
        name="second_half",
    )(
        table["rowscan"],
        table["level"],
        table["column_last"],
        table["level_last"],
        table["two"],
        table["two_column"],
        partial,
        coarse,
        *got_second,
    )


def solution(mesh):
    placed = (P("slab", None, "tile"), P("slab"), P())
    return jax.shard_map(
        body,
        mesh=mesh,
        in_specs=placed,
        out_specs=(P("slab", None, "tile"), P("slab", None, "tile"), P("slab", None, "tile")),
        check_vma=False,
    )
```

```python
import functools
import math

import jax
import jax.numpy as jnp
import ml_dtypes
import numpy as np
from jax import lax
from jax.experimental import pallas as pl
from jax.experimental.pallas import tpu as pltpu
from jax.sharding import PartitionSpec as P

SLAB_ROWS = 16
STRIP = 6
RADIUS = 4
LOW = 6
HIGH = 4
PAIR = 2 * SLAB_ROWS + LOW + HIGH
NEED = SLAB_ROWS + LOW + HIGH
LEVEL = 11
LANE = 128
F32 = jnp.float32
BF16 = jnp.bfloat16


def gauss_taps(sigma_value):
    entries = [math.exp(-(j * j) / (2.0 * sigma_value * sigma_value)) for j in range(-RADIUS, RADIUS + 1)]
    weight_sum = sum(entries)
    return np.array([entry / weight_sum for entry in entries], np.float64)


BINOMIAL = np.array([1.0, 4.0, 6.0, 4.0, 1.0], np.float64) / 16.0


def band(weights, source, target):
    reach = len(weights) // 2
    offset = source[None, :] - target[:, None] + reach
    inside = (offset >= 0) & (offset < len(weights))
    return np.where(inside, weights[np.clip(offset, 0, len(weights) - 1)], 0.0)


def two_parts(table):
    high = table.astype(ml_dtypes.bfloat16)
    return [high, (table - high.astype(np.float64)).astype(ml_dtypes.bfloat16)]


def row_scan_table(row_band, scan_band, groups):
    rows_out, rows_in = row_band.shape
    scans_out = scan_band.shape[0]
    scans = scan_band.reshape(scans_out, groups, 4)
    table = np.einsum("yr,sgp->ysgrp", row_band, scans)
    table = table.reshape(rows_out * scans_out, groups, rows_in * 4)
    table = np.pad(table, ((0, 0), (0, 0), (0, LANE - rows_in * 4)))
    return table.reshape(rows_out * scans_out, groups * LANE)


def tables(scans, columns):
    row_in = np.arange(NEED) - LOW
    own = np.arange(SLAB_ROWS)
    near = np.arange(16) - 4
    block = np.arange(8)
    cut = columns - LANE
    rim = np.where(np.arange(LANE) < LANE // 2, columns, -LANE) + np.arange(LANE)
    last = np.concatenate([np.arange(cut, columns), rim])
    touched = np.concatenate([np.arange(cut, columns), np.arange(LANE // 2), np.arange(cut - LANE // 2, cut)])
    rowscan, column_first, column_last = [], [], []
    for sigma, sign in ((1.0, 1.0), (1.6, -1.0)):
        taps = gauss_taps(sigma)
        rowscan += two_parts(row_scan_table(band(taps, row_in, own), band(taps, near, block), 4))
        column_first += two_parts(sign * band(taps, np.arange(4 * LANE) - LANE, np.arange(2 * LANE)).T)
        column_last += two_parts(sign * band(taps, last, touched).T)
    level_rows = 2 * np.arange(LEVEL) - 4
    level_scans = 2 * np.arange(scans // 2)
    level = row_scan_table(
        band(BINOMIAL, row_in, level_rows), band(BINOMIAL, np.arange(scans), level_scans), scans // 4
    )
    edges = np.array([-4, -2, columns, columns + 2])
    targets = np.concatenate([2 * np.arange(columns // 2), edges])
    two = np.einsum(
        "yr,sp->ysrp",
        band(BINOMIAL, np.arange(LEVEL) - 2, 2 * np.arange(4)),
        band(BINOMIAL, np.arange(scans // 2), 2 * np.arange(scans // 4)),
    ).reshape(scans, LEVEL * scans // 2)
    fill = ((0, 0), (0, LANE - 4))
    small = ml_dtypes.bfloat16
    return dict(
        rowscan=np.concatenate(rowscan, 0),
        level=level.astype(small),
        column_first=np.stack(column_first),
        column_last=np.stack(column_last),
        level_first=np.pad(band(BINOMIAL, np.arange(cut), targets).T, fill).astype(small),
        level_last=np.pad(band(BINOMIAL, last, targets).T, fill).astype(small),
        two=two.astype(small),
        two_column=np.pad(band(BINOMIAL, targets // 2, 2 * np.arange(columns // 4)), fill).T.astype(small),
    )


def dot(left, right):
    return jnp.dot(left, right, preferred_element_type=F32)


def dot_rows(left, right):
    return lax.dot_general(left, right, (((1,), (1,)), ((), ())), preferred_element_type=F32)


def place_table(shift, group, camera):
    slots = shift.shape[0]
    slot = lax.broadcasted_iota(jnp.int32, (slots, 1), 0)
    plane, row = slot & 3, slot >> 2
    source = group * (2 * SLAB_ROWS) - LOW + row - shift
    inside = (source >= 0) & (source < camera) & (row < PAIR)
    wanted = jnp.where(inside, plane * camera + source, -1)
    lane = lax.broadcasted_iota(jnp.int32, (slots, 4 * camera), 1)
    return jnp.where(lane == wanted, 1.0, 0.0).astype(BF16)


def pack_first(raw_ref, shear_ref, width_ref, right_ref, left_ref, kept_ref, shift_ref, *refs):
    out_refs, (shears, widths, raw_sem, shear_sem, width_sem) = refs[:-5], refs[-5:]
    load_raw = pltpu.make_async_copy(raw_ref, kept_ref, raw_sem)
    load_shear = pltpu.make_async_copy(shear_ref, shears, shear_sem)
    load_width = pltpu.make_async_copy(width_ref, widths, width_sem)
    load_raw.start()
    load_shear.start()
    load_width.start()
    camera = raw_ref.shape[0] // 4
    columns = raw_ref.shape[1]
    tile = lax.axis_index("tile")
    tiles = lax.axis_size("tile")
    mine = lax.axis_index("slab") >> 1
    lane = lax.broadcasted_iota(jnp.int32, (8, columns), 1)
    line = lax.broadcasted_iota(jnp.int32, (8, columns), 0)
    load_shear.wait()
    load_width.wait()
    right_width = widths[jnp.minimum(tile, tiles - 2)]
    left_width = widths[jnp.maximum(tile - 1, 0)]
    toward_right = jnp.where((lane == columns - right_width - 8 + line) & (line >= 2), 1.0, 0.0).astype(BF16)
    toward_left = jnp.where((lane == left_width + line) & (line < 6), 1.0, 0.0).astype(BF16)
    plane = lax.broadcasted_iota(jnp.int32, shift_ref.shape, 0) & 3
    shift_ref[...] = jnp.where(plane < 2, jnp.where(plane == 0, shears[0], shears[1]), jnp.where(plane == 2, shears[2], shears[3]))
    load_raw.wait()
    for step, out_ref in enumerate(out_refs):
        table = place_table(shift_ref[: PAIR * 4, :1], mine ^ step, camera)
        out_ref[...] = dot(table, kept_ref[:, : columns - LANE]).astype(BF16)
    right_ref[...] = dot_rows(toward_right, kept_ref[...]).astype(BF16)
    left_ref[...] = dot_rows(toward_left, kept_ref[...]).astype(BF16)


def stage(order_ref, *refs):
    sems, refs = refs[-1], refs[:-1]
    count = len(refs) // 2
    loads = [pltpu.make_async_copy(refs[index], refs[count + index], sems.at[index]) for index in range(count)]
    for load in loads:
        load.start()
    for load in loads:
        load.wait()


def pack_second(raw_ref, shift_ref, from_left_ref, from_right_ref, order_ref, *out_refs):
    camera = raw_ref.shape[0] // 4
    columns = raw_ref.shape[1]
    mine = lax.axis_index("slab") >> 1
    tile = lax.axis_index("tile")
    right = jnp.where(tile < lax.axis_size("tile") - 1, from_right_ref[...].astype(F32), 0.0)
    left = jnp.where(tile > 0, from_left_ref[...].astype(F32), 0.0)
    strips = jnp.concatenate([right, left], 0).astype(BF16)
    for step, out_ref in enumerate(out_refs):
        table = place_table(shift_ref[:, :1], mine ^ step, camera)
        out_ref[: PAIR * 4, :] = dot(table[: PAIR * 4], raw_ref[:, columns - LANE :]).astype(BF16)
        placed = dot_rows(strips, table).astype(BF16)
        out_ref[PAIR * 4 : PAIR * 4 + 16, :] = placed[:, :LANE]
        out_ref[PAIR * 4 + 16 :, :] = placed[:, LANE:]


def collect(in_refs, volume, scans):
    slab = lax.axis_index("slab")
    core = slab & 1
    lanes = in_refs[0].shape[-1]
    groups = scans // 4
    outside = jnp.zeros((LANE,) + volume.shape[2:], BF16)
    volume[0] = outside
    volume[groups + 1] = outside
    for index, in_ref in enumerate(in_refs):
        group = (slab ^ index) + 1
        start = pl.multiple_of(core * (SLAB_ROWS * 4), SLAB_ROWS * 4)
        volume[group, : NEED * 4, :lanes] = in_ref[pl.ds(start, NEED * 4), :]
        volume[group, NEED * 4 :, :lanes] = jnp.zeros((LANE - NEED * 4, lanes), BF16)


def split(value):
    high = value.astype(BF16)
    return high, (value - high.astype(F32)).astype(BF16)


def row_scan(rowscan_ref, volume, block, wide):
    rows = 8 * SLAB_ROWS
    both = dot(rowscan_ref[...], volume[2 * block : 2 * block + 4].reshape(4 * LANE, volume.shape[-1]))
    for sigma in range(2):
        total = both[2 * sigma * rows : (2 * sigma + 1) * rows] + both[(2 * sigma + 1) * rows : (2 * sigma + 2) * rows]
        high, low = split(total)
        wide[2 * sigma, block * rows : (block + 1) * rows, :] = high
        wide[2 * sigma + 1, block * rows : (block + 1) * rows, :] = low


def across(wide, rows, lanes, column_ref, taken):
    total = None
    for sigma in range(2):
        high, low = wide[2 * sigma, rows, lanes], wide[2 * sigma + 1, rows, lanes]
        part = dot(high, column_ref[2 * sigma, taken]) + dot(low, column_ref[2 * sigma, taken])
        part = part + dot(high, column_ref[2 * sigma + 1, taken])
        total = part if total is None else total + part
    return total


def level_part(level_ref, level_column_ref, volume, scans):
    groups = scans // 4
    high, low = split(dot(level_ref[...], volume[1 : groups + 1].reshape(groups * LANE, volume.shape[-1])))
    return dot(high, level_column_ref[...]) + dot(low, level_column_ref[...])


def first_half(count, scans, rowscan_ref, level_ref, column_ref, level_column_ref, *refs):
    in_refs, (partial_ref, coarse_ref, volume, wide) = refs[:count], refs[count:]
    collect(in_refs, volume, scans)
    for block in range(scans // 8):
        row_scan(rowscan_ref, volume, block, wide)
    cut = wide.shape[-1]
    for start in range(0, partial_ref.shape[1], 2 * LANE):
        low, high = max(start - LANE, 0), min(start + 3 * LANE, cut)
        taken = slice(low - start + LANE, high - start + LANE)
        partial_ref[:, start : start + 2 * LANE] = across(wide, slice(None), slice(low, high), column_ref, taken)
    coarse_ref[...] = level_part(level_ref, level_column_ref, volume, scans)


def second_half(count, scans, rowscan_ref, level_ref, column_ref, level_column_ref, two_ref, two_column_ref, *refs):
    partial_ref, coarse_ref, *in_refs = refs[: 2 + count]
    difference_ref, one_ref, second_ref, volume, strips, wide, held, sems = refs[2 + count :]
    slab = lax.axis_index("slab")
    slabs = lax.axis_size("slab")
    tile = lax.axis_index("tile")
    tiles = lax.axis_size("tile")
    core = slab & 1
    groups = scans // 4
    columns = partial_ref.shape[1]
    cut = columns - LANE
    collect(in_refs, volume, scans)
    for index, in_ref in enumerate(in_refs):
        place = pl.multiple_of((slab ^ index) * LANE, LANE)
        both = jnp.concatenate([in_ref[PAIR * 4 : PAIR * 4 + 16, :], in_ref[PAIR * 4 + 16 :, :]], 1).astype(F32)
        both = jnp.where(core == 0, both[:, :LANE], both[:, SLAB_ROWS * 4 : SLAB_ROWS * 4 + LANE])
        strips[:, pl.ds(place, LANE)] = both.astype(BF16)
    line = lax.broadcasted_iota(jnp.int32, (16, LANE), 0)
    lane = lax.broadcasted_iota(jnp.int32, (16, LANE), 1)
    spread = jnp.where(lane == jnp.where(line < 8, line, line + LANE - 16), 1.0, 0.0).astype(BF16)
    rim = lax.dot_general(strips[...], spread, (((0,), (0,)), ((), ())), preferred_element_type=F32)
    volume[1 : groups + 1, :, LANE:] = rim.astype(BF16).reshape(groups, LANE, LANE)

    level = coarse_ref[...] + level_part(level_ref, level_column_ref, volume, scans)
    half = columns // 2
    shape = (LEVEL, scans // 2, level.shape[-1])
    level = level.reshape(shape)
    row = slab * (SLAB_ROWS // 2) - 2 + lax.broadcasted_iota(jnp.int32, shape, 0)
    place = lax.broadcasted_iota(jnp.int32, shape, 2) - half
    keep = (row >= 0) & (row < slabs * (SLAB_ROWS // 2))
    keep = keep & ((place < 0) | (place >= 2) | (tile > 0)) & ((place < 2) | (tile < tiles - 1))
    ready = jnp.where(keep, level, 0.0).astype(BF16)
    one_ref[...] = ready[2:10, :, :half]
    high, low = split(dot(two_ref[...], ready.reshape(LEVEL * scans // 2, level.shape[-1])))
    second = dot(high, two_column_ref[...]) + dot(low, two_column_ref[...])
    second_ref[...] = second.reshape(second_ref.shape).astype(BF16)

    copies = []
    rows = 8 * SLAB_ROWS
    left = lax.broadcasted_iota(jnp.int32, (2 * rows, LANE), 1) < LANE // 2
    for pair in range(scans // 16):
        for block in (2 * pair, 2 * pair + 1):
            row_scan(rowscan_ref, volume, block, wide)
        here = slice(2 * pair * rows, 2 * (pair + 1) * rows)
        late = across(wide, here, slice(None), column_ref, slice(None))
        ends = late[:, LANE:]
        for start in range(0, columns, LANE):
            total = partial_ref[here, start : start + LANE]
            if start == cut:
                total = total + late[:, :LANE]
            if start == 0:
                total = total + jnp.where(left, ends, 0.0)
            if start == cut - LANE:
                total = total + jnp.where(left, 0.0, ends)
            total = total.reshape(2, SLAB_ROWS, 8, LANE)
            joined = jnp.concatenate([total[0], total[1]], 1)
            held[:, 16 * pair : 16 * pair + 16, start : start + LANE] = joined.astype(BF16)
        copy = pltpu.make_async_copy(
            held.at[:, 16 * pair : 16 * pair + 16, :], difference_ref.at[:, 16 * pair : 16 * pair + 16, :], sems.at[pair]
        )
        copy.start()
        copies.append(copy)
    for copy in copies:
        copy.wait()


VECTOR = pl.BlockSpec(memory_space=pltpu.VMEM)
ANYWHERE = pl.BlockSpec(memory_space=pl.ANY)
OUTSIDE = pl.BlockSpec(memory_space=pltpu.HBM)
PARAMS = pltpu.CompilerParams(vmem_limit_bytes=20 * 1024 * 1024)


def along(chunks, slabs):
    held = {}
    for step in sorted(range(1, len(chunks)), key=lambda step: (-(step & -step), step)):
        held[step] = lax.ppermute(chunks[step], "slab", [(i, i ^ (2 * step)) for i in range(slabs)])
    return held


def within(held, slabs):
    result = []
    for step in range(len(held)):
        result += [held[step], lax.ppermute(held[step], "slab", [(i, i ^ 1) for i in range(slabs)])]
    return result


def shifted(block, distance):
    count = lax.axis_size("tile")
    return lax.ppermute(block, "tile", [(i, (i + distance) % count) for i in range(count)])


def body(raw_stack, shear_offsets, intersection_widths):
    slabs = lax.axis_size("slab")
    planes, camera, columns = raw_stack.shape
    scans = planes * slabs
    cut = columns - LANE
    pairs = slabs // 2
    table = {name: jnp.asarray(value) for name, value in tables(scans, columns).items()}
    outside = [raw_stack.reshape(planes * camera, columns), shear_offsets, intersection_widths]
    outside = [pltpu.with_memory_space_constraint(each, pltpu.HBM) for each in outside]
    strip = jax.ShapeDtypeStruct((8, planes * camera), BF16)
    first = jax.ShapeDtypeStruct((PAIR * planes, cut), BF16)
    toward_right, toward_left, raw, shift, *chunks = pl.pallas_call(
        pack_first,
        out_shape=[strip, strip, jax.ShapeDtypeStruct((planes * camera, columns), BF16), jax.ShapeDtypeStruct((2 * LANE, LANE), jnp.int32)]
        + [first] * pairs,
        in_specs=[OUTSIDE] * 3,
        out_specs=[VECTOR] * (4 + pairs),
        scratch_shapes=[pltpu.SMEM(shear_offsets.shape, jnp.int32), pltpu.SMEM(intersection_widths.shape, jnp.int32)]
        + [pltpu.SemaphoreType.DMA] * 3,
        compiler_params=PARAMS,
        name="pack_first",
    )(*outside)
    first_held = along(chunks, slabs)
    from_left = shifted(toward_right, 1)
    from_right = shifted(toward_left, -1)
    own = chunks[0]
    second = jax.ShapeDtypeStruct((PAIR * planes + 32, LANE), BF16)
    names = list(table)
    staged = pl.pallas_call(
        stage,
        out_shape=[jax.ShapeDtypeStruct(table[name].shape, BF16) for name in names],
        in_specs=[ANYWHERE] + [OUTSIDE] * len(names),
        out_specs=[VECTOR] * len(names),
        scratch_shapes=[pltpu.SemaphoreType.DMA((len(names),))],
        compiler_params=PARAMS,
        name="stage",
    )(toward_left, *[pltpu.with_memory_space_constraint(table[name], pltpu.HBM) for name in names])
    table = dict(zip(names, staged))
    chunks = pl.pallas_call(
        pack_second,
        out_shape=[second] * pairs,
        in_specs=[VECTOR] * 4 + [ANYWHERE],
        out_specs=[VECTOR] * pairs,
        compiler_params=PARAMS,
        name="pack_second",
    )(raw, shift, from_left, from_right, table["two"])
    second_held = along(chunks, slabs)
    first_held[0] = own
    first_held[0] = lax.optimization_barrier((first_held[0], chunks))[0]
    got_first = within(first_held, slabs)
    partial, coarse = pl.pallas_call(
        functools.partial(first_half, slabs, scans),
        out_shape=[
            jax.ShapeDtypeStruct((scans * SLAB_ROWS, columns), F32),
            jax.ShapeDtypeStruct((LEVEL * scans // 2, columns // 2 + LANE), F32),
        ],
        in_specs=[VECTOR] * (4 + slabs),
        out_specs=[VECTOR] * 2,
        scratch_shapes=[
            pltpu.VMEM((slabs + 2, LANE, cut), BF16),
            pltpu.VMEM((4, scans * SLAB_ROWS, cut), BF16),
        ],
        compiler_params=PARAMS,
        name="first_half",
    )(table["rowscan"], table["level"], table["column_first"], table["level_first"], *got_first)
    second_held[0] = chunks[0]
    second_held, partial = lax.optimization_barrier((second_held, partial))
    got_second = within(second_held, slabs)
    return pl.pallas_call(
        functools.partial(second_half, slabs, scans),
        out_shape=[
            jax.ShapeDtypeStruct((SLAB_ROWS, scans, columns), BF16),
            jax.ShapeDtypeStruct((SLAB_ROWS // 2, scans // 2, columns // 2), BF16),
            jax.ShapeDtypeStruct((SLAB_ROWS // 4, scans // 4, columns // 4), BF16),
        ],
        in_specs=[VECTOR] * (8 + slabs),
        out_specs=[OUTSIDE, VECTOR, VECTOR],
        scratch_shapes=[
            pltpu.VMEM((slabs + 2, LANE, 2 * LANE), BF16),
            pltpu.VMEM((16, slabs * LANE), BF16),
            pltpu.VMEM((4, scans * SLAB_ROWS, 2 * LANE), BF16),
            pltpu.VMEM((SLAB_ROWS, scans, columns), BF16),
            pltpu.SemaphoreType.DMA((scans // 16,)),
        ],
        compiler_params=PARAMS,
        name="second_half",
    )(
        table["rowscan"],
        table["level"],
        table["column_last"],
        table["level_last"],
        table["two"],
        table["two_column"],
        partial,
        coarse,
        *got_second,
    )


def solution(mesh):
    placed = (P("slab", None, "tile"), P("slab"), P())
    return jax.shard_map(
        body,
        mesh=mesh,
        in_specs=placed,
        out_specs=(P("slab", None, "tile"), P("slab", None, "tile"), P("slab", None, "tile")),
        check_vma=False,
    )
```

```python
import functools
import math

import jax
import jax.numpy as jnp
import ml_dtypes
import numpy as np
from jax import lax
from jax.experimental import pallas as pl
from jax.experimental.pallas import tpu as pltpu
from jax.sharding import PartitionSpec as P

SLAB_ROWS = 16
STRIP = 6
RADIUS = 4
LOW = 6
HIGH = 4
NEED = SLAB_ROWS + LOW + HIGH
SLOTS = 4 * NEED
LEVEL = 11
LANE = 128
F32 = jnp.float32
BF16 = jnp.bfloat16


def gauss_taps(sigma_value):
    entries = [math.exp(-(j * j) / (2.0 * sigma_value * sigma_value)) for j in range(-RADIUS, RADIUS + 1)]
    weight_sum = sum(entries)
    return np.array([entry / weight_sum for entry in entries], np.float64)


BINOMIAL = np.array([1.0, 4.0, 6.0, 4.0, 1.0], np.float64) / 16.0


def band(weights, source, target):
    reach = len(weights) // 2
    offset = source[None, :] - target[:, None] + reach
    inside = (offset >= 0) & (offset < len(weights))
    return np.where(inside, weights[np.clip(offset, 0, len(weights) - 1)], 0.0)


def two_parts(table):
    high = table.astype(ml_dtypes.bfloat16)
    return [high, (table - high.astype(np.float64)).astype(ml_dtypes.bfloat16)]


def row_scan_table(row_band, scan_band, groups):
    rows_out, rows_in = row_band.shape
    scans_out = scan_band.shape[0]
    scans = scan_band.reshape(scans_out, groups, 4)
    table = np.einsum("yr,sgp->ysgrp", row_band, scans)
    table = table.reshape(rows_out * scans_out, groups, rows_in * 4)
    table = np.pad(table, ((0, 0), (0, 0), (0, LANE - rows_in * 4)))
    return table.reshape(rows_out * scans_out, groups * LANE)


def tables(scans, columns):
    row_in = np.arange(NEED) - LOW
    own = np.arange(SLAB_ROWS)
    near = np.arange(16) - 4
    block = np.arange(8)
    cut = columns - LANE
    rim = np.where(np.arange(LANE) < LANE // 2, columns, -LANE) + np.arange(LANE)
    last = np.concatenate([np.arange(cut, columns), rim])
    touched = np.concatenate([np.arange(cut, columns), np.arange(LANE // 2), np.arange(cut - LANE // 2, cut)])
    rowscan, column_first, column_last = [], [], []
    for sigma, sign in ((1.0, 1.0), (1.6, -1.0)):
        taps = gauss_taps(sigma)
        rowscan += two_parts(row_scan_table(band(taps, row_in, own), band(taps, near, block), 4))
        column_first += two_parts(sign * band(taps, np.arange(4 * LANE) - LANE, np.arange(2 * LANE)).T)
        column_last += two_parts(sign * band(taps, last, touched).T)
    level_rows = 2 * np.arange(LEVEL) - 4
    level_scans = 2 * np.arange(scans // 2)
    level = row_scan_table(
        band(BINOMIAL, row_in, level_rows), band(BINOMIAL, np.arange(scans), level_scans), scans // 4
    )
    edges = np.array([-4, -2, columns, columns + 2])
    targets = np.concatenate([2 * np.arange(columns // 2), edges])
    two = np.einsum(
        "yr,sp->ysrp",
        band(BINOMIAL, np.arange(LEVEL) - 2, 2 * np.arange(4)),
        band(BINOMIAL, np.arange(scans // 2), 2 * np.arange(scans // 4)),
    ).reshape(scans, LEVEL * scans // 2)
    fill = ((0, 0), (0, LANE - 4))
    small = ml_dtypes.bfloat16
    return dict(
        rowscan=np.concatenate(rowscan, 0),
        level=level.astype(small),
        column_first=np.stack(column_first),
        column_last=np.stack(column_last),
        level_first=np.pad(band(BINOMIAL, np.arange(cut), targets).T, fill).astype(small),
        level_last=np.pad(band(BINOMIAL, last, targets).T, fill).astype(small),
        two=two.astype(small),
        two_column=np.pad(band(BINOMIAL, targets // 2, 2 * np.arange(columns // 4)), fill).T.astype(small),
    )


def dot(left, right):
    return jnp.dot(left, right, preferred_element_type=F32)


def dot_rows(left, right):
    return lax.dot_general(left, right, (((1,), (1,)), ((), ())), preferred_element_type=F32)


def place_table(shift, slab, camera):
    slots = shift.shape[0]
    slot = lax.broadcasted_iota(jnp.int32, (slots, 1), 0)
    plane, row = slot & 3, slot >> 2
    source = slab * SLAB_ROWS - LOW + row - shift
    inside = (source >= 0) & (source < camera) & (row < NEED)
    wanted = jnp.where(inside, plane * camera + source, -1)
    lane = lax.broadcasted_iota(jnp.int32, (slots, 4 * camera), 1)
    return jnp.where(lane == wanted, 1.0, 0.0).astype(BF16)


def pack_first(raw_ref, other_ref, shear_ref, other_shear_ref, width_ref, right_ref, left_ref, kept_ref, shift_ref, *refs):
    out_refs, (shears, other_shears, widths, sems) = refs[:-4], refs[-4:]
    loads = [
        pltpu.make_async_copy(source, target, sems.at[index])
        for index, (source, target) in enumerate(
            ((raw_ref, kept_ref), (shear_ref, shears), (other_shear_ref, other_shears), (width_ref, widths))
        )
    ]
    for load in loads:
        load.start()
    camera = raw_ref.shape[0] // 4
    columns = raw_ref.shape[1]
    tile = lax.axis_index("tile")
    tiles = lax.axis_size("tile")
    slab = lax.axis_index("slab")
    lane = lax.broadcasted_iota(jnp.int32, (8, columns), 1)
    line = lax.broadcasted_iota(jnp.int32, (8, columns), 0)
    for load in loads[1:]:
        load.wait()
    right_width = widths[jnp.minimum(tile, tiles - 2)]
    left_width = widths[jnp.maximum(tile - 1, 0)]
    toward_right = jnp.where((lane == columns - right_width - 8 + line) & (line >= 2), 1.0, 0.0).astype(BF16)
    toward_left = jnp.where((lane == left_width + line) & (line < 6), 1.0, 0.0).astype(BF16)
    plane = lax.broadcasted_iota(jnp.int32, shift_ref.shape[1:], 0) & 3
    for owner, values in enumerate((shears, other_shears)):
        shift_ref[owner] = jnp.where(
            plane < 2, jnp.where(plane == 0, values[0], values[1]), jnp.where(plane == 2, values[2], values[3])
        )
    loads[0].wait()
    for step, out_ref in enumerate(out_refs):
        for owner, planes_ref in enumerate((kept_ref, other_ref)):
            table = place_table(shift_ref[owner, :SLOTS, :1], slab ^ (2 * step), camera)
            placed = dot(table, planes_ref[:, : columns - LANE])
            out_ref[owner * SLOTS : (owner + 1) * SLOTS, :] = placed.astype(BF16)
    for owner, planes_ref in enumerate((kept_ref, other_ref)):
        right_ref[8 * owner : 8 * owner + 8, :] = dot_rows(toward_right, planes_ref[...]).astype(BF16)
        left_ref[8 * owner : 8 * owner + 8, :] = dot_rows(toward_left, planes_ref[...]).astype(BF16)


def stage(order_ref, *refs):
    sems, refs = refs[-1], refs[:-1]
    count = len(refs) // 2
    loads = [pltpu.make_async_copy(refs[index], refs[count + index], sems.at[index]) for index in range(count)]
    for load in loads:
        load.start()
    for load in loads:
        load.wait()


def pack_second(raw_ref, other_ref, shift_ref, from_left_ref, from_right_ref, order_ref, *out_refs):
    camera = raw_ref.shape[0] // 4
    columns = raw_ref.shape[1]
    slab = lax.axis_index("slab")
    tile = lax.axis_index("tile")
    right = jnp.where(tile < lax.axis_size("tile") - 1, from_right_ref[...].astype(F32), 0.0)
    left = jnp.where(tile > 0, from_left_ref[...].astype(F32), 0.0)
    for step, out_ref in enumerate(out_refs):
        for owner, planes_ref in enumerate((raw_ref, other_ref)):
            table = place_table(shift_ref[owner, :, :1], slab ^ (2 * step), camera)
            placed = dot(table[:SLOTS], planes_ref[:, columns - LANE :])
            out_ref[owner * SLOTS : (owner + 1) * SLOTS, :] = placed.astype(BF16)
            own = slice(8 * owner, 8 * owner + 8)
            strips = jnp.concatenate([right[own], left[own]], 0).astype(BF16)
            start = 2 * SLOTS + 16 * owner
            out_ref[start : start + 16, :] = dot_rows(strips, table).astype(BF16)


def collect(in_refs, volume, scans):
    slab = lax.axis_index("slab")
    lanes = in_refs[0].shape[-1]
    groups = scans // 4
    outside = jnp.zeros((LANE,) + volume.shape[2:], BF16)
    volume[0] = outside
    volume[groups + 1] = outside
    for index in range(groups):
        group = (slab ^ index) + 1
        start = (index & 1) * SLOTS
        volume[group, :SLOTS, :lanes] = in_refs[index >> 1][start : start + SLOTS, :]
        volume[group, SLOTS:, :lanes] = jnp.zeros((LANE - SLOTS, lanes), BF16)


def split(value):
    high = value.astype(BF16)
    return high, (value - high.astype(F32)).astype(BF16)


def row_scan(rowscan_ref, volume, block, wide):
    rows = 8 * SLAB_ROWS
    both = dot(rowscan_ref[...], volume[2 * block : 2 * block + 4].reshape(4 * LANE, volume.shape[-1]))
    for sigma in range(2):
        total = both[2 * sigma * rows : (2 * sigma + 1) * rows] + both[(2 * sigma + 1) * rows : (2 * sigma + 2) * rows]
        high, low = split(total)
        wide[2 * sigma, block * rows : (block + 1) * rows, :] = high
        wide[2 * sigma + 1, block * rows : (block + 1) * rows, :] = low


def across(wide, rows, lanes, column_ref, taken):
    total = None
    for sigma in range(2):
        high, low = wide[2 * sigma, rows, lanes], wide[2 * sigma + 1, rows, lanes]
        part = dot(high, column_ref[2 * sigma, taken]) + dot(low, column_ref[2 * sigma, taken])
        part = part + dot(high, column_ref[2 * sigma + 1, taken])
        total = part if total is None else total + part
    return total


def level_part(level_ref, level_column_ref, volume, scans):
    groups = scans // 4
    high, low = split(dot(level_ref[...], volume[1 : groups + 1].reshape(groups * LANE, volume.shape[-1])))
    return dot(high, level_column_ref[...]) + dot(low, level_column_ref[...])


def first_half(count, scans, rowscan_ref, level_ref, column_ref, level_column_ref, *refs):
    in_refs, (partial_ref, coarse_ref, volume, wide) = refs[:count], refs[count:]
    collect(in_refs, volume, scans)
    for block in range(scans // 8):
        row_scan(rowscan_ref, volume, block, wide)
    cut = wide.shape[-1]
    for start in range(0, partial_ref.shape[1], 2 * LANE):
        low, high = max(start - LANE, 0), min(start + 3 * LANE, cut)
        taken = slice(low - start + LANE, high - start + LANE)
        partial_ref[:, start : start + 2 * LANE] = across(wide, slice(None), slice(low, high), column_ref, taken)
    coarse_ref[...] = level_part(level_ref, level_column_ref, volume, scans)


def second_half(count, scans, rowscan_ref, level_ref, column_ref, level_column_ref, two_ref, two_column_ref, *refs):
    partial_ref, coarse_ref, *in_refs = refs[: 2 + count]
    difference_ref, one_ref, second_ref, volume, strips, wide, held, sems = refs[2 + count :]
    slab = lax.axis_index("slab")
    slabs = lax.axis_size("slab")
    tile = lax.axis_index("tile")
    tiles = lax.axis_size("tile")
    groups = scans // 4
    columns = partial_ref.shape[1]
    cut = columns - LANE
    collect(in_refs, volume, scans)
    for index in range(groups):
        place = pl.multiple_of((slab ^ index) * LANE, LANE)
        start = 2 * SLOTS + 16 * (index & 1)
        strips[:, pl.ds(place, LANE)] = in_refs[index >> 1][start : start + 16, :]
    line = lax.broadcasted_iota(jnp.int32, (16, LANE), 0)
    lane = lax.broadcasted_iota(jnp.int32, (16, LANE), 1)
    spread = jnp.where(lane == jnp.where(line < 8, line, line + LANE - 16), 1.0, 0.0).astype(BF16)
    rim = lax.dot_general(strips[...], spread, (((0,), (0,)), ((), ())), preferred_element_type=F32)
    volume[1 : groups + 1, :, LANE:] = rim.astype(BF16).reshape(groups, LANE, LANE)

    level = coarse_ref[...] + level_part(level_ref, level_column_ref, volume, scans)
    half = columns // 2
    shape = (LEVEL, scans // 2, level.shape[-1])
    level = level.reshape(shape)
    row = slab * (SLAB_ROWS // 2) - 2 + lax.broadcasted_iota(jnp.int32, shape, 0)
    place = lax.broadcasted_iota(jnp.int32, shape, 2) - half
    keep = (row >= 0) & (row < slabs * (SLAB_ROWS // 2))
    keep = keep & ((place < 0) | (place >= 2) | (tile > 0)) & ((place < 2) | (tile < tiles - 1))
    ready = jnp.where(keep, level, 0.0).astype(BF16)
    one_ref[...] = ready[2:10, :, :half]
    high, low = split(dot(two_ref[...], ready.reshape(LEVEL * scans // 2, level.shape[-1])))
    second = dot(high, two_column_ref[...]) + dot(low, two_column_ref[...])
    second_ref[...] = second.reshape(second_ref.shape).astype(BF16)

    copies = []
    rows = 8 * SLAB_ROWS
    left = lax.broadcasted_iota(jnp.int32, (2 * rows, LANE), 1) < LANE // 2
    for pair in range(scans // 16):
        for block in (2 * pair, 2 * pair + 1):
            row_scan(rowscan_ref, volume, block, wide)
        here = slice(2 * pair * rows, 2 * (pair + 1) * rows)
        late = across(wide, here, slice(None), column_ref, slice(None))
        ends = late[:, LANE:]
        for start in range(0, columns, LANE):
            total = partial_ref[here, start : start + LANE]
            if start == cut:
                total = total + late[:, :LANE]
            if start == 0:
                total = total + jnp.where(left, ends, 0.0)
            if start == cut - LANE:
                total = total + jnp.where(left, 0.0, ends)
            total = total.reshape(2, SLAB_ROWS, 8, LANE)
            joined = jnp.concatenate([total[0], total[1]], 1)
            held[:, 16 * pair : 16 * pair + 16, start : start + LANE] = joined.astype(BF16)
        copy = pltpu.make_async_copy(
            held.at[:, 16 * pair : 16 * pair + 16, :], difference_ref.at[:, 16 * pair : 16 * pair + 16, :], sems.at[pair]
        )
        copy.start()
        copies.append(copy)
    for copy in copies:
        copy.wait()


VECTOR = pl.BlockSpec(memory_space=pltpu.VMEM)
ANYWHERE = pl.BlockSpec(memory_space=pl.ANY)
OUTSIDE = pl.BlockSpec(memory_space=pltpu.HBM)
PARAMS = pltpu.CompilerParams(vmem_limit_bytes=20 * 1024 * 1024)


def along(chunks, slabs):
    got = list(chunks)
    for step in sorted(range(1, len(chunks)), key=lambda step: (-(step & -step), step)):
        got[step] = lax.ppermute(chunks[step], "slab", [(i, i ^ (2 * step)) for i in range(slabs)])
    return got


def shifted(block, distance):
    count = lax.axis_size("tile")
    return lax.ppermute(block, "tile", [(i, (i + distance) % count) for i in range(count)])


def body(raw_stack, shear_offsets, intersection_widths):
    slabs = lax.axis_size("slab")
    planes, camera, columns = raw_stack.shape
    scans = planes * slabs
    cut = columns - LANE
    pairs = slabs // 2
    table = {name: jnp.asarray(value) for name, value in tables(scans, columns).items()}
    raw = raw_stack.reshape(planes * camera, columns)
    swap = [(i, i ^ 1) for i in range(slabs)]
    other = lax.ppermute(raw, "slab", swap)
    other_shear = lax.ppermute(shear_offsets, "slab", swap)
    outside = [pltpu.with_memory_space_constraint(each, pltpu.HBM) for each in (raw, shear_offsets, intersection_widths)]
    strip = jax.ShapeDtypeStruct((16, planes * camera), BF16)
    first = jax.ShapeDtypeStruct((2 * SLOTS, cut), BF16)
    toward_right, toward_left, raw, shift, *chunks = pl.pallas_call(
        pack_first,
        out_shape=[
            strip,
            strip,
            jax.ShapeDtypeStruct((planes * camera, columns), BF16),
            jax.ShapeDtypeStruct((2, LANE, LANE), jnp.int32),
        ]
        + [first] * pairs,
        in_specs=[OUTSIDE, VECTOR, OUTSIDE, ANYWHERE, OUTSIDE],
        out_specs=[VECTOR] * (4 + pairs),
        scratch_shapes=[
            pltpu.SMEM(shear_offsets.shape, jnp.int32),
            pltpu.SMEM(shear_offsets.shape, jnp.int32),
            pltpu.SMEM(intersection_widths.shape, jnp.int32),
            pltpu.SemaphoreType.DMA((4,)),
        ],
        compiler_params=PARAMS,
        name="pack_first",
    )(outside[0], other, outside[1], other_shear, outside[2])
    got_first = along(chunks, slabs)
    from_left = shifted(toward_right, 1)
    from_right = shifted(toward_left, -1)
    second = jax.ShapeDtypeStruct((2 * SLOTS + 32, LANE), BF16)
    names = list(table)
    staged = pl.pallas_call(
        stage,
        out_shape=[jax.ShapeDtypeStruct(table[name].shape, BF16) for name in names],
        in_specs=[ANYWHERE] + [OUTSIDE] * len(names),
        out_specs=[VECTOR] * len(names),
        scratch_shapes=[pltpu.SemaphoreType.DMA((len(names),))],
        compiler_params=PARAMS,
        name="stage",
    )(toward_left, *[pltpu.with_memory_space_constraint(table[name], pltpu.HBM) for name in names])
    table = dict(zip(names, staged))
    chunks = pl.pallas_call(
        pack_second,
        out_shape=[second] * pairs,
        in_specs=[VECTOR] * 5 + [ANYWHERE],
        out_specs=[VECTOR] * pairs,
        compiler_params=PARAMS,
        name="pack_second",
    )(raw, other, shift, from_left, from_right, table["two"])
    chunks, got_first[2] = lax.optimization_barrier((chunks, got_first[2]))
    got_second = along(chunks, slabs)
    partial, coarse = pl.pallas_call(
        functools.partial(first_half, pairs, scans),
        out_shape=[
            jax.ShapeDtypeStruct((scans * SLAB_ROWS, columns), F32),
            jax.ShapeDtypeStruct((LEVEL * scans // 2, columns // 2 + LANE), F32),
        ],
        in_specs=[VECTOR] * (4 + pairs),
        out_specs=[VECTOR] * 2,
        scratch_shapes=[
            pltpu.VMEM((slabs + 2, LANE, cut), BF16),
            pltpu.VMEM((4, scans * SLAB_ROWS, cut), BF16),
        ],
        compiler_params=PARAMS,
        name="first_half",
    )(table["rowscan"], table["level"], table["column_first"], table["level_first"], *got_first)
    got_second, partial = lax.optimization_barrier((got_second, partial))
    return pl.pallas_call(
        functools.partial(second_half, pairs, scans),
        out_shape=[
            jax.ShapeDtypeStruct((SLAB_ROWS, scans, columns), BF16),
            jax.ShapeDtypeStruct((SLAB_ROWS // 2, scans // 2, columns // 2), BF16),
            jax.ShapeDtypeStruct((SLAB_ROWS // 4, scans // 4, columns // 4), BF16),
        ],
        in_specs=[VECTOR] * (8 + pairs),
        out_specs=[OUTSIDE, VECTOR, VECTOR],
        scratch_shapes=[
            pltpu.VMEM((slabs + 2, LANE, 2 * LANE), BF16),
            pltpu.VMEM((16, slabs * LANE), BF16),
            pltpu.VMEM((4, scans * SLAB_ROWS, 2 * LANE), BF16),
            pltpu.VMEM((SLAB_ROWS, scans, columns), BF16),
            pltpu.SemaphoreType.DMA((scans // 16,)),
        ],
        compiler_params=PARAMS,
        name="second_half",
    )(
        table["rowscan"],
        table["level"],
        table["column_last"],
        table["level_last"],
        table["two"],
        table["two_column"],
        partial,
        coarse,
        *got_second,
    )


def solution(mesh):
    placed = (P("slab", None, "tile"), P("slab"), P())
    return jax.shard_map(
        body,
        mesh=mesh,
        in_specs=placed,
        out_specs=(P("slab", None, "tile"), P("slab", None, "tile"), P("slab", None, "tile")),
        check_vma=False,
    )
```

```python
import functools
import math

import jax
import jax.numpy as jnp
import ml_dtypes
import numpy as np
from jax import lax
from jax.experimental import pallas as pl
from jax.experimental.pallas import tpu as pltpu
from jax.sharding import PartitionSpec as P

SLAB_ROWS = 16
STRIP = 6
RADIUS = 4
LOW = 6
HIGH = 4
NEED = SLAB_ROWS + LOW + HIGH
SLOTS = 4 * NEED
LEVEL = 11
LANE = 128
F32 = jnp.float32
BF16 = jnp.bfloat16


def gauss_taps(sigma_value):
    entries = [math.exp(-(j * j) / (2.0 * sigma_value * sigma_value)) for j in range(-RADIUS, RADIUS + 1)]
    weight_sum = sum(entries)
    return np.array([entry / weight_sum for entry in entries], np.float64)


BINOMIAL = np.array([1.0, 4.0, 6.0, 4.0, 1.0], np.float64) / 16.0


def band(weights, source, target):
    reach = len(weights) // 2
    offset = source[None, :] - target[:, None] + reach
    inside = (offset >= 0) & (offset < len(weights))
    return np.where(inside, weights[np.clip(offset, 0, len(weights) - 1)], 0.0)


def two_parts(table):
    high = table.astype(ml_dtypes.bfloat16)
    return [high, (table - high.astype(np.float64)).astype(ml_dtypes.bfloat16)]


def row_scan_table(row_band, scan_band, groups):
    rows_out, rows_in = row_band.shape
    scans_out = scan_band.shape[0]
    scans = scan_band.reshape(scans_out, groups, 4)
    table = np.einsum("yr,sgp->ysgrp", row_band, scans)
    table = table.reshape(rows_out * scans_out, groups, rows_in * 4)
    table = np.pad(table, ((0, 0), (0, 0), (0, LANE - rows_in * 4)))
    return table.reshape(rows_out * scans_out, groups * LANE)


def tables(scans, columns):
    row_in = np.arange(NEED) - LOW
    own = np.arange(SLAB_ROWS)
    near = np.arange(16) - 4
    block = np.arange(8)
    cut = columns - LANE
    rim = np.where(np.arange(LANE) < LANE // 2, columns, -LANE) + np.arange(LANE)
    last = np.concatenate([np.arange(cut, columns), rim])
    touched = np.concatenate([np.arange(cut, columns), np.arange(LANE // 2), np.arange(cut - LANE // 2, cut)])
    rowscan, column_first, column_last = [], [], []
    for sigma, sign in ((1.0, 1.0), (1.6, -1.0)):
        taps = gauss_taps(sigma)
        rowscan += two_parts(row_scan_table(band(taps, row_in, own), band(taps, near, block), 4))
        column_first += two_parts(sign * band(taps, np.arange(4 * LANE) - LANE, np.arange(2 * LANE)).T)
        column_last += two_parts(sign * band(taps, last, touched).T)
    level_rows = 2 * np.arange(LEVEL) - 4
    level_scans = 2 * np.arange(scans // 2)
    level = row_scan_table(
        band(BINOMIAL, row_in, level_rows), band(BINOMIAL, np.arange(scans), level_scans), scans // 4
    )
    edges = np.array([-4, -2, columns, columns + 2])
    targets = np.concatenate([2 * np.arange(columns // 2), edges])
    two = np.einsum(
        "yr,sp->ysrp",
        band(BINOMIAL, np.arange(LEVEL) - 2, 2 * np.arange(4)),
        band(BINOMIAL, np.arange(scans // 2), 2 * np.arange(scans // 4)),
    ).reshape(scans, LEVEL * scans // 2)
    fill = ((0, 0), (0, LANE - 4))
    small = ml_dtypes.bfloat16
    return dict(
        rowscan=np.concatenate(rowscan, 0),
        level=level.astype(small),
        column_first=np.stack(column_first),
        column_last=np.stack(column_last),
        level_first=np.pad(band(BINOMIAL, np.arange(cut), targets).T, fill).astype(small),
        level_last=np.pad(band(BINOMIAL, last, targets).T, fill).astype(small),
        two=two.astype(small),
        two_column=np.pad(band(BINOMIAL, targets // 2, 2 * np.arange(columns // 4)), fill).T.astype(small),
    )


def dot(left, right):
    return jnp.dot(left, right, preferred_element_type=F32)


def dot_rows(left, right):
    return lax.dot_general(left, right, (((1,), (1,)), ((), ())), preferred_element_type=F32)


def place_table(shift, slab, camera):
    slots = shift.shape[0]
    slot = lax.broadcasted_iota(jnp.int32, (slots, 1), 0)
    plane, row = slot & 3, slot >> 2
    source = slab * SLAB_ROWS - LOW + row - shift
    inside = (source >= 0) & (source < camera) & (row < NEED)
    wanted = jnp.where(inside, plane * camera + source, -1)
    lane = lax.broadcasted_iota(jnp.int32, (slots, 4 * camera), 1)
    return jnp.where(lane == wanted, 1.0, 0.0).astype(BF16)


def pack_first(raw_ref, other_ref, shear_ref, other_shear_ref, width_ref, right_ref, left_ref, kept_ref, shift_ref, *refs):
    out_refs, (shears, other_shears, widths, sems) = refs[:-4], refs[-4:]
    loads = [
        pltpu.make_async_copy(source, target, sems.at[index])
        for index, (source, target) in enumerate(
            ((raw_ref, kept_ref), (shear_ref, shears), (other_shear_ref, other_shears), (width_ref, widths))
        )
    ]
    for load in loads:
        load.start()
    camera = raw_ref.shape[0] // 4
    columns = raw_ref.shape[1]
    tile = lax.axis_index("tile")
    tiles = lax.axis_size("tile")
    slab = lax.axis_index("slab")
    lane = lax.broadcasted_iota(jnp.int32, (8, columns), 1)
    line = lax.broadcasted_iota(jnp.int32, (8, columns), 0)
    for load in loads[1:]:
        load.wait()
    right_width = widths[jnp.minimum(tile, tiles - 2)]
    left_width = widths[jnp.maximum(tile - 1, 0)]
    toward_right = jnp.where((lane == columns - right_width - 8 + line) & (line >= 2), 1.0, 0.0).astype(BF16)
    toward_left = jnp.where((lane == left_width + line) & (line < 6), 1.0, 0.0).astype(BF16)
    plane = lax.broadcasted_iota(jnp.int32, shift_ref.shape[1:], 0) & 3
    for owner, values in enumerate((shears, other_shears)):
        shift_ref[owner] = jnp.where(
            plane < 2, jnp.where(plane == 0, values[0], values[1]), jnp.where(plane == 2, values[2], values[3])
        )
    loads[0].wait()
    for step, out_ref in enumerate(out_refs):
        for owner, planes_ref in enumerate((kept_ref, other_ref)):
            table = place_table(shift_ref[owner, :SLOTS, :1], slab ^ (2 * step), camera)
            placed = dot(table, planes_ref[:, : columns - LANE])
            out_ref[owner * SLOTS : (owner + 1) * SLOTS, :] = placed.astype(BF16)
    for owner, planes_ref in enumerate((kept_ref, other_ref)):
        right_ref[8 * owner : 8 * owner + 8, :] = dot_rows(toward_right, planes_ref[...]).astype(BF16)
        left_ref[8 * owner : 8 * owner + 8, :] = dot_rows(toward_left, planes_ref[...]).astype(BF16)


def stage(order_ref, *refs):
    sems, refs = refs[-1], refs[:-1]
    count = len(refs) // 2
    loads = [pltpu.make_async_copy(refs[index], refs[count + index], sems.at[index]) for index in range(count)]
    for load in loads:
        load.start()
    for load in loads:
        load.wait()


def pack_second(raw_ref, other_ref, shift_ref, from_left_ref, from_right_ref, order_ref, *out_refs):
    camera = raw_ref.shape[0] // 4
    columns = raw_ref.shape[1]
    slab = lax.axis_index("slab")
    tile = lax.axis_index("tile")
    right = jnp.where(tile < lax.axis_size("tile") - 1, from_right_ref[...].astype(F32), 0.0)
    left = jnp.where(tile > 0, from_left_ref[...].astype(F32), 0.0)
    for step, out_ref in enumerate(out_refs):
        for owner, planes_ref in enumerate((raw_ref, other_ref)):
            table = place_table(shift_ref[owner, :, :1], slab ^ (2 * step), camera)
            placed = dot(table[:SLOTS], planes_ref[:, columns - LANE :])
            out_ref[owner * SLOTS : (owner + 1) * SLOTS, :] = placed.astype(BF16)
            own = slice(8 * owner, 8 * owner + 8)
            strips = jnp.concatenate([right[own], left[own]], 0).astype(BF16)
            start = 2 * SLOTS + 16 * owner
            out_ref[start : start + 16, :] = dot_rows(strips, table).astype(BF16)


def collect(in_refs, volume, scans):
    slab = lax.axis_index("slab")
    lanes = in_refs[0].shape[-1]
    groups = scans // 4
    outside = jnp.zeros((LANE,) + volume.shape[2:], BF16)
    volume[0] = outside
    volume[groups + 1] = outside
    for index in range(groups):
        group = (slab ^ index) + 1
        start = (index & 1) * SLOTS
        volume[group, :SLOTS, :lanes] = in_refs[index >> 1][start : start + SLOTS, :]
        volume[group, SLOTS:, :lanes] = jnp.zeros((LANE - SLOTS, lanes), BF16)


def split(value):
    high = value.astype(BF16)
    return high, (value - high.astype(F32)).astype(BF16)


def row_scan(rowscan_ref, volume, block, wide):
    rows = 8 * SLAB_ROWS
    both = dot(rowscan_ref[...], volume[2 * block : 2 * block + 4].reshape(4 * LANE, volume.shape[-1]))
    for sigma in range(2):
        total = both[2 * sigma * rows : (2 * sigma + 1) * rows] + both[(2 * sigma + 1) * rows : (2 * sigma + 2) * rows]
        high, low = split(total)
        wide[2 * sigma, block * rows : (block + 1) * rows, :] = high
        wide[2 * sigma + 1, block * rows : (block + 1) * rows, :] = low


def across(wide, rows, lanes, column_ref, taken):
    total = None
    for sigma in range(2):
        high, low = wide[2 * sigma, rows, lanes], wide[2 * sigma + 1, rows, lanes]
        part = dot(high, column_ref[2 * sigma, taken]) + dot(low, column_ref[2 * sigma, taken])
        part = part + dot(high, column_ref[2 * sigma + 1, taken])
        total = part if total is None else total + part
    return total


def level_part(level_ref, level_column_ref, volume, scans):
    groups = scans // 4
    high, low = split(dot(level_ref[...], volume[1 : groups + 1].reshape(groups * LANE, volume.shape[-1])))
    return dot(high, level_column_ref[...]) + dot(low, level_column_ref[...])


def first_half(count, scans, rowscan_ref, level_ref, column_ref, level_column_ref, *refs):
    in_refs, (partial_ref, coarse_ref, volume, wide) = refs[:count], refs[count:]
    collect(in_refs, volume, scans)
    for block in range(scans // 8):
        row_scan(rowscan_ref, volume, block, wide)
    cut = wide.shape[-1]
    for start in range(0, partial_ref.shape[1], 2 * LANE):
        low, high = max(start - LANE, 0), min(start + 3 * LANE, cut)
        taken = slice(low - start + LANE, high - start + LANE)
        partial_ref[:, start : start + 2 * LANE] = across(wide, slice(None), slice(low, high), column_ref, taken)
    coarse_ref[...] = level_part(level_ref, level_column_ref, volume, scans)


def second_half(count, scans, rowscan_ref, level_ref, column_ref, level_column_ref, two_ref, two_column_ref, *refs):
    partial_ref, coarse_ref, *in_refs = refs[: 2 + count]
    difference_ref, one_ref, second_ref, volume, strips, wide, held, held_one, held_second, sems = refs[2 + count :]
    slab = lax.axis_index("slab")
    slabs = lax.axis_size("slab")
    tile = lax.axis_index("tile")
    tiles = lax.axis_size("tile")
    groups = scans // 4
    columns = partial_ref.shape[1]
    cut = columns - LANE
    collect(in_refs, volume, scans)
    for index in range(groups):
        place = pl.multiple_of((slab ^ index) * LANE, LANE)
        start = 2 * SLOTS + 16 * (index & 1)
        strips[:, pl.ds(place, LANE)] = in_refs[index >> 1][start : start + 16, :]
    line = lax.broadcasted_iota(jnp.int32, (16, LANE), 0)
    lane = lax.broadcasted_iota(jnp.int32, (16, LANE), 1)
    spread = jnp.where(lane == jnp.where(line < 8, line, line + LANE - 16), 1.0, 0.0).astype(BF16)
    rim = lax.dot_general(strips[...], spread, (((0,), (0,)), ((), ())), preferred_element_type=F32)
    volume[1 : groups + 1, :, LANE:] = rim.astype(BF16).reshape(groups, LANE, LANE)

    copies = []
    rows = 8 * SLAB_ROWS
    left = lax.broadcasted_iota(jnp.int32, (2 * rows, LANE), 1) < LANE // 2
    for pair in range(scans // 16):
        for block in (2 * pair, 2 * pair + 1):
            row_scan(rowscan_ref, volume, block, wide)
        here = slice(2 * pair * rows, 2 * (pair + 1) * rows)
        late = across(wide, here, slice(None), column_ref, slice(None))
        ends = late[:, LANE:]
        for start in range(0, columns, LANE):
            total = partial_ref[here, start : start + LANE]
            if start == cut:
                total = total + late[:, :LANE]
            if start == 0:
                total = total + jnp.where(left, ends, 0.0)
            if start == cut - LANE:
                total = total + jnp.where(left, 0.0, ends)
            total = total.reshape(2, SLAB_ROWS, 8, LANE)
            joined = jnp.concatenate([total[0], total[1]], 1)
            held[:, 16 * pair : 16 * pair + 16, start : start + LANE] = joined.astype(BF16)
        copy = pltpu.make_async_copy(
            held.at[:, 16 * pair : 16 * pair + 16, :], difference_ref.at[:, 16 * pair : 16 * pair + 16, :], sems.at[pair]
        )
        copy.start()
        copies.append(copy)
    level = coarse_ref[...] + level_part(level_ref, level_column_ref, volume, scans)
    half = columns // 2
    shape = (LEVEL, scans // 2, level.shape[-1])
    level = level.reshape(shape)
    row = slab * (SLAB_ROWS // 2) - 2 + lax.broadcasted_iota(jnp.int32, shape, 0)
    place = lax.broadcasted_iota(jnp.int32, shape, 2) - half
    keep = (row >= 0) & (row < slabs * (SLAB_ROWS // 2))
    keep = keep & ((place < 0) | (place >= 2) | (tile > 0)) & ((place < 2) | (tile < tiles - 1))
    ready = jnp.where(keep, level, 0.0).astype(BF16)
    held_one[...] = ready[2:10, :, :half]
    copy = pltpu.make_async_copy(held_one, one_ref, sems.at[scans // 16])
    copy.start()
    copies.append(copy)

    high, low = split(dot(two_ref[...], ready.reshape(LEVEL * scans // 2, level.shape[-1])))
    second = dot(high, two_column_ref[...]) + dot(low, two_column_ref[...])
    held_second[...] = second.reshape(second_ref.shape).astype(BF16)
    copy = pltpu.make_async_copy(held_second, second_ref, sems.at[scans // 16 + 1])
    copy.start()
    copies.append(copy)

    for copy in copies:
        copy.wait()


VECTOR = pl.BlockSpec(memory_space=pltpu.VMEM)
ANYWHERE = pl.BlockSpec(memory_space=pl.ANY)
OUTSIDE = pl.BlockSpec(memory_space=pltpu.HBM)
PARAMS = pltpu.CompilerParams(vmem_limit_bytes=20 * 1024 * 1024)


def along(chunks, slabs):
    got = list(chunks)
    for step in sorted(range(1, len(chunks)), key=lambda step: (-(step & -step), step)):
        got[step] = lax.ppermute(chunks[step], "slab", [(i, i ^ (2 * step)) for i in range(slabs)])
    return got


def shifted(block, distance):
    count = lax.axis_size("tile")
    return lax.ppermute(block, "tile", [(i, (i + distance) % count) for i in range(count)])


def body(raw_stack, shear_offsets, intersection_widths):
    slabs = lax.axis_size("slab")
    planes, camera, columns = raw_stack.shape
    scans = planes * slabs
    cut = columns - LANE
    pairs = slabs // 2
    table = {name: jnp.asarray(value) for name, value in tables(scans, columns).items()}
    raw = raw_stack.reshape(planes * camera, columns)
    swap = [(i, i ^ 1) for i in range(slabs)]
    other = lax.ppermute(raw, "slab", swap)
    other_shear = lax.ppermute(shear_offsets, "slab", swap)
    outside = [pltpu.with_memory_space_constraint(each, pltpu.HBM) for each in (raw, shear_offsets, intersection_widths)]
    strip = jax.ShapeDtypeStruct((16, planes * camera), BF16)
    first = jax.ShapeDtypeStruct((2 * SLOTS, cut), BF16)
    toward_right, toward_left, raw, shift, *chunks = pl.pallas_call(
        pack_first,
        out_shape=[
            strip,
            strip,
            jax.ShapeDtypeStruct((planes * camera, columns), BF16),
            jax.ShapeDtypeStruct((2, LANE, LANE), jnp.int32),
        ]
        + [first] * pairs,
        in_specs=[OUTSIDE, VECTOR, OUTSIDE, ANYWHERE, OUTSIDE],
        out_specs=[VECTOR] * (4 + pairs),
        scratch_shapes=[
            pltpu.SMEM(shear_offsets.shape, jnp.int32),
            pltpu.SMEM(shear_offsets.shape, jnp.int32),
            pltpu.SMEM(intersection_widths.shape, jnp.int32),
            pltpu.SemaphoreType.DMA((4,)),
        ],
        compiler_params=PARAMS,
        name="pack_first",
    )(outside[0], other, outside[1], other_shear, outside[2])
    got_first = along(chunks, slabs)
    from_left = shifted(toward_right, 1)
    from_right = shifted(toward_left, -1)
    second = jax.ShapeDtypeStruct((2 * SLOTS + 32, LANE), BF16)
    names = list(table)
    staged = pl.pallas_call(
        stage,
        out_shape=[jax.ShapeDtypeStruct(table[name].shape, BF16) for name in names],
        in_specs=[ANYWHERE] + [OUTSIDE] * len(names),
        out_specs=[VECTOR] * len(names),
        scratch_shapes=[pltpu.SemaphoreType.DMA((len(names),))],
        compiler_params=PARAMS,
        name="stage",
    )(toward_left, *[pltpu.with_memory_space_constraint(table[name], pltpu.HBM) for name in names])
    table = dict(zip(names, staged))
    chunks = pl.pallas_call(
        pack_second,
        out_shape=[second] * pairs,
        in_specs=[VECTOR] * 5 + [ANYWHERE],
        out_specs=[VECTOR] * pairs,
        compiler_params=PARAMS,
        name="pack_second",
    )(raw, other, shift, from_left, from_right, table["two"])
    chunks, got_first[2] = lax.optimization_barrier((chunks, got_first[2]))
    got_second = along(chunks, slabs)
    partial, coarse = pl.pallas_call(
        functools.partial(first_half, pairs, scans),
        out_shape=[
            jax.ShapeDtypeStruct((scans * SLAB_ROWS, columns), F32),
            jax.ShapeDtypeStruct((LEVEL * scans // 2, columns // 2 + LANE), F32),
        ],
        in_specs=[VECTOR] * (4 + pairs),
        out_specs=[VECTOR] * 2,
        scratch_shapes=[
            pltpu.VMEM((slabs + 2, LANE, cut), BF16),
            pltpu.VMEM((4, scans * SLAB_ROWS, cut), BF16),
        ],
        compiler_params=PARAMS,
        name="first_half",
    )(table["rowscan"], table["level"], table["column_first"], table["level_first"], *got_first)
    got_second, partial = lax.optimization_barrier((got_second, partial))
    return pl.pallas_call(
        functools.partial(second_half, pairs, scans),
        out_shape=[
            jax.ShapeDtypeStruct((SLAB_ROWS, scans, columns), BF16),
            jax.ShapeDtypeStruct((SLAB_ROWS // 2, scans // 2, columns // 2), BF16),
            jax.ShapeDtypeStruct((SLAB_ROWS // 4, scans // 4, columns // 4), BF16),
        ],
        in_specs=[VECTOR] * (8 + pairs),
        out_specs=[OUTSIDE] * 3,
        scratch_shapes=[
            pltpu.VMEM((slabs + 2, LANE, 2 * LANE), BF16),
            pltpu.VMEM((16, slabs * LANE), BF16),
            pltpu.VMEM((4, scans * SLAB_ROWS, 2 * LANE), BF16),
            pltpu.VMEM((SLAB_ROWS, scans, columns), BF16),
            pltpu.VMEM((SLAB_ROWS // 2, scans // 2, columns // 2), BF16),
            pltpu.VMEM((SLAB_ROWS // 4, scans // 4, columns // 4), BF16),
            pltpu.SemaphoreType.DMA((scans // 16 + 2,)),
        ],
        compiler_params=PARAMS,
        name="second_half",
    )(
        table["rowscan"],
        table["level"],
        table["column_last"],
        table["level_last"],
        table["two"],
        table["two_column"],
        partial,
        coarse,
        *got_second,
    )


def solution(mesh):
    placed = (P("slab", None, "tile"), P("slab"), P())
    return jax.shard_map(
        body,
        mesh=mesh,
        in_specs=placed,
        out_specs=(P("slab", None, "tile"), P("slab", None, "tile"), P("slab", None, "tile")),
        check_vma=False,
    )
```

```python
import functools
import math

import jax
import jax.numpy as jnp
import ml_dtypes
import numpy as np
from jax import lax
from jax.experimental import pallas as pl
from jax.experimental.pallas import tpu as pltpu
from jax.sharding import PartitionSpec as P

SLAB_ROWS = 16
STRIP = 6
RADIUS = 4
LOW = 6
HIGH = 4
NEED = SLAB_ROWS + LOW + HIGH
SLOTS = 4 * NEED
LEVEL = 11
LANE = 128
F32 = jnp.float32
BF16 = jnp.bfloat16


def gauss_taps(sigma_value):
    entries = [math.exp(-(j * j) / (2.0 * sigma_value * sigma_value)) for j in range(-RADIUS, RADIUS + 1)]
    weight_sum = sum(entries)
    return np.array([entry / weight_sum for entry in entries], np.float64)


BINOMIAL = np.array([1.0, 4.0, 6.0, 4.0, 1.0], np.float64) / 16.0


def band(weights, source, target):
    reach = len(weights) // 2
    offset = source[None, :] - target[:, None] + reach
    inside = (offset >= 0) & (offset < len(weights))
    return np.where(inside, weights[np.clip(offset, 0, len(weights) - 1)], 0.0)


def two_parts(table):
    high = table.astype(ml_dtypes.bfloat16)
    return [high, (table - high.astype(np.float64)).astype(ml_dtypes.bfloat16)]


def row_scan_table(row_band, scan_band, groups):
    rows_out, rows_in = row_band.shape
    scans_out = scan_band.shape[0]
    scans = scan_band.reshape(scans_out, groups, 4)
    table = np.einsum("yr,sgp->ysgrp", row_band, scans)
    table = table.reshape(rows_out * scans_out, groups, rows_in * 4)
    table = np.pad(table, ((0, 0), (0, 0), (0, LANE - rows_in * 4)))
    return table.reshape(rows_out * scans_out, groups * LANE)


def tables(scans, columns):
    row_in = np.arange(NEED) - LOW
    own = np.arange(SLAB_ROWS)
    near = np.arange(16) - 4
    block = np.arange(8)
    cut = columns - LANE
    rim = np.where(np.arange(LANE) < LANE // 2, columns, -LANE) + np.arange(LANE)
    last = np.concatenate([np.arange(cut, columns), rim])
    touched = np.concatenate([np.arange(cut, columns), np.arange(LANE // 2), np.arange(cut - LANE // 2, cut)])
    rowscan, column_first, column_last = [], [], []
    for sigma, sign in ((1.0, 1.0), (1.6, -1.0)):
        taps = gauss_taps(sigma)
        rowscan += two_parts(row_scan_table(band(taps, row_in, own), band(taps, near, block), 4))
        column_first += two_parts(sign * band(taps, np.arange(4 * LANE) - LANE, np.arange(2 * LANE)).T)
        column_last += two_parts(sign * band(taps, last, touched).T)
    level_rows = 2 * np.arange(LEVEL) - 4
    level_scans = 2 * np.arange(scans // 2)
    level = row_scan_table(
        band(BINOMIAL, row_in, level_rows), band(BINOMIAL, np.arange(scans), level_scans), scans // 4
    )
    edges = np.array([-4, -2, columns, columns + 2])
    targets = np.concatenate([2 * np.arange(columns // 2), edges])
    two = np.einsum(
        "yr,sp->ysrp",
        band(BINOMIAL, np.arange(LEVEL) - 2, 2 * np.arange(4)),
        band(BINOMIAL, np.arange(scans // 2), 2 * np.arange(scans // 4)),
    ).reshape(scans, LEVEL * scans // 2)
    fill = ((0, 0), (0, LANE - 4))
    small = ml_dtypes.bfloat16
    return dict(
        rowscan=np.concatenate(rowscan, 0),
        level=level.astype(small),
        column_first=np.stack(column_first),
        column_last=np.stack(column_last),
        level_first=np.pad(band(BINOMIAL, np.arange(cut), targets).T, fill).astype(small),
        level_last=np.pad(band(BINOMIAL, last, targets).T, fill).astype(small),
        two=two.astype(small),
        two_column=np.pad(band(BINOMIAL, targets // 2, 2 * np.arange(columns // 4)), fill).T.astype(small),
    )


def dot(left, right):
    return jnp.dot(left, right, preferred_element_type=F32)


def dot_rows(left, right):
    return lax.dot_general(left, right, (((1,), (1,)), ((), ())), preferred_element_type=F32)


def place_table(shift, slab, camera):
    slots = shift.shape[0]
    slot = lax.broadcasted_iota(jnp.int32, (slots, 1), 0)
    plane, row = slot & 3, slot >> 2
    source = slab * SLAB_ROWS - LOW + row - shift
    inside = (source >= 0) & (source < camera) & (row < NEED)
    wanted = jnp.where(inside, plane * camera + source, -1)
    lane = lax.broadcasted_iota(jnp.int32, (slots, 4 * camera), 1)
    return jnp.where(lane == wanted, 1.0, 0.0).astype(BF16)


def spread_shifts(values, slots):
    plane = lax.broadcasted_iota(jnp.int32, (slots, LANE), 0) & 3
    return jnp.where(plane < 2, jnp.where(plane == 0, values[0], values[1]), jnp.where(plane == 2, values[2], values[3]))


def strip_picks(widths, columns):
    tile = lax.axis_index("tile")
    tiles = lax.axis_size("tile")
    lane = lax.broadcasted_iota(jnp.int32, (8, columns), 1)
    line = lax.broadcasted_iota(jnp.int32, (8, columns), 0)
    right_width = widths[jnp.minimum(tile, tiles - 2)]
    left_width = widths[jnp.maximum(tile - 1, 0)]
    toward_right = jnp.where((lane == columns - right_width - 8 + line) & (line >= 2), 1.0, 0.0)
    toward_left = jnp.where((lane == left_width + line) & (line < 6), 1.0, 0.0)
    return jnp.concatenate([toward_right, toward_left], 0).astype(BF16)


def pack_own(raw_ref, shear_ref, width_ref, kept_ref, shift_ref, pick_ref, strip_ref, *refs):
    out_refs, (shears, widths, sems) = refs[:-3], refs[-3:]
    loads = [
        pltpu.make_async_copy(source, target, sems.at[index])
        for index, (source, target) in enumerate(((raw_ref, kept_ref), (shear_ref, shears), (width_ref, widths)))
    ]
    for load in loads:
        load.start()
    camera = raw_ref.shape[0] // 4
    columns = raw_ref.shape[1]
    slab = lax.axis_index("slab")
    for load in loads[1:]:
        load.wait()
    pick_ref[...] = strip_picks(widths, columns)
    shift_ref[...] = spread_shifts(shears, LANE)
    loads[0].wait()
    for step, out_ref in enumerate(out_refs):
        table = place_table(shift_ref[:SLOTS, :1], slab ^ (2 * step), camera)
        out_ref[...] = dot(table, kept_ref[:, : columns - LANE]).astype(BF16)
    strip_ref[...] = dot_rows(pick_ref[...], kept_ref[...])


def pack_other(other_ref, shear_ref, pick_ref, strip_ref, *refs):
    (shears, sem), refs = refs[-2:], refs[:-2]
    pairs = (len(refs) - 3) // 2
    own_refs, (right_ref, left_ref, shift_ref), out_refs = refs[:pairs], refs[pairs : pairs + 3], refs[pairs + 3 :]
    load = pltpu.make_async_copy(shear_ref, shears, sem)
    load.start()
    camera = other_ref.shape[0] // 4
    columns = other_ref.shape[1]
    slab = lax.axis_index("slab")
    for own_ref, out_ref in zip(own_refs, out_refs):
        out_ref[:SLOTS, :] = own_ref[...]
    strips = jnp.concatenate([strip_ref[...], dot_rows(pick_ref[...], other_ref[...])], 0)
    right_ref[...] = jnp.concatenate([strips[:8], strips[16:24]], 0).astype(BF16)
    left_ref[...] = jnp.concatenate([strips[8:16], strips[24:]], 0).astype(BF16)
    load.wait()
    shift_ref[...] = spread_shifts(shears, LANE)
    for step, out_ref in enumerate(out_refs):
        table = place_table(shift_ref[:SLOTS, :1], slab ^ (2 * step), camera)
        out_ref[SLOTS:, :] = dot(table, other_ref[:, : columns - LANE]).astype(BF16)


def stage(order_ref, *refs):
    sems, refs = refs[-1], refs[:-1]
    count = len(refs) // 2
    loads = [pltpu.make_async_copy(refs[index], refs[count + index], sems.at[index]) for index in range(count)]
    for load in loads:
        load.start()
    for load in loads:
        load.wait()


def pack_second(raw_ref, other_ref, shift_ref, other_shift_ref, from_left_ref, from_right_ref, order_ref, *out_refs):
    camera = raw_ref.shape[0] // 4
    columns = raw_ref.shape[1]
    slab = lax.axis_index("slab")
    tile = lax.axis_index("tile")
    right = jnp.where(tile < lax.axis_size("tile") - 1, from_right_ref[...].astype(F32), 0.0)
    left = jnp.where(tile > 0, from_left_ref[...].astype(F32), 0.0)
    for step, out_ref in enumerate(out_refs):
        for owner, (planes_ref, shifts_ref) in enumerate(((raw_ref, shift_ref), (other_ref, other_shift_ref))):
            table = place_table(shifts_ref[:, :1], slab ^ (2 * step), camera)
            placed = dot(table[:SLOTS], planes_ref[:, columns - LANE :])
            out_ref[owner * SLOTS : (owner + 1) * SLOTS, :] = placed.astype(BF16)
            own = slice(8 * owner, 8 * owner + 8)
            strips = jnp.concatenate([right[own], left[own]], 0).astype(BF16)
            start = 2 * SLOTS + 16 * owner
            out_ref[start : start + 16, :] = dot_rows(strips, table).astype(BF16)


def collect(in_refs, volume, scans):
    slab = lax.axis_index("slab")
    lanes = in_refs[0].shape[-1]
    groups = scans // 4
    outside = jnp.zeros((LANE,) + volume.shape[2:], BF16)
    volume[0] = outside
    volume[groups + 1] = outside
    for index in range(groups):
        group = (slab ^ index) + 1
        start = (index & 1) * SLOTS
        volume[group, :SLOTS, :lanes] = in_refs[index >> 1][start : start + SLOTS, :]
        volume[group, SLOTS:, :lanes] = jnp.zeros((LANE - SLOTS, lanes), BF16)


def split(value):
    high = value.astype(BF16)
    return high, (value - high.astype(F32)).astype(BF16)


def row_scan(rowscan_ref, volume, block, wide):
    rows = 8 * SLAB_ROWS
    both = dot(rowscan_ref[...], volume[2 * block : 2 * block + 4].reshape(4 * LANE, volume.shape[-1]))
    for sigma in range(2):
        total = both[2 * sigma * rows : (2 * sigma + 1) * rows] + both[(2 * sigma + 1) * rows : (2 * sigma + 2) * rows]
        high, low = split(total)
        wide[2 * sigma, block * rows : (block + 1) * rows, :] = high
        wide[2 * sigma + 1, block * rows : (block + 1) * rows, :] = low


def across(wide, rows, lanes, column_ref, taken):
    total = None
    for sigma in range(2):
        high, low = wide[2 * sigma, rows, lanes], wide[2 * sigma + 1, rows, lanes]
        part = dot(high, column_ref[2 * sigma, taken]) + dot(low, column_ref[2 * sigma, taken])
        part = part + dot(high, column_ref[2 * sigma + 1, taken])
        total = part if total is None else total + part
    return total


def level_part(level_ref, level_column_ref, volume, scans):
    groups = scans // 4
    high, low = split(dot(level_ref[...], volume[1 : groups + 1].reshape(groups * LANE, volume.shape[-1])))
    return dot(high, level_column_ref[...]) + dot(low, level_column_ref[...])


def first_half(count, scans, rowscan_ref, level_ref, column_ref, level_column_ref, *refs):
    in_refs, (partial_ref, coarse_ref, volume, wide) = refs[:count], refs[count:]
    collect(in_refs, volume, scans)
    for block in range(scans // 8):
        row_scan(rowscan_ref, volume, block, wide)
    cut = wide.shape[-1]
    for start in range(0, partial_ref.shape[1], 2 * LANE):
        low, high = max(start - LANE, 0), min(start + 3 * LANE, cut)
        taken = slice(low - start + LANE, high - start + LANE)
        partial_ref[:, start : start + 2 * LANE] = across(wide, slice(None), slice(low, high), column_ref, taken)
    coarse_ref[...] = level_part(level_ref, level_column_ref, volume, scans)


def second_half(count, scans, rowscan_ref, level_ref, column_ref, level_column_ref, two_ref, two_column_ref, *refs):
    partial_ref, coarse_ref, *in_refs = refs[: 2 + count]
    difference_ref, one_ref, second_ref, volume, strips, wide, held, held_one, held_second, sems = refs[2 + count :]
    slab = lax.axis_index("slab")
    slabs = lax.axis_size("slab")
    tile = lax.axis_index("tile")
    tiles = lax.axis_size("tile")
    groups = scans // 4
    columns = partial_ref.shape[1]
    cut = columns - LANE
    collect(in_refs, volume, scans)
    for index in range(groups):
        place = pl.multiple_of((slab ^ index) * LANE, LANE)
        start = 2 * SLOTS + 16 * (index & 1)
        strips[:, pl.ds(place, LANE)] = in_refs[index >> 1][start : start + 16, :]
    line = lax.broadcasted_iota(jnp.int32, (16, LANE), 0)
    lane = lax.broadcasted_iota(jnp.int32, (16, LANE), 1)
    spread = jnp.where(lane == jnp.where(line < 8, line, line + LANE - 16), 1.0, 0.0).astype(BF16)
    rim = lax.dot_general(strips[...], spread, (((0,), (0,)), ((), ())), preferred_element_type=F32)
    volume[1 : groups + 1, :, LANE:] = rim.astype(BF16).reshape(groups, LANE, LANE)

    copies = []
    rows = 8 * SLAB_ROWS
    left = lax.broadcasted_iota(jnp.int32, (2 * rows, LANE), 1) < LANE // 2
    for pair in range(scans // 16):
        for block in (2 * pair, 2 * pair + 1):
            row_scan(rowscan_ref, volume, block, wide)
        here = slice(2 * pair * rows, 2 * (pair + 1) * rows)
        late = across(wide, here, slice(None), column_ref, slice(None))
        ends = late[:, LANE:]
        for start in range(0, columns, LANE):
            total = partial_ref[here, start : start + LANE]
            if start == cut:
                total = total + late[:, :LANE]
            if start == 0:
                total = total + jnp.where(left, ends, 0.0)
            if start == cut - LANE:
                total = total + jnp.where(left, 0.0, ends)
            total = total.reshape(2, SLAB_ROWS, 8, LANE)
            joined = jnp.concatenate([total[0], total[1]], 1)
            held[:, 16 * pair : 16 * pair + 16, start : start + LANE] = joined.astype(BF16)
        copy = pltpu.make_async_copy(
            held.at[:, 16 * pair : 16 * pair + 16, :], difference_ref.at[:, 16 * pair : 16 * pair + 16, :], sems.at[pair]
        )
        copy.start()
        copies.append(copy)
    level = coarse_ref[...] + level_part(level_ref, level_column_ref, volume, scans)
    half = columns // 2
    shape = (LEVEL, scans // 2, level.shape[-1])
    level = level.reshape(shape)
    row = slab * (SLAB_ROWS // 2) - 2 + lax.broadcasted_iota(jnp.int32, shape, 0)
    place = lax.broadcasted_iota(jnp.int32, shape, 2) - half
    keep = (row >= 0) & (row < slabs * (SLAB_ROWS // 2))
    keep = keep & ((place < 0) | (place >= 2) | (tile > 0)) & ((place < 2) | (tile < tiles - 1))
    ready = jnp.where(keep, level, 0.0).astype(BF16)
    held_one[...] = ready[2:10, :, :half]
    copy = pltpu.make_async_copy(held_one, one_ref, sems.at[scans // 16])
    copy.start()
    copies.append(copy)

    high, low = split(dot(two_ref[...], ready.reshape(LEVEL * scans // 2, level.shape[-1])))
    second = dot(high, two_column_ref[...]) + dot(low, two_column_ref[...])
    held_second[...] = second.reshape(second_ref.shape).astype(BF16)
    copy = pltpu.make_async_copy(held_second, second_ref, sems.at[scans // 16 + 1])
    copy.start()
    copies.append(copy)

    for copy in copies:
        copy.wait()


VECTOR = pl.BlockSpec(memory_space=pltpu.VMEM)
ANYWHERE = pl.BlockSpec(memory_space=pl.ANY)
OUTSIDE = pl.BlockSpec(memory_space=pltpu.HBM)
PARAMS = pltpu.CompilerParams(vmem_limit_bytes=20 * 1024 * 1024)


def along(chunks, slabs):
    got = list(chunks)
    for step in sorted(range(1, len(chunks)), key=lambda step: (-(step & -step), step)):
        got[step] = lax.ppermute(chunks[step], "slab", [(i, i ^ (2 * step)) for i in range(slabs)])
    return got


def shifted(block, distance):
    count = lax.axis_size("tile")
    return lax.ppermute(block, "tile", [(i, (i + distance) % count) for i in range(count)])


def body(raw_stack, shear_offsets, intersection_widths):
    slabs = lax.axis_size("slab")
    planes, camera, columns = raw_stack.shape
    scans = planes * slabs
    cut = columns - LANE
    pairs = slabs // 2
    table = {name: jnp.asarray(value) for name, value in tables(scans, columns).items()}
    raw = raw_stack.reshape(planes * camera, columns)
    swap = [(i, i ^ 1) for i in range(slabs)]
    other = lax.ppermute(raw, "slab", swap)
    other_shear = lax.ppermute(shear_offsets, "slab", swap)
    outside = [pltpu.with_memory_space_constraint(each, pltpu.HBM) for each in (raw, shear_offsets, intersection_widths)]
    strip = jax.ShapeDtypeStruct((16, planes * camera), BF16)
    shift = jax.ShapeDtypeStruct((LANE, LANE), jnp.int32)
    raw, own_shift, pick, own_strip, *own = pl.pallas_call(
        pack_own,
        out_shape=[
            jax.ShapeDtypeStruct((planes * camera, columns), BF16),
            shift,
            jax.ShapeDtypeStruct((16, columns), BF16),
            jax.ShapeDtypeStruct((16, planes * camera), F32),
        ]
        + [jax.ShapeDtypeStruct((SLOTS, cut), BF16)] * pairs,
        in_specs=[OUTSIDE] * 3,
        out_specs=[VECTOR] * (4 + pairs),
        scratch_shapes=[
            pltpu.SMEM(shear_offsets.shape, jnp.int32),
            pltpu.SMEM(intersection_widths.shape, jnp.int32),
            pltpu.SemaphoreType.DMA((3,)),
        ],
        compiler_params=PARAMS,
        name="pack_own",
    )(*outside)
    toward_right, toward_left, other_shift, *chunks = pl.pallas_call(
        pack_other,
        out_shape=[strip, strip, shift] + [jax.ShapeDtypeStruct((2 * SLOTS, cut), BF16)] * pairs,
        in_specs=[VECTOR, ANYWHERE] + [VECTOR] * (2 + pairs),
        out_specs=[VECTOR] * (3 + pairs),
        scratch_shapes=[pltpu.SMEM(shear_offsets.shape, jnp.int32), pltpu.SemaphoreType.DMA],
        compiler_params=PARAMS,
        name="pack_other",
    )(other, other_shear, pick, own_strip, *own)
    got_first = along(chunks, slabs)
    from_left = shifted(toward_right, 1)
    from_right = shifted(toward_left, -1)
    second = jax.ShapeDtypeStruct((2 * SLOTS + 32, LANE), BF16)
    names = list(table)
    staged = pl.pallas_call(
        stage,
        out_shape=[jax.ShapeDtypeStruct(table[name].shape, BF16) for name in names],
        in_specs=[ANYWHERE] + [OUTSIDE] * len(names),
        out_specs=[VECTOR] * len(names),
        scratch_shapes=[pltpu.SemaphoreType.DMA((len(names),))],
        compiler_params=PARAMS,
        name="stage",
    )(toward_left, *[pltpu.with_memory_space_constraint(table[name], pltpu.HBM) for name in names])
    table = dict(zip(names, staged))
    chunks = pl.pallas_call(
        pack_second,
        out_shape=[second] * pairs,
        in_specs=[VECTOR] * 6 + [ANYWHERE],
        out_specs=[VECTOR] * pairs,
        compiler_params=PARAMS,
        name="pack_second",
    )(raw, other, own_shift, other_shift, from_left, from_right, table["two"])
    chunks, got_first[2] = lax.optimization_barrier((chunks, got_first[2]))
    got_second = along(chunks, slabs)
    partial, coarse = pl.pallas_call(
        functools.partial(first_half, pairs, scans),
        out_shape=[
            jax.ShapeDtypeStruct((scans * SLAB_ROWS, columns), F32),
            jax.ShapeDtypeStruct((LEVEL * scans // 2, columns // 2 + LANE), F32),
        ],
        in_specs=[VECTOR] * (4 + pairs),
        out_specs=[VECTOR] * 2,
        scratch_shapes=[
            pltpu.VMEM((slabs + 2, LANE, cut), BF16),
            pltpu.VMEM((4, scans * SLAB_ROWS, cut), BF16),
        ],
        compiler_params=PARAMS,
        name="first_half",
    )(table["rowscan"], table["level"], table["column_first"], table["level_first"], *got_first)
    got_second, partial = lax.optimization_barrier((got_second, partial))
    return pl.pallas_call(
        functools.partial(second_half, pairs, scans),
        out_shape=[
            jax.ShapeDtypeStruct((SLAB_ROWS, scans, columns), BF16),
            jax.ShapeDtypeStruct((SLAB_ROWS // 2, scans // 2, columns // 2), BF16),
            jax.ShapeDtypeStruct((SLAB_ROWS // 4, scans // 4, columns // 4), BF16),
        ],
        in_specs=[VECTOR] * (8 + pairs),
        out_specs=[OUTSIDE] * 3,
        scratch_shapes=[
            pltpu.VMEM((slabs + 2, LANE, 2 * LANE), BF16),
            pltpu.VMEM((16, slabs * LANE), BF16),
            pltpu.VMEM((4, scans * SLAB_ROWS, 2 * LANE), BF16),
            pltpu.VMEM((SLAB_ROWS, scans, columns), BF16),
            pltpu.VMEM((SLAB_ROWS // 2, scans // 2, columns // 2), BF16),
            pltpu.VMEM((SLAB_ROWS // 4, scans // 4, columns // 4), BF16),
            pltpu.SemaphoreType.DMA((scans // 16 + 2,)),
        ],
        compiler_params=PARAMS,
        name="second_half",
    )(
        table["rowscan"],
        table["level"],
        table["column_last"],
        table["level_last"],
        table["two"],
        table["two_column"],
        partial,
        coarse,
        *got_second,
    )


def solution(mesh):
    placed = (P("slab", None, "tile"), P("slab"), P())
    return jax.shard_map(
        body,
        mesh=mesh,
        in_specs=placed,
        out_specs=(P("slab", None, "tile"), P("slab", None, "tile"), P("slab", None, "tile")),
        check_vma=False,
    )
```

```python
import functools
import math

import jax
import jax.numpy as jnp
import ml_dtypes
import numpy as np
from jax import lax
from jax.experimental import pallas as pl
from jax.experimental.pallas import tpu as pltpu
from jax.sharding import PartitionSpec as P

SLAB_ROWS = 16
STRIP = 6
RADIUS = 4
NEED = SLAB_ROWS + 2 * RADIUS
PLACED = 4 * NEED
SLOTS = PLACED + 8
LEVEL = 11
LANE = 128
F32 = jnp.float32
BF16 = jnp.bfloat16


def gauss_taps(sigma_value):
    entries = [math.exp(-(j * j) / (2.0 * sigma_value * sigma_value)) for j in range(-RADIUS, RADIUS + 1)]
    weight_sum = sum(entries)
    return np.array([entry / weight_sum for entry in entries], np.float64)


BINOMIAL = np.array([1.0, 4.0, 6.0, 4.0, 1.0], np.float64) / 16.0


def band(weights, source, target):
    reach = len(weights) // 2
    offset = source[None, :] - target[:, None] + reach
    inside = (offset >= 0) & (offset < len(weights))
    return np.where(inside, weights[np.clip(offset, 0, len(weights) - 1)], 0.0)


def two_parts(table):
    high = table.astype(ml_dtypes.bfloat16)
    return [high, (table - high.astype(np.float64)).astype(ml_dtypes.bfloat16)]


def row_scan_table(row_band, scan_band, groups, early=None):
    rows_out, rows_in = row_band.shape
    scans_out = scan_band.shape[0]
    scans = scan_band.reshape(scans_out, groups, 4)
    table = np.zeros((rows_out, scans_out, groups, LANE))
    table[..., :PLACED] = np.einsum("yr,sgp->ysgrp", row_band, scans).reshape(rows_out, scans_out, groups, PLACED)
    if early is not None:
        for group in range(groups):
            start = PLACED + 4 * (group & 1)
            table[:, :, group, start : start + 4] = early[:, None, None] * scans[:, group]
    return table.reshape(rows_out * scans_out, groups * LANE)


def tables(scans, columns):
    row_in = np.arange(NEED) - RADIUS
    own = np.arange(SLAB_ROWS)
    near = np.arange(16) - 4
    block = np.arange(8)
    cut = columns - LANE
    rim = np.where(np.arange(LANE) < LANE // 2, columns, -LANE) + np.arange(LANE)
    last = np.concatenate([np.arange(cut, columns), rim])
    touched = np.concatenate([np.arange(cut, columns), np.arange(LANE // 2), np.arange(cut - LANE // 2, cut)])
    rowscan, column_first, column_last = [], [], []
    for sigma, sign in ((1.0, 1.0), (1.6, -1.0)):
        taps = gauss_taps(sigma)
        rowscan += two_parts(row_scan_table(band(taps, row_in, own), band(taps, near, block), 4))
        column_first += two_parts(sign * band(taps, np.arange(4 * LANE) - LANE, np.arange(2 * LANE)).T)
        column_last += two_parts(sign * band(taps, last, touched).T)
    level_rows = 2 * np.arange(LEVEL) - 4
    level_scans = 2 * np.arange(scans // 2)
    early = np.arange(LEVEL) == 0
    level = row_scan_table(
        band(BINOMIAL, row_in, level_rows) * ~early[:, None],
        band(BINOMIAL, np.arange(scans), level_scans),
        scans // 4,
        early * 1.0,
    )
    edges = np.array([-4, -2, columns, columns + 2])
    targets = np.concatenate([2 * np.arange(columns // 2), edges])
    two = np.einsum(
        "yr,sp->ysrp",
        band(BINOMIAL, np.arange(LEVEL) - 2, 2 * np.arange(4)),
        band(BINOMIAL, np.arange(scans // 2), 2 * np.arange(scans // 4)),
    ).reshape(scans, LEVEL * scans // 2)
    fill = ((0, 0), (0, LANE - 4))
    small = ml_dtypes.bfloat16
    return dict(
        rowscan=np.concatenate(rowscan, 0),
        level=level.astype(small),
        column_first=np.stack(column_first),
        column_last=np.stack(column_last),
        level_first=np.pad(band(BINOMIAL, np.arange(cut), targets).T, fill).astype(small),
        level_last=np.pad(band(BINOMIAL, last, targets).T, fill).astype(small),
        two=two.astype(small),
        two_column=np.pad(band(BINOMIAL, targets // 2, 2 * np.arange(columns // 4)), fill).T.astype(small),
    )


def dot(left, right):
    return jnp.dot(left, right, preferred_element_type=F32)


def dot_rows(left, right):
    return lax.dot_general(left, right, (((1,), (1,)), ((), ())), preferred_element_type=F32)


def place_table(shift, slab, camera, owner):
    lanes = 4 * camera
    slot = lax.broadcasted_iota(jnp.int32, (PLACED, 1), 0)
    plane = slot & 3
    source = slab * SLAB_ROWS - RADIUS + (slot >> 2) - shift[:PLACED]
    wanted = jnp.where((source >= 0) & (source < camera), plane * camera + source, -1)
    lane = lax.broadcasted_iota(jnp.int32, (PLACED, lanes), 1)
    rows = jnp.where(lane == wanted, 1.0, 0.0).astype(BF16)
    slot = lax.broadcasted_iota(jnp.int32, (8, 1), 0)
    source = lax.broadcasted_iota(jnp.int32, (8, lanes), 1) - (slot & 3) * camera
    tap = source + shift[:8] - (slab * SLAB_ROWS - 6)
    inside = (source >= 0) & (source < camera) & ((slot >> 2) == owner) & (tap >= 0) & (tap < 5)
    weight = jnp.where(tap == 2, 6.0 / 16.0, jnp.where((tap == 1) | (tap == 3), 4.0 / 16.0, 1.0 / 16.0))
    return rows, jnp.where(inside, weight, 0.0).astype(BF16)


def place_tables(stack, pairs, shift, slab, camera, owner):
    for step in range(pairs):
        rows, early = place_table(shift, slab ^ (2 * step), camera, owner)
        stack[step * LANE : step * LANE + PLACED, :] = rows
        stack[step * LANE + PLACED : step * LANE + SLOTS, :] = early
        stack[step * LANE + SLOTS : (step + 1) * LANE, :] = jnp.zeros((LANE - SLOTS, 4 * camera), BF16)


def spread_shifts(values, slots):
    plane = lax.broadcasted_iota(jnp.int32, (slots, LANE), 0) & 3
    return jnp.where(plane < 2, jnp.where(plane == 0, values[0], values[1]), jnp.where(plane == 2, values[2], values[3]))


def strip_picks(widths, columns):
    tile = lax.axis_index("tile")
    tiles = lax.axis_size("tile")
    lane = lax.broadcasted_iota(jnp.int32, (8, columns), 1)
    line = lax.broadcasted_iota(jnp.int32, (8, columns), 0)
    right_width = widths[jnp.minimum(tile, tiles - 2)]
    left_width = widths[jnp.maximum(tile - 1, 0)]
    toward_right = jnp.where((lane == columns - right_width - 8 + line) & (line >= 2), 1.0, 0.0)
    toward_left = jnp.where((lane == left_width + line) & (line < 6), 1.0, 0.0)
    return jnp.concatenate([toward_right, toward_left], 0).astype(BF16)


def pack_own(raw_ref, shear_ref, width_ref, kept_ref, shift_ref, pick_ref, strip_ref, early_ref, *refs):
    out_refs, (shears, widths, sems, stack) = refs[:-4], refs[-4:]
    loads = [
        pltpu.make_async_copy(source, target, sems.at[index])
        for index, (source, target) in enumerate(((raw_ref, kept_ref), (shear_ref, shears), (width_ref, widths)))
    ]
    for load in loads:
        load.start()
    camera = raw_ref.shape[0] // 4
    columns = raw_ref.shape[1]
    slab = lax.axis_index("slab")
    for load in loads[1:]:
        load.wait()
    pick_ref[...] = strip_picks(widths, columns)
    shift_ref[...] = spread_shifts(shears, LANE)
    place_tables(stack, len(out_refs), shift_ref[:, :1], slab, camera, slab & 1)
    loads[0].wait()
    placed = dot(stack[...], kept_ref[:, : columns - LANE])
    for step, out_ref in enumerate(out_refs):
        out_ref[...] = placed[step * LANE : step * LANE + PLACED].astype(BF16)
        early_ref[step] = placed[step * LANE + PLACED : step * LANE + SLOTS]
    strip_ref[...] = dot_rows(pick_ref[...], kept_ref[...])


def pack_other(other_ref, shear_ref, pick_ref, strip_ref, early_ref, *refs):
    (shears, sem, stack), refs = refs[-3:], refs[:-3]
    pairs = (len(refs) - 3) // 2
    own_refs, (right_ref, left_ref, shift_ref), out_refs = refs[:pairs], refs[pairs : pairs + 3], refs[pairs + 3 :]
    load = pltpu.make_async_copy(shear_ref, shears, sem)
    load.start()
    camera = other_ref.shape[0] // 4
    columns = other_ref.shape[1]
    slab = lax.axis_index("slab")
    for own_ref, out_ref in zip(own_refs, out_refs):
        out_ref[:PLACED, :] = own_ref[...]
    strips = jnp.concatenate([strip_ref[...], dot_rows(pick_ref[...], other_ref[...])], 0)
    right_ref[...] = jnp.concatenate([strips[:8], strips[16:24]], 0).astype(BF16)
    left_ref[...] = jnp.concatenate([strips[8:16], strips[24:]], 0).astype(BF16)
    load.wait()
    shift_ref[...] = spread_shifts(shears, LANE)
    place_tables(stack, pairs, shift_ref[:, :1], slab, camera, ~slab & 1)
    placed = dot(stack[...], other_ref[:, : columns - LANE])
    for step, out_ref in enumerate(out_refs):
        out_ref[PLACED : 2 * PLACED, :] = placed[step * LANE : step * LANE + PLACED].astype(BF16)
        out_ref[2 * PLACED :, :] = (early_ref[step] + placed[step * LANE + PLACED : step * LANE + SLOTS]).astype(BF16)


def stage(order_ref, *refs):
    sems, refs = refs[-1], refs[:-1]
    count = len(refs) // 2
    loads = [pltpu.make_async_copy(refs[index], refs[count + index], sems.at[index]) for index in range(count)]
    for load in loads:
        load.start()
    for load in loads:
        load.wait()


def pack_second(raw_ref, other_ref, shift_ref, other_shift_ref, from_left_ref, from_right_ref, order_ref, *out_refs):
    camera = raw_ref.shape[0] // 4
    columns = raw_ref.shape[1]
    slab = lax.axis_index("slab")
    tile = lax.axis_index("tile")
    right = jnp.where(tile < lax.axis_size("tile") - 1, from_right_ref[...].astype(F32), 0.0)
    left = jnp.where(tile > 0, from_left_ref[...].astype(F32), 0.0)
    for step, out_ref in enumerate(out_refs):
        total = 0.0
        for owner, (planes_ref, shifts_ref) in enumerate(((raw_ref, shift_ref), (other_ref, other_shift_ref))):
            rows, early = place_table(shifts_ref[:, :1], slab ^ (2 * step), camera, (slab & 1) ^ owner)
            planes = planes_ref[:, columns - LANE :]
            out_ref[owner * PLACED : (owner + 1) * PLACED, :] = dot(rows, planes).astype(BF16)
            total = total + dot(early, planes)
            own = slice(8 * owner, 8 * owner + 8)
            strips = jnp.concatenate([right[own], left[own]], 0).astype(BF16)
            start = 2 * PLACED + 8 + 16 * owner
            table = jnp.concatenate(
                [rows.astype(F32), early.astype(F32), jnp.zeros((LANE - SLOTS, rows.shape[1]), F32)], 0
            )
            out_ref[start : start + 16, :] = dot_rows(strips, table.astype(BF16)).astype(BF16)
        out_ref[2 * PLACED : 2 * PLACED + 8, :] = total.astype(BF16)


def collect(in_refs, volume, scans):
    slab = lax.axis_index("slab")
    lanes = in_refs[0].shape[-1]
    groups = scans // 4
    outside = jnp.zeros((LANE,) + volume.shape[2:], BF16)
    volume[0] = outside
    volume[groups + 1] = outside
    for index in range(groups):
        group = (slab ^ index) + 1
        start = (index & 1) * PLACED
        volume[group, :PLACED, :lanes] = in_refs[index >> 1][start : start + PLACED, :]
        volume[group, PLACED:SLOTS, :lanes] = in_refs[index >> 1][2 * PLACED : 2 * PLACED + 8, :]
        volume[group, SLOTS:, :lanes] = jnp.zeros((LANE - SLOTS, lanes), BF16)


def split(value):
    high = value.astype(BF16)
    return high, (value - high.astype(F32)).astype(BF16)


def row_scan(rowscan_ref, volume, block, wide):
    rows = 8 * SLAB_ROWS
    both = dot(rowscan_ref[...], volume[2 * block : 2 * block + 4].reshape(4 * LANE, volume.shape[-1]))
    for sigma in range(2):
        total = both[2 * sigma * rows : (2 * sigma + 1) * rows] + both[(2 * sigma + 1) * rows : (2 * sigma + 2) * rows]
        high, low = split(total)
        wide[2 * sigma, block * rows : (block + 1) * rows, :] = high
        wide[2 * sigma + 1, block * rows : (block + 1) * rows, :] = low


def across(wide, rows, lanes, column_ref, taken):
    total = None
    for sigma in range(2):
        high, low = wide[2 * sigma, rows, lanes], wide[2 * sigma + 1, rows, lanes]
        part = dot(high, column_ref[2 * sigma, taken]) + dot(low, column_ref[2 * sigma, taken])
        part = part + dot(high, column_ref[2 * sigma + 1, taken])
        total = part if total is None else total + part
    return total


def level_part(level_ref, level_column_ref, volume, scans):
    groups = scans // 4
    high, low = split(dot(level_ref[...], volume[1 : groups + 1].reshape(groups * LANE, volume.shape[-1])))
    return dot(high, level_column_ref[...]) + dot(low, level_column_ref[...])


def first_half(count, scans, rowscan_ref, level_ref, column_ref, level_column_ref, *refs):
    in_refs, (partial_ref, coarse_ref, volume, wide) = refs[:count], refs[count:]
    collect(in_refs, volume, scans)
    for block in range(scans // 8):
        row_scan(rowscan_ref, volume, block, wide)
    cut = wide.shape[-1]
    for start in range(0, partial_ref.shape[1], 2 * LANE):
        low, high = max(start - LANE, 0), min(start + 3 * LANE, cut)
        taken = slice(low - start + LANE, high - start + LANE)
        partial_ref[:, start : start + 2 * LANE] = across(wide, slice(None), slice(low, high), column_ref, taken)
    coarse_ref[...] = level_part(level_ref, level_column_ref, volume, scans)


def second_half(count, scans, rowscan_ref, level_ref, column_ref, level_column_ref, two_ref, two_column_ref, *refs):
    partial_ref, coarse_ref, *in_refs = refs[: 2 + count]
    difference_ref, one_ref, second_ref, volume, strips, wide, held, held_one, held_second, sems = refs[2 + count :]
    slab = lax.axis_index("slab")
    slabs = lax.axis_size("slab")
    tile = lax.axis_index("tile")
    tiles = lax.axis_size("tile")
    groups = scans // 4
    columns = partial_ref.shape[1]
    cut = columns - LANE
    collect(in_refs, volume, scans)
    for index in range(groups):
        place = pl.multiple_of((slab ^ index) * LANE, LANE)
        start = 2 * PLACED + 8 + 16 * (index & 1)
        strips[:, pl.ds(place, LANE)] = in_refs[index >> 1][start : start + 16, :]
    line = lax.broadcasted_iota(jnp.int32, (16, LANE), 0)
    lane = lax.broadcasted_iota(jnp.int32, (16, LANE), 1)
    spread = jnp.where(lane == jnp.where(line < 8, line, line + LANE - 16), 1.0, 0.0).astype(BF16)
    rim = lax.dot_general(strips[...], spread, (((0,), (0,)), ((), ())), preferred_element_type=F32)
    volume[1 : groups + 1, :, LANE:] = rim.astype(BF16).reshape(groups, LANE, LANE)

    copies = []
    rows = 8 * SLAB_ROWS
    left = lax.broadcasted_iota(jnp.int32, (2 * rows, LANE), 1) < LANE // 2
    for pair in range(scans // 16):
        for block in (2 * pair, 2 * pair + 1):
            row_scan(rowscan_ref, volume, block, wide)
        here = slice(2 * pair * rows, 2 * (pair + 1) * rows)
        late = across(wide, here, slice(None), column_ref, slice(None))
        ends = late[:, LANE:]
        for start in range(0, columns, LANE):
            total = partial_ref[here, start : start + LANE]
            if start == cut:
                total = total + late[:, :LANE]
            if start == 0:
                total = total + jnp.where(left, ends, 0.0)
            if start == cut - LANE:
                total = total + jnp.where(left, 0.0, ends)
            total = total.reshape(2, SLAB_ROWS, 8, LANE)
            joined = jnp.concatenate([total[0], total[1]], 1)
            held[:, 16 * pair : 16 * pair + 16, start : start + LANE] = joined.astype(BF16)
        copy = pltpu.make_async_copy(
            held.at[:, 16 * pair : 16 * pair + 16, :], difference_ref.at[:, 16 * pair : 16 * pair + 16, :], sems.at[pair]
        )
        copy.start()
        copies.append(copy)
    level = coarse_ref[...] + level_part(level_ref, level_column_ref, volume, scans)
    half = columns // 2
    shape = (LEVEL, scans // 2, level.shape[-1])
    level = level.reshape(shape)
    row = slab * (SLAB_ROWS // 2) - 2 + lax.broadcasted_iota(jnp.int32, shape, 0)
    place = lax.broadcasted_iota(jnp.int32, shape, 2) - half
    keep = (row >= 0) & (row < slabs * (SLAB_ROWS // 2))
    keep = keep & ((place < 0) | (place >= 2) | (tile > 0)) & ((place < 2) | (tile < tiles - 1))
    ready = jnp.where(keep, level, 0.0).astype(BF16)
    held_one[...] = ready[2:10, :, :half]
    copy = pltpu.make_async_copy(held_one, one_ref, sems.at[scans // 16])
    copy.start()
    copies.append(copy)

    high, low = split(dot(two_ref[...], ready.reshape(LEVEL * scans // 2, level.shape[-1])))
    second = dot(high, two_column_ref[...]) + dot(low, two_column_ref[...])
    held_second[...] = second.reshape(second_ref.shape).astype(BF16)
    copy = pltpu.make_async_copy(held_second, second_ref, sems.at[scans // 16 + 1])
    copy.start()
    copies.append(copy)

    for copy in copies:
        copy.wait()


VECTOR = pl.BlockSpec(memory_space=pltpu.VMEM)
ANYWHERE = pl.BlockSpec(memory_space=pl.ANY)
OUTSIDE = pl.BlockSpec(memory_space=pltpu.HBM)
PARAMS = pltpu.CompilerParams(vmem_limit_bytes=20 * 1024 * 1024)


def along(chunks, slabs):
    got = list(chunks)
    for step in sorted(range(1, len(chunks)), key=lambda step: (-(step & -step), step)):
        got[step] = lax.ppermute(chunks[step], "slab", [(i, i ^ (2 * step)) for i in range(slabs)])
    return got


def shifted(block, distance):
    count = lax.axis_size("tile")
    return lax.ppermute(block, "tile", [(i, (i + distance) % count) for i in range(count)])


def body(raw_stack, shear_offsets, intersection_widths):
    slabs = lax.axis_size("slab")
    planes, camera, columns = raw_stack.shape
    scans = planes * slabs
    cut = columns - LANE
    pairs = slabs // 2
    table = {name: jnp.asarray(value) for name, value in tables(scans, columns).items()}
    raw = raw_stack.reshape(planes * camera, columns)
    swap = [(i, i ^ 1) for i in range(slabs)]
    other = lax.ppermute(raw, "slab", swap)
    other_shear = lax.ppermute(shear_offsets, "slab", swap)
    outside = [pltpu.with_memory_space_constraint(each, pltpu.HBM) for each in (raw, shear_offsets, intersection_widths)]
    strip = jax.ShapeDtypeStruct((16, planes * camera), BF16)
    shift = jax.ShapeDtypeStruct((LANE, LANE), jnp.int32)
    raw, own_shift, pick, own_strip, early, *own = pl.pallas_call(
        pack_own,
        out_shape=[
            jax.ShapeDtypeStruct((planes * camera, columns), BF16),
            shift,
            jax.ShapeDtypeStruct((16, columns), BF16),
            jax.ShapeDtypeStruct((16, planes * camera), F32),
            jax.ShapeDtypeStruct((pairs, 8, cut), F32),
        ]
        + [jax.ShapeDtypeStruct((PLACED, cut), BF16)] * pairs,
        in_specs=[OUTSIDE] * 3,
        out_specs=[VECTOR] * (5 + pairs),
        scratch_shapes=[
            pltpu.SMEM(shear_offsets.shape, jnp.int32),
            pltpu.SMEM(intersection_widths.shape, jnp.int32),
            pltpu.SemaphoreType.DMA((3,)),
            pltpu.VMEM((pairs * LANE, planes * camera), BF16),
        ],
        compiler_params=PARAMS,
        name="pack_own",
    )(*outside)
    toward_right, toward_left, other_shift, *chunks = pl.pallas_call(
        pack_other,
        out_shape=[strip, strip, shift] + [jax.ShapeDtypeStruct((2 * PLACED + 8, cut), BF16)] * pairs,
        in_specs=[VECTOR, ANYWHERE] + [VECTOR] * (3 + pairs),
        out_specs=[VECTOR] * (3 + pairs),
        scratch_shapes=[
            pltpu.SMEM(shear_offsets.shape, jnp.int32),
            pltpu.SemaphoreType.DMA,
            pltpu.VMEM((pairs * LANE, planes * camera), BF16),
        ],
        compiler_params=PARAMS,
        name="pack_other",
    )(other, other_shear, pick, own_strip, early, *own)
    got_first = along(chunks, slabs)
    from_left = shifted(toward_right, 1)
    from_right = shifted(toward_left, -1)
    second = jax.ShapeDtypeStruct((2 * PLACED + 40, LANE), BF16)
    names = list(table)
    staged = pl.pallas_call(
        stage,
        out_shape=[jax.ShapeDtypeStruct(table[name].shape, BF16) for name in names],
        in_specs=[ANYWHERE] + [OUTSIDE] * len(names),
        out_specs=[VECTOR] * len(names),
        scratch_shapes=[pltpu.SemaphoreType.DMA((len(names),))],
        compiler_params=PARAMS,
        name="stage",
    )(toward_left, *[pltpu.with_memory_space_constraint(table[name], pltpu.HBM) for name in names])
    table = dict(zip(names, staged))
    chunks = pl.pallas_call(
        pack_second,
        out_shape=[second] * pairs,
        in_specs=[VECTOR] * 6 + [ANYWHERE],
        out_specs=[VECTOR] * pairs,
        compiler_params=PARAMS,
        name="pack_second",
    )(raw, other, own_shift, other_shift, from_left, from_right, table["two"])
    chunks, got_first[2] = lax.optimization_barrier((chunks, got_first[2]))
    got_second = along(chunks, slabs)
    partial, coarse = pl.pallas_call(
        functools.partial(first_half, pairs, scans),
        out_shape=[
            jax.ShapeDtypeStruct((scans * SLAB_ROWS, columns), F32),
            jax.ShapeDtypeStruct((LEVEL * scans // 2, columns // 2 + LANE), F32),
        ],
        in_specs=[VECTOR] * (4 + pairs),
        out_specs=[VECTOR] * 2,
        scratch_shapes=[
            pltpu.VMEM((slabs + 2, LANE, cut), BF16),
            pltpu.VMEM((4, scans * SLAB_ROWS, cut), BF16),
        ],
        compiler_params=PARAMS,
        name="first_half",
    )(table["rowscan"], table["level"], table["column_first"], table["level_first"], *got_first)
    got_second, partial = lax.optimization_barrier((got_second, partial))
    return pl.pallas_call(
        functools.partial(second_half, pairs, scans),
        out_shape=[
            jax.ShapeDtypeStruct((SLAB_ROWS, scans, columns), BF16),
            jax.ShapeDtypeStruct((SLAB_ROWS // 2, scans // 2, columns // 2), BF16),
            jax.ShapeDtypeStruct((SLAB_ROWS // 4, scans // 4, columns // 4), BF16),
        ],
        in_specs=[VECTOR] * (8 + pairs),
        out_specs=[OUTSIDE] * 3,
        scratch_shapes=[
            pltpu.VMEM((slabs + 2, LANE, 2 * LANE), BF16),
            pltpu.VMEM((16, slabs * LANE), BF16),
            pltpu.VMEM((4, scans * SLAB_ROWS, 2 * LANE), BF16),
            pltpu.VMEM((SLAB_ROWS, scans, columns), BF16),
            pltpu.VMEM((SLAB_ROWS // 2, scans // 2, columns // 2), BF16),
            pltpu.VMEM((SLAB_ROWS // 4, scans // 4, columns // 4), BF16),
            pltpu.SemaphoreType.DMA((scans // 16 + 2,)),
        ],
        compiler_params=PARAMS,
        name="second_half",
    )(
        table["rowscan"],
        table["level"],
        table["column_last"],
        table["level_last"],
        table["two"],
        table["two_column"],
        partial,
        coarse,
        *got_second,
    )


def solution(mesh):
    placed = (P("slab", None, "tile"), P("slab"), P())
    return jax.shard_map(
        body,
        mesh=mesh,
        in_specs=placed,
        out_specs=(P("slab", None, "tile"), P("slab", None, "tile"), P("slab", None, "tile")),
        check_vma=False,
    )
```

```python
import functools
import math

import jax
import jax.numpy as jnp
import ml_dtypes
import numpy as np
from jax import lax
from jax.experimental import pallas as pl
from jax.experimental.pallas import tpu as pltpu
from jax.sharding import PartitionSpec as P

SLAB_ROWS = 16
STRIP = 6
RADIUS = 4
NEED = SLAB_ROWS + 2 * RADIUS
PLACED = 4 * NEED
SLOTS = PLACED + 8
LEVEL = 11
LANE = 128
F32 = jnp.float32
BF16 = jnp.bfloat16


def gauss_taps(sigma_value):
    entries = [math.exp(-(j * j) / (2.0 * sigma_value * sigma_value)) for j in range(-RADIUS, RADIUS + 1)]
    weight_sum = sum(entries)
    return np.array([entry / weight_sum for entry in entries], np.float64)


BINOMIAL = np.array([1.0, 4.0, 6.0, 4.0, 1.0], np.float64) / 16.0


def band(weights, source, target):
    reach = len(weights) // 2
    offset = source[None, :] - target[:, None] + reach
    inside = (offset >= 0) & (offset < len(weights))
    return np.where(inside, weights[np.clip(offset, 0, len(weights) - 1)], 0.0)


def two_parts(table):
    high = table.astype(ml_dtypes.bfloat16)
    return [high, (table - high.astype(np.float64)).astype(ml_dtypes.bfloat16)]


def row_scan_table(row_band, scan_band, groups, early=None):
    rows_out, rows_in = row_band.shape
    scans_out = scan_band.shape[0]
    scans = scan_band.reshape(scans_out, groups, 4)
    table = np.zeros((rows_out, scans_out, groups, LANE))
    table[..., :PLACED] = np.einsum("yr,sgp->ysgrp", row_band, scans).reshape(rows_out, scans_out, groups, PLACED)
    if early is not None:
        for group in range(groups):
            start = PLACED + 4 * (group & 1)
            table[:, :, group, start : start + 4] = early[:, None, None] * scans[:, group]
    return table.reshape(rows_out * scans_out, groups * LANE)


def tables(scans, columns):
    row_in = np.arange(NEED) - RADIUS
    own = np.arange(SLAB_ROWS)
    near = np.arange(16) - 4
    block = np.arange(8)
    cut = columns - LANE
    rim = np.where(np.arange(LANE) < LANE // 2, columns, -LANE) + np.arange(LANE)
    last = np.concatenate([np.arange(cut, columns), rim])
    touched = np.concatenate([np.arange(cut, columns), np.arange(LANE // 2), np.arange(cut - LANE // 2, cut)])
    rowscan, column_first, column_last = [], [], []
    for sigma, sign in ((1.0, 1.0), (1.6, -1.0)):
        taps = gauss_taps(sigma)
        rowscan += two_parts(row_scan_table(band(taps, row_in, own), band(taps, near, block), 4))
        column_first += two_parts(sign * band(taps, np.arange(4 * LANE) - LANE, np.arange(2 * LANE)).T)
        column_last += two_parts(sign * band(taps, last, touched).T)
    level_rows = 2 * np.arange(LEVEL) - 4
    level_scans = 2 * np.arange(scans // 2)
    early = np.arange(LEVEL) == 0
    level = row_scan_table(
        band(BINOMIAL, row_in, level_rows) * ~early[:, None],
        band(BINOMIAL, np.arange(scans), level_scans),
        scans // 4,
        early * 1.0,
    )
    edges = np.array([-4, -2, columns, columns + 2])
    targets = np.concatenate([2 * np.arange(columns // 2), edges])
    two = np.einsum(
        "yr,sp->ysrp",
        band(BINOMIAL, np.arange(LEVEL) - 2, 2 * np.arange(4)),
        band(BINOMIAL, np.arange(scans // 2), 2 * np.arange(scans // 4)),
    ).reshape(scans, LEVEL * scans // 2)
    fill = ((0, 0), (0, LANE - 4))
    small = ml_dtypes.bfloat16
    return dict(
        rowscan=np.concatenate(rowscan, 0),
        level=level.astype(small),
        column_first=np.stack(column_first),
        column_last=np.stack(column_last),
        level_first=np.pad(band(BINOMIAL, np.arange(cut), targets).T, fill).astype(small),
        level_last=np.pad(band(BINOMIAL, last, targets).T, fill).astype(small),
        two=two.astype(small),
        two_column=np.pad(band(BINOMIAL, targets // 2, 2 * np.arange(columns // 4)), fill).T.astype(small),
    )


def dot(left, right):
    return jnp.dot(left, right, preferred_element_type=F32)


def dot_rows(left, right):
    return lax.dot_general(left, right, (((1,), (1,)), ((), ())), preferred_element_type=F32)


def place_table(shift, slab, camera, owner):
    lanes = 4 * camera
    slot = lax.broadcasted_iota(jnp.int32, (PLACED, 1), 0)
    plane = slot & 3
    source = slab * SLAB_ROWS - RADIUS + (slot >> 2) - shift[:PLACED]
    wanted = jnp.where((source >= 0) & (source < camera), plane * camera + source, -1)
    lane = lax.broadcasted_iota(jnp.int32, (PLACED, lanes), 1)
    rows = jnp.where(lane == wanted, 1.0, 0.0).astype(BF16)
    slot = lax.broadcasted_iota(jnp.int32, (8, 1), 0)
    source = lax.broadcasted_iota(jnp.int32, (8, lanes), 1) - (slot & 3) * camera
    tap = source + shift[:8] - (slab * SLAB_ROWS - 6)
    inside = (source >= 0) & (source < camera) & ((slot >> 2) == owner) & (tap >= 0) & (tap < 5)
    weight = jnp.where(tap == 2, 6.0 / 16.0, jnp.where((tap == 1) | (tap == 3), 4.0 / 16.0, 1.0 / 16.0))
    return rows, jnp.where(inside, weight, 0.0).astype(BF16)


def place_tables(stack, pairs, shift, slab, camera, owner):
    for step in range(pairs):
        rows, early = place_table(shift, slab ^ (2 * step), camera, owner)
        stack[step * LANE : step * LANE + PLACED, :] = rows
        stack[step * LANE + PLACED : step * LANE + SLOTS, :] = early
        stack[step * LANE + SLOTS : (step + 1) * LANE, :] = jnp.zeros((LANE - SLOTS, 4 * camera), BF16)


def spread_shifts(values, slots):
    plane = lax.broadcasted_iota(jnp.int32, (slots, LANE), 0) & 3
    return jnp.where(plane < 2, jnp.where(plane == 0, values[0], values[1]), jnp.where(plane == 2, values[2], values[3]))


def strip_picks(widths, columns):
    tile = lax.axis_index("tile")
    tiles = lax.axis_size("tile")
    lane = lax.broadcasted_iota(jnp.int32, (8, columns), 1)
    line = lax.broadcasted_iota(jnp.int32, (8, columns), 0)
    right_width = widths[jnp.minimum(tile, tiles - 2)]
    left_width = widths[jnp.maximum(tile - 1, 0)]
    toward_right = jnp.where((lane == columns - right_width - 8 + line) & (line >= 2), 1.0, 0.0)
    toward_left = jnp.where((lane == left_width + line) & (line < 6), 1.0, 0.0)
    return jnp.concatenate([toward_right, toward_left], 0).astype(BF16)


def pack_own(raw_ref, shear_ref, width_ref, kept_ref, shift_ref, pick_ref, strip_ref, early_ref, *refs):
    out_refs, (shears, widths, sems, stack) = refs[:-4], refs[-4:]
    loads = [
        pltpu.make_async_copy(source, target, sems.at[index])
        for index, (source, target) in enumerate(((raw_ref, kept_ref), (shear_ref, shears), (width_ref, widths)))
    ]
    for load in loads:
        load.start()
    camera = raw_ref.shape[0] // 4
    columns = raw_ref.shape[1]
    slab = lax.axis_index("slab")
    for load in loads[1:]:
        load.wait()
    pick_ref[...] = strip_picks(widths, columns)
    shift_ref[...] = spread_shifts(shears, LANE)
    place_tables(stack, len(out_refs), shift_ref[:, :1], slab, camera, slab & 1)
    loads[0].wait()
    placed = dot(stack[...], kept_ref[:, : columns - LANE])
    for step, out_ref in enumerate(out_refs):
        out_ref[...] = placed[step * LANE : step * LANE + PLACED].astype(BF16)
        early_ref[step] = placed[step * LANE + PLACED : step * LANE + SLOTS]
    strip_ref[...] = dot_rows(pick_ref[...], kept_ref[...])


def pack_other(other_ref, shear_ref, pick_ref, strip_ref, early_ref, *refs):
    (shears, sem, stack), refs = refs[-3:], refs[:-3]
    pairs = (len(refs) - 3) // 2
    own_refs, (right_ref, left_ref, shift_ref), out_refs = refs[:pairs], refs[pairs : pairs + 3], refs[pairs + 3 :]
    load = pltpu.make_async_copy(shear_ref, shears, sem)
    load.start()
    camera = other_ref.shape[0] // 4
    columns = other_ref.shape[1]
    slab = lax.axis_index("slab")
    for own_ref, out_ref in zip(own_refs, out_refs):
        out_ref[:PLACED, :] = own_ref[...]
    strips = jnp.concatenate([strip_ref[...], dot_rows(pick_ref[...], other_ref[...])], 0)
    right_ref[...] = jnp.concatenate([strips[:8], strips[16:24]], 0).astype(BF16)
    left_ref[...] = jnp.concatenate([strips[8:16], strips[24:]], 0).astype(BF16)
    load.wait()
    shift_ref[...] = spread_shifts(shears, LANE)
    place_tables(stack, pairs, shift_ref[:, :1], slab, camera, ~slab & 1)
    placed = dot(stack[...], other_ref[:, : columns - LANE])
    for step, out_ref in enumerate(out_refs):
        out_ref[PLACED : 2 * PLACED, :] = placed[step * LANE : step * LANE + PLACED].astype(BF16)
        out_ref[2 * PLACED :, :] = (early_ref[step] + placed[step * LANE + PLACED : step * LANE + SLOTS]).astype(BF16)


def stage(order_ref, *refs):
    sems, refs = refs[-1], refs[:-1]
    count = len(refs) // 2
    loads = [pltpu.make_async_copy(refs[index], refs[count + index], sems.at[index]) for index in range(count)]
    for load in loads:
        load.start()
    for load in loads:
        load.wait()


def pack_second(raw_ref, other_ref, shift_ref, other_shift_ref, from_left_ref, from_right_ref, order_ref, *out_refs):
    camera = raw_ref.shape[0] // 4
    columns = raw_ref.shape[1]
    slab = lax.axis_index("slab")
    tile = lax.axis_index("tile")
    right = jnp.where(tile < lax.axis_size("tile") - 1, from_right_ref[...].astype(F32), 0.0)
    left = jnp.where(tile > 0, from_left_ref[...].astype(F32), 0.0)
    for step, out_ref in enumerate(out_refs):
        total = 0.0
        for owner, (planes_ref, shifts_ref) in enumerate(((raw_ref, shift_ref), (other_ref, other_shift_ref))):
            rows, early = place_table(shifts_ref[:, :1], slab ^ (2 * step), camera, (slab & 1) ^ owner)
            planes = planes_ref[:, columns - LANE :]
            out_ref[owner * PLACED : (owner + 1) * PLACED, :] = dot(rows, planes).astype(BF16)
            total = total + dot(early, planes)
            own = slice(8 * owner, 8 * owner + 8)
            strips = jnp.concatenate([right[own], left[own]], 0).astype(BF16)
            start = 2 * PLACED + 8 + 16 * owner
            table = jnp.concatenate(
                [rows.astype(F32), early.astype(F32), jnp.zeros((LANE - SLOTS, rows.shape[1]), F32)], 0
            )
            out_ref[start : start + 16, :] = dot_rows(strips, table.astype(BF16)).astype(BF16)
        out_ref[2 * PLACED : 2 * PLACED + 8, :] = total.astype(BF16)


def collect(in_refs, volume, scans):
    slab = lax.axis_index("slab")
    lanes = in_refs[0].shape[-1]
    groups = scans // 4
    outside = jnp.zeros((LANE,) + volume.shape[2:], BF16)
    volume[0] = outside
    volume[groups + 1] = outside
    for index in range(groups):
        group = (slab ^ index) + 1
        start = (index & 1) * PLACED
        volume[group, :PLACED, :lanes] = in_refs[index >> 1][start : start + PLACED, :]
        volume[group, PLACED:SLOTS, :lanes] = in_refs[index >> 1][2 * PLACED : 2 * PLACED + 8, :]
        volume[group, SLOTS:, :lanes] = jnp.zeros((LANE - SLOTS, lanes), BF16)


def split(value):
    high = value.astype(BF16)
    return high, (value - high.astype(F32)).astype(BF16)


def row_scan(rowscan_ref, volume, block, wide):
    rows = 8 * SLAB_ROWS
    both = dot(rowscan_ref[...], volume[2 * block : 2 * block + 4].reshape(4 * LANE, volume.shape[-1]))
    for sigma in range(2):
        total = both[2 * sigma * rows : (2 * sigma + 1) * rows] + both[(2 * sigma + 1) * rows : (2 * sigma + 2) * rows]
        high, low = split(total)
        wide[2 * sigma, block * rows : (block + 1) * rows, :] = high
        wide[2 * sigma + 1, block * rows : (block + 1) * rows, :] = low


def dot_parts(high, low, right):
    both = dot(jnp.concatenate([high, low], 0), right)
    return both[: high.shape[0]] + both[high.shape[0] :]


def across(wide, rows, lanes, column_ref, taken):
    total = None
    for sigma in range(2):
        high, low = wide[2 * sigma, rows, lanes], wide[2 * sigma + 1, rows, lanes]
        table = column_ref[2 * sigma, taken]
        if rows == slice(None):
            right = jnp.concatenate([table, table, column_ref[2 * sigma + 1, taken]], 0)
            part = dot(jnp.concatenate([high, low, high], 1), right)
        else:
            part = dot(high, table) + dot(low, table) + dot(high, column_ref[2 * sigma + 1, taken])
        total = part if total is None else total + part
    return total


def level_part(level_ref, level_column_ref, volume, scans):
    groups = scans // 4
    high, low = split(dot(level_ref[...], volume[1 : groups + 1].reshape(groups * LANE, volume.shape[-1])))
    return dot_parts(high, low, level_column_ref[...])


def first_half(count, scans, rowscan_ref, level_ref, column_ref, level_column_ref, *refs):
    in_refs, (partial_ref, coarse_ref, volume, wide) = refs[:count], refs[count:]
    collect(in_refs, volume, scans)
    for block in range(scans // 8):
        row_scan(rowscan_ref, volume, block, wide)
    cut = wide.shape[-1]
    for start in range(0, partial_ref.shape[1], 2 * LANE):
        low, high = max(start - LANE, 0), min(start + 3 * LANE, cut)
        taken = slice(low - start + LANE, high - start + LANE)
        partial_ref[:, start : start + 2 * LANE] = across(wide, slice(None), slice(low, high), column_ref, taken)
    coarse_ref[...] = level_part(level_ref, level_column_ref, volume, scans)


def second_half(count, scans, rowscan_ref, level_ref, column_ref, level_column_ref, two_ref, two_column_ref, *refs):
    partial_ref, coarse_ref, *in_refs = refs[: 2 + count]
    difference_ref, one_ref, second_ref, volume, strips, wide, held, held_one, held_second, sems = refs[2 + count :]
    slab = lax.axis_index("slab")
    slabs = lax.axis_size("slab")
    tile = lax.axis_index("tile")
    tiles = lax.axis_size("tile")
    groups = scans // 4
    columns = partial_ref.shape[1]
    cut = columns - LANE
    collect(in_refs, volume, scans)
    for index in range(groups):
        place = pl.multiple_of((slab ^ index) * LANE, LANE)
        start = 2 * PLACED + 8 + 16 * (index & 1)
        strips[:, pl.ds(place, LANE)] = in_refs[index >> 1][start : start + 16, :]
    line = lax.broadcasted_iota(jnp.int32, (16, LANE), 0)
    lane = lax.broadcasted_iota(jnp.int32, (16, LANE), 1)
    spread = jnp.where(lane == jnp.where(line < 8, line, line + LANE - 16), 1.0, 0.0).astype(BF16)
    rim = lax.dot_general(strips[...], spread, (((0,), (0,)), ((), ())), preferred_element_type=F32)
    volume[1 : groups + 1, :, LANE:] = rim.astype(BF16).reshape(groups, LANE, LANE)

    copies = []
    rows = 8 * SLAB_ROWS
    left = lax.broadcasted_iota(jnp.int32, (2 * rows, LANE), 1) < LANE // 2
    for pair in range(scans // 16):
        for block in (2 * pair, 2 * pair + 1):
            row_scan(rowscan_ref, volume, block, wide)
        here = slice(2 * pair * rows, 2 * (pair + 1) * rows)
        late = across(wide, here, slice(None), column_ref, slice(None))
        ends = late[:, LANE:]
        for start in range(0, columns, LANE):
            total = partial_ref[here, start : start + LANE]
            if start == cut:
                total = total + late[:, :LANE]
            if start == 0:
                total = total + jnp.where(left, ends, 0.0)
            if start == cut - LANE:
                total = total + jnp.where(left, 0.0, ends)
            total = total.reshape(2, SLAB_ROWS, 8, LANE)
            joined = jnp.concatenate([total[0], total[1]], 1)
            held[:, 16 * pair : 16 * pair + 16, start : start + LANE] = joined.astype(BF16)
        copy = pltpu.make_async_copy(
            held.at[:, 16 * pair : 16 * pair + 16, :], difference_ref.at[:, 16 * pair : 16 * pair + 16, :], sems.at[pair]
        )
        copy.start()
        copies.append(copy)
    level = coarse_ref[...] + level_part(level_ref, level_column_ref, volume, scans)
    half = columns // 2
    shape = (LEVEL, scans // 2, level.shape[-1])
    level = level.reshape(shape)
    row = slab * (SLAB_ROWS // 2) - 2 + lax.broadcasted_iota(jnp.int32, shape, 0)
    place = lax.broadcasted_iota(jnp.int32, shape, 2) - half
    keep = (row >= 0) & (row < slabs * (SLAB_ROWS // 2))
    keep = keep & ((place < 0) | (place >= 2) | (tile > 0)) & ((place < 2) | (tile < tiles - 1))
    ready = jnp.where(keep, level, 0.0).astype(BF16)
    held_one[...] = ready[2:10, :, :half]
    copy = pltpu.make_async_copy(held_one, one_ref, sems.at[scans // 16])
    copy.start()
    copies.append(copy)

    high, low = split(dot(two_ref[...], ready.reshape(LEVEL * scans // 2, level.shape[-1])))
    second = dot_parts(high, low, two_column_ref[...])
    held_second[...] = second.reshape(second_ref.shape).astype(BF16)
    copy = pltpu.make_async_copy(held_second, second_ref, sems.at[scans // 16 + 1])
    copy.start()
    copies.append(copy)

    for copy in copies:
        copy.wait()


VECTOR = pl.BlockSpec(memory_space=pltpu.VMEM)
ANYWHERE = pl.BlockSpec(memory_space=pl.ANY)
OUTSIDE = pl.BlockSpec(memory_space=pltpu.HBM)
PARAMS = pltpu.CompilerParams(vmem_limit_bytes=20 * 1024 * 1024)


def along(chunks, slabs):
    got = list(chunks)
    for step in sorted(range(1, len(chunks)), key=lambda step: (-(step & -step), step)):
        got[step] = lax.ppermute(chunks[step], "slab", [(i, i ^ (2 * step)) for i in range(slabs)])
    return got


def shifted(block, distance):
    count = lax.axis_size("tile")
    return lax.ppermute(block, "tile", [(i, (i + distance) % count) for i in range(count)])


def body(raw_stack, shear_offsets, intersection_widths):
    slabs = lax.axis_size("slab")
    planes, camera, columns = raw_stack.shape
    scans = planes * slabs
    cut = columns - LANE
    pairs = slabs // 2
    table = {name: jnp.asarray(value) for name, value in tables(scans, columns).items()}
    raw = raw_stack.reshape(planes * camera, columns)
    swap = [(i, i ^ 1) for i in range(slabs)]
    other = lax.ppermute(raw, "slab", swap)
    other_shear = lax.ppermute(shear_offsets, "slab", swap)
    outside = [pltpu.with_memory_space_constraint(each, pltpu.HBM) for each in (raw, shear_offsets, intersection_widths)]
    strip = jax.ShapeDtypeStruct((16, planes * camera), BF16)
    shift = jax.ShapeDtypeStruct((LANE, LANE), jnp.int32)
    raw, own_shift, pick, own_strip, early, *own = pl.pallas_call(
        pack_own,
        out_shape=[
            jax.ShapeDtypeStruct((planes * camera, columns), BF16),
            shift,
            jax.ShapeDtypeStruct((16, columns), BF16),
            jax.ShapeDtypeStruct((16, planes * camera), F32),
            jax.ShapeDtypeStruct((pairs, 8, cut), F32),
        ]
        + [jax.ShapeDtypeStruct((PLACED, cut), BF16)] * pairs,
        in_specs=[OUTSIDE] * 3,
        out_specs=[VECTOR] * (5 + pairs),
        scratch_shapes=[
            pltpu.SMEM(shear_offsets.shape, jnp.int32),
            pltpu.SMEM(intersection_widths.shape, jnp.int32),
            pltpu.SemaphoreType.DMA((3,)),
            pltpu.VMEM((pairs * LANE, planes * camera), BF16),
        ],
        compiler_params=PARAMS,
        name="pack_own",
    )(*outside)
    toward_right, toward_left, other_shift, *chunks = pl.pallas_call(
        pack_other,
        out_shape=[strip, strip, shift] + [jax.ShapeDtypeStruct((2 * PLACED + 8, cut), BF16)] * pairs,
        in_specs=[VECTOR, ANYWHERE] + [VECTOR] * (3 + pairs),
        out_specs=[VECTOR] * (3 + pairs),
        scratch_shapes=[
            pltpu.SMEM(shear_offsets.shape, jnp.int32),
            pltpu.SemaphoreType.DMA,
            pltpu.VMEM((pairs * LANE, planes * camera), BF16),
        ],
        compiler_params=PARAMS,
        name="pack_other",
    )(other, other_shear, pick, own_strip, early, *own)
    got_first = along(chunks, slabs)
    from_left = shifted(toward_right, 1)
    from_right = shifted(toward_left, -1)
    second = jax.ShapeDtypeStruct((2 * PLACED + 40, LANE), BF16)
    names = list(table)
    staged = pl.pallas_call(
        stage,
        out_shape=[jax.ShapeDtypeStruct(table[name].shape, BF16) for name in names],
        in_specs=[ANYWHERE] + [OUTSIDE] * len(names),
        out_specs=[VECTOR] * len(names),
        scratch_shapes=[pltpu.SemaphoreType.DMA((len(names),))],
        compiler_params=PARAMS,
        name="stage",
    )(toward_left, *[pltpu.with_memory_space_constraint(table[name], pltpu.HBM) for name in names])
    table = dict(zip(names, staged))
    chunks = pl.pallas_call(
        pack_second,
        out_shape=[second] * pairs,
        in_specs=[VECTOR] * 6 + [ANYWHERE],
        out_specs=[VECTOR] * pairs,
        compiler_params=PARAMS,
        name="pack_second",
    )(raw, other, own_shift, other_shift, from_left, from_right, table["two"])
    chunks, got_first[2] = lax.optimization_barrier((chunks, got_first[2]))
    got_second = along(chunks, slabs)
    partial, coarse = pl.pallas_call(
        functools.partial(first_half, pairs, scans),
        out_shape=[
            jax.ShapeDtypeStruct((scans * SLAB_ROWS, columns), F32),
            jax.ShapeDtypeStruct((LEVEL * scans // 2, columns // 2 + LANE), F32),
        ],
        in_specs=[VECTOR] * (4 + pairs),
        out_specs=[VECTOR] * 2,
        scratch_shapes=[
            pltpu.VMEM((slabs + 2, LANE, cut), BF16),
            pltpu.VMEM((4, scans * SLAB_ROWS, cut), BF16),
        ],
        compiler_params=PARAMS,
        name="first_half",
    )(table["rowscan"], table["level"], table["column_first"], table["level_first"], *got_first)
    got_second, partial = lax.optimization_barrier((got_second, partial))
    return pl.pallas_call(
        functools.partial(second_half, pairs, scans),
        out_shape=[
            jax.ShapeDtypeStruct((SLAB_ROWS, scans, columns), BF16),
            jax.ShapeDtypeStruct((SLAB_ROWS // 2, scans // 2, columns // 2), BF16),
            jax.ShapeDtypeStruct((SLAB_ROWS // 4, scans // 4, columns // 4), BF16),
        ],
        in_specs=[VECTOR] * (8 + pairs),
        out_specs=[OUTSIDE] * 3,
        scratch_shapes=[
            pltpu.VMEM((slabs + 2, LANE, 2 * LANE), BF16),
            pltpu.VMEM((16, slabs * LANE), BF16),
            pltpu.VMEM((4, scans * SLAB_ROWS, 2 * LANE), BF16),
            pltpu.VMEM((SLAB_ROWS, scans, columns), BF16),
            pltpu.VMEM((SLAB_ROWS // 2, scans // 2, columns // 2), BF16),
            pltpu.VMEM((SLAB_ROWS // 4, scans // 4, columns // 4), BF16),
            pltpu.SemaphoreType.DMA((scans // 16 + 2,)),
        ],
        compiler_params=PARAMS,
        name="second_half",
    )(
        table["rowscan"],
        table["level"],
        table["column_last"],
        table["level_last"],
        table["two"],
        table["two_column"],
        partial,
        coarse,
        *got_second,
    )


def solution(mesh):
    placed = (P("slab", None, "tile"), P("slab"), P())
    return jax.shard_map(
        body,
        mesh=mesh,
        in_specs=placed,
        out_specs=(P("slab", None, "tile"), P("slab", None, "tile"), P("slab", None, "tile")),
        check_vma=False,
    )
```

```python
import functools
import math

import jax
import jax.numpy as jnp
import ml_dtypes
import numpy as np
from jax import lax
from jax.experimental import pallas as pl
from jax.experimental.pallas import tpu as pltpu
from jax.sharding import PartitionSpec as P

SLAB_ROWS = 16
STRIP = 6
RADIUS = 4
NEED = SLAB_ROWS + 2 * RADIUS
PLACED = 4 * NEED
SLOTS = PLACED + 8
LEVEL = 11
LANE = 128
BLOCK = 48
F32 = jnp.float32
BF16 = jnp.bfloat16


def gauss_taps(sigma_value):
    entries = [math.exp(-(j * j) / (2.0 * sigma_value * sigma_value)) for j in range(-RADIUS, RADIUS + 1)]
    weight_sum = sum(entries)
    return np.array([entry / weight_sum for entry in entries], np.float64)


BINOMIAL = np.array([1.0, 4.0, 6.0, 4.0, 1.0], np.float64) / 16.0


def band(weights, source, target):
    reach = len(weights) // 2
    offset = source[None, :] - target[:, None] + reach
    inside = (offset >= 0) & (offset < len(weights))
    return np.where(inside, weights[np.clip(offset, 0, len(weights) - 1)], 0.0)


def two_parts(table):
    high = table.astype(ml_dtypes.bfloat16)
    return [high, (table - high.astype(np.float64)).astype(ml_dtypes.bfloat16)]


def row_scan_table(row_band, scan_band, early=None):
    rows_out, rows_in = row_band.shape
    scans_out, groups = scan_band.shape[0], scan_band.shape[1] // 4
    scans = scan_band.reshape(scans_out, groups, 4)
    table = np.zeros((rows_out, scans_out, groups, LANE))
    table[..., :PLACED] = np.einsum("yr,sgp->ysgrp", row_band, scans).reshape(rows_out, scans_out, groups, PLACED)
    if early is not None:
        for group in range(groups):
            start = PLACED + 4 * (~group & 1)
            table[:, :, group, start : start + 4] = early[:, None, None] * scans[:, group]
    return table.reshape(rows_out * scans_out, groups * LANE)


def tables(scans, columns):
    row_in = np.arange(NEED) - RADIUS
    own = np.arange(SLAB_ROWS)
    near = np.arange(16) - 4
    block = np.arange(8)
    cut = columns - LANE
    rim = np.where(np.arange(LANE) < LANE // 2, columns, -LANE) + np.arange(LANE)
    last = np.concatenate([np.arange(cut, columns), rim])
    touched = np.concatenate([np.arange(cut, columns), np.arange(LANE // 2), np.arange(cut - LANE // 2, cut)])
    rowscan, column_first, column_last = [], [], []
    for sigma, sign in ((1.0, 1.0), (1.6, -1.0)):
        taps = gauss_taps(sigma)
        rowscan += two_parts(row_scan_table(band(taps, row_in, own), band(taps, near, block)))
        column_first += two_parts(sign * band(taps, np.arange(4 * LANE) - LANE, np.arange(2 * LANE)).T)
        column_last += two_parts(sign * band(taps, last, touched).T)
    level_rows = 2 * np.arange(LEVEL) - 4
    early = np.arange(LEVEL) == 0
    level = row_scan_table(
        band(BINOMIAL, row_in, level_rows) * ~early[:, None], band(BINOMIAL, near, 2 * np.arange(4)), early * 1.0
    )
    level = np.pad(level, ((0, BLOCK - 4 * LEVEL), (0, 0))).astype(ml_dtypes.bfloat16)
    edges = np.array([-4, -2, columns, columns + 2])
    targets = np.concatenate([2 * np.arange(columns // 2), edges])
    two = np.einsum(
        "yr,sbp->ysbrp",
        band(BINOMIAL, np.arange(LEVEL) - 2, 2 * np.arange(4)),
        band(BINOMIAL, np.arange(scans // 2), 2 * np.arange(scans // 4)).reshape(scans // 4, scans // 8, 4),
    ).reshape(scans, scans // 8, 4 * LEVEL)
    two = np.pad(two, ((0, 0), (0, 0), (0, BLOCK - 4 * LEVEL))).reshape(scans, scans // 8 * BLOCK)
    row, scan = np.divmod(np.arange(SLAB_ROWS // 2 * scans // 2), scans // 2)
    order = np.arange(scans // 8 * BLOCK)[None, :] == (scan // 4 * BLOCK + 4 * (row + 2) + scan % 4)[:, None]
    fill = ((0, 0), (0, LANE - 4))
    small = ml_dtypes.bfloat16
    return dict(
        rowscan=np.concatenate(rowscan + [level], 0),
        order=order.astype(small),
        column_first=np.stack(column_first),
        column_last=np.stack(column_last),
        level_first=np.pad(band(BINOMIAL, np.arange(cut), targets).T, fill).astype(small),
        level_last=np.pad(band(BINOMIAL, last, targets).T, fill).astype(small),
        two=two.astype(small),
        two_column=np.pad(band(BINOMIAL, targets // 2, 2 * np.arange(columns // 4)), fill).T.astype(small),
    )


def dot(left, right):
    return jnp.dot(left, right, preferred_element_type=F32)


def dot_rows(left, right):
    return lax.dot_general(left, right, (((1,), (1,)), ((), ())), preferred_element_type=F32)


def place_table(shift, slab, camera, owner):
    lanes = 4 * camera
    slot = lax.broadcasted_iota(jnp.int32, (PLACED, 1), 0)
    plane = slot & 3
    source = slab * SLAB_ROWS - RADIUS + (slot >> 2) - shift[:PLACED]
    wanted = jnp.where((source >= 0) & (source < camera), plane * camera + source, -1)
    lane = lax.broadcasted_iota(jnp.int32, (PLACED, lanes), 1)
    rows = jnp.where(lane == wanted, 1.0, 0.0).astype(BF16)
    slot = lax.broadcasted_iota(jnp.int32, (8, 1), 0)
    source = lax.broadcasted_iota(jnp.int32, (8, lanes), 1) - (slot & 3) * camera
    tap = source + shift[:8] - (slab * SLAB_ROWS - 6)
    inside = (source >= 0) & (source < camera) & ((slot >> 2) == owner) & (tap >= 0) & (tap < 5)
    weight = jnp.where(tap == 2, 6.0 / 16.0, jnp.where((tap == 1) | (tap == 3), 4.0 / 16.0, 1.0 / 16.0))
    return rows, jnp.where(inside, weight, 0.0).astype(BF16)


def place_tables(stack, pairs, shift, slab, camera, owner):
    for step in range(pairs):
        rows, early = place_table(shift, slab ^ (2 * step), camera, owner)
        stack[step * LANE : step * LANE + PLACED, :] = rows
        stack[step * LANE + PLACED : step * LANE + SLOTS, :] = early
        stack[step * LANE + SLOTS : (step + 1) * LANE, :] = jnp.zeros((LANE - SLOTS, 4 * camera), BF16)


def spread_shifts(values, slots):
    plane = lax.broadcasted_iota(jnp.int32, (slots, LANE), 0) & 3
    return jnp.where(plane < 2, jnp.where(plane == 0, values[0], values[1]), jnp.where(plane == 2, values[2], values[3]))


def strip_picks(widths, columns):
    tile = lax.axis_index("tile")
    tiles = lax.axis_size("tile")
    lane = lax.broadcasted_iota(jnp.int32, (8, columns), 1)
    line = lax.broadcasted_iota(jnp.int32, (8, columns), 0)
    right_width = widths[jnp.minimum(tile, tiles - 2)]
    left_width = widths[jnp.maximum(tile - 1, 0)]
    toward_right = jnp.where((lane == columns - right_width - 8 + line) & (line >= 2), 1.0, 0.0)
    toward_left = jnp.where((lane == left_width + line) & (line < 6), 1.0, 0.0)
    return jnp.concatenate([toward_right, toward_left], 0).astype(BF16)


def pack_own(raw_ref, shear_ref, width_ref, kept_ref, shift_ref, pick_ref, strip_ref, early_ref, *refs):
    out_refs, (shears, widths, sems, stack) = refs[:-4], refs[-4:]
    loads = [
        pltpu.make_async_copy(source, target, sems.at[index])
        for index, (source, target) in enumerate(((raw_ref, kept_ref), (shear_ref, shears), (width_ref, widths)))
    ]
    for load in loads:
        load.start()
    camera = raw_ref.shape[0] // 4
    columns = raw_ref.shape[1]
    slab = lax.axis_index("slab")
    for load in loads[1:]:
        load.wait()
    pick_ref[...] = strip_picks(widths, columns)
    shift_ref[...] = spread_shifts(shears, LANE)
    place_tables(stack, len(out_refs), shift_ref[:, :1], slab, camera, slab & 1)
    loads[0].wait()
    placed = dot(stack[...], kept_ref[:, : columns - LANE])
    for step, out_ref in enumerate(out_refs):
        out_ref[...] = placed[step * LANE : step * LANE + PLACED].astype(BF16)
        early_ref[step] = placed[step * LANE + PLACED : step * LANE + SLOTS]
    strip_ref[...] = dot_rows(pick_ref[...], kept_ref[...])


def pack_other(other_ref, shear_ref, pick_ref, strip_ref, early_ref, *refs):
    (shears, sem, stack), refs = refs[-3:], refs[:-3]
    pairs = (len(refs) - 3) // 2
    own_refs, (right_ref, left_ref, shift_ref), out_refs = refs[:pairs], refs[pairs : pairs + 3], refs[pairs + 3 :]
    load = pltpu.make_async_copy(shear_ref, shears, sem)
    load.start()
    camera = other_ref.shape[0] // 4
    columns = other_ref.shape[1]
    slab = lax.axis_index("slab")
    for own_ref, out_ref in zip(own_refs, out_refs):
        out_ref[:PLACED, :] = own_ref[...]
    strips = jnp.concatenate([strip_ref[...], dot_rows(pick_ref[...], other_ref[...])], 0)
    right_ref[...] = jnp.concatenate([strips[:8], strips[16:24]], 0).astype(BF16)
    left_ref[...] = jnp.concatenate([strips[8:16], strips[24:]], 0).astype(BF16)
    load.wait()
    shift_ref[...] = spread_shifts(shears, LANE)
    place_tables(stack, pairs, shift_ref[:, :1], slab, camera, ~slab & 1)
    placed = dot(stack[...], other_ref[:, : columns - LANE])
    for step, out_ref in enumerate(out_refs):
        out_ref[PLACED : 2 * PLACED, :] = placed[step * LANE : step * LANE + PLACED].astype(BF16)
        out_ref[2 * PLACED :, :] = (early_ref[step] + placed[step * LANE + PLACED : step * LANE + SLOTS]).astype(BF16)


def stage(order_ref, *refs):
    sems, refs = refs[-1], refs[:-1]
    count = len(refs) // 2
    loads = [pltpu.make_async_copy(refs[index], refs[count + index], sems.at[index]) for index in range(count)]
    for load in loads:
        load.start()
    for load in loads:
        load.wait()


def pack_second(raw_ref, other_ref, shift_ref, other_shift_ref, from_left_ref, from_right_ref, order_ref, *out_refs):
    camera = raw_ref.shape[0] // 4
    columns = raw_ref.shape[1]
    slab = lax.axis_index("slab")
    tile = lax.axis_index("tile")
    right = jnp.where(tile < lax.axis_size("tile") - 1, from_right_ref[...].astype(F32), 0.0)
    left = jnp.where(tile > 0, from_left_ref[...].astype(F32), 0.0)
    for step, out_ref in enumerate(out_refs):
        total, placed = 0.0, []
        for owner, (planes_ref, shifts_ref) in enumerate(((raw_ref, shift_ref), (other_ref, other_shift_ref))):
            rows, early = place_table(shifts_ref[:, :1], slab ^ (2 * step), camera, (slab & 1) ^ owner)
            planes = planes_ref[:, columns - LANE :]
            out_ref[owner * PLACED : (owner + 1) * PLACED, :] = dot(rows, planes).astype(BF16)
            total = total + dot(early, planes)
            own = slice(8 * owner, 8 * owner + 8)
            strips = jnp.concatenate([right[own], left[own]], 0).astype(BF16)
            table = jnp.concatenate(
                [rows.astype(F32), early.astype(F32), jnp.zeros((LANE - SLOTS, rows.shape[1]), F32)], 0
            )
            columns_of = dot_rows(strips, table.astype(BF16))
            placed += [columns_of[:STRIP], columns_of[16 - STRIP :]]
        out_ref[2 * PLACED : 2 * PLACED + 8, :] = total.astype(BF16)
        out_ref[2 * PLACED + 8 :, :] = jnp.concatenate(placed, 0).astype(BF16)


def collect(in_refs, volume, scans):
    slab = lax.axis_index("slab")
    lanes = in_refs[0].shape[-1]
    groups = scans // 4
    outside = jnp.zeros((LANE,) + volume.shape[2:], BF16)
    volume[0] = outside
    volume[groups + 1] = outside
    for index in range(groups):
        group = (slab ^ index) + 1
        start = (index & 1) * PLACED
        volume[group, :PLACED, :lanes] = in_refs[index >> 1][start : start + PLACED, :]
        volume[group, PLACED:SLOTS, :lanes] = in_refs[index >> 1][2 * PLACED : 2 * PLACED + 8, :]
        volume[group, SLOTS:, :lanes] = jnp.zeros((LANE - SLOTS, lanes), BF16)


def split(value):
    high = value.astype(BF16)
    return high, (value - high.astype(F32)).astype(BF16)


def row_scan(rowscan_ref, volume, block, wide, rough):
    rows = 8 * SLAB_ROWS
    both = dot(rowscan_ref[...], volume[2 * block : 2 * block + 4].reshape(4 * LANE, volume.shape[-1]))
    for sigma in range(2):
        total = both[2 * sigma * rows : (2 * sigma + 1) * rows] + both[(2 * sigma + 1) * rows : (2 * sigma + 2) * rows]
        high, low = split(total)
        wide[2 * sigma, block * rows : (block + 1) * rows, :] = high
        wide[2 * sigma + 1, block * rows : (block + 1) * rows, :] = low
    rough[block * BLOCK : (block + 1) * BLOCK, :] = both[4 * rows :]


def dot_parts(high, low, right):
    both = dot(jnp.concatenate([high, low], 0), right)
    return both[: high.shape[0]] + both[high.shape[0] :]


def across(wide, rows, lanes, column_ref, taken):
    total = None
    for sigma in range(2):
        high, low = wide[2 * sigma, rows, lanes], wide[2 * sigma + 1, rows, lanes]
        table = column_ref[2 * sigma, taken]
        if rows == slice(None):
            right = jnp.concatenate([table, table, column_ref[2 * sigma + 1, taken]], 0)
            part = dot(jnp.concatenate([high, low, high], 1), right)
        else:
            part = dot(high, table) + dot(low, table) + dot(high, column_ref[2 * sigma + 1, taken])
        total = part if total is None else total + part
    return total


def level_part(rough, level_column_ref):
    high, low = split(rough[...])
    return dot_parts(high, low, level_column_ref[...])


def first_half(count, scans, rowscan_ref, column_ref, level_column_ref, *refs):
    in_refs, (partial_ref, coarse_ref, volume, wide, rough) = refs[:count], refs[count:]
    collect(in_refs, volume, scans)
    for block in range(scans // 8):
        row_scan(rowscan_ref, volume, block, wide, rough)
    cut = wide.shape[-1]
    for start in range(0, partial_ref.shape[1], 2 * LANE):
        low, high = max(start - LANE, 0), min(start + 3 * LANE, cut)
        taken = slice(low - start + LANE, high - start + LANE)
        partial_ref[:, start : start + 2 * LANE] = across(wide, slice(None), slice(low, high), column_ref, taken)
    coarse_ref[...] = level_part(rough, level_column_ref)


def second_half(count, scans, rowscan_ref, order_ref, column_ref, level_column_ref, two_ref, two_column_ref, *refs):
    partial_ref, coarse_ref, *in_refs = refs[: 2 + count]
    difference_ref, one_ref, second_ref, volume, strips, wide, rough, held, held_one, held_second, sems = refs[2 + count :]
    slab = lax.axis_index("slab")
    slabs = lax.axis_size("slab")
    tile = lax.axis_index("tile")
    tiles = lax.axis_size("tile")
    groups = scans // 4
    columns = partial_ref.shape[1]
    cut = columns - LANE
    collect(in_refs, volume, scans)
    for index in range(groups):
        place = pl.multiple_of((slab ^ index) * LANE, LANE)
        start = 2 * STRIP * (index & 1)
        both = in_refs[index >> 1][2 * PLACED + 8 :, :].astype(F32)[start : start + 2 * STRIP]
        both = jnp.concatenate([both, jnp.zeros((16 - 2 * STRIP, LANE), F32)], 0)
        strips[:, pl.ds(place, LANE)] = both.astype(BF16)
    line = lax.broadcasted_iota(jnp.int32, (16, LANE), 0)
    lane = lax.broadcasted_iota(jnp.int32, (16, LANE), 1)
    spread = jnp.where(lane == jnp.where(line < STRIP, line, line + LANE - 2 * STRIP), 1.0, 0.0).astype(BF16)
    rim = lax.dot_general(strips[...], spread, (((0,), (0,)), ((), ())), preferred_element_type=F32)
    volume[1 : groups + 1, :, LANE:] = rim.astype(BF16).reshape(groups, LANE, LANE)

    copies = []
    rows = 8 * SLAB_ROWS
    left = lax.broadcasted_iota(jnp.int32, (2 * rows, LANE), 1) < LANE // 2
    for pair in range(scans // 16):
        for block in (2 * pair, 2 * pair + 1):
            row_scan(rowscan_ref, volume, block, wide, rough)
        here = slice(2 * pair * rows, 2 * (pair + 1) * rows)
        late = across(wide, here, slice(None), column_ref, slice(None))
        ends = late[:, LANE:]
        for start in range(0, columns, LANE):
            total = partial_ref[here, start : start + LANE]
            if start == cut:
                total = total + late[:, :LANE]
            if start == 0:
                total = total + jnp.where(left, ends, 0.0)
            if start == cut - LANE:
                total = total + jnp.where(left, 0.0, ends)
            total = total.reshape(2, SLAB_ROWS, 8, LANE)
            joined = jnp.concatenate([total[0], total[1]], 1)
            held[:, 16 * pair : 16 * pair + 16, start : start + LANE] = joined.astype(BF16)
        copy = pltpu.make_async_copy(
            held.at[:, 16 * pair : 16 * pair + 16, :], difference_ref.at[:, 16 * pair : 16 * pair + 16, :], sems.at[pair]
        )
        copy.start()
        copies.append(copy)
    level = coarse_ref[...] + level_part(rough, level_column_ref)
    half = columns // 2
    row = lax.broadcasted_iota(jnp.int32, level.shape, 0)
    within = row
    for block in range(1, scans // 8):
        within = within - jnp.where(row >= block * BLOCK, BLOCK, 0)
    row = slab * (SLAB_ROWS // 2) - 2 + (within >> 2)
    place = lax.broadcasted_iota(jnp.int32, level.shape, 1) - half
    keep = (row >= 0) & (row < slabs * (SLAB_ROWS // 2))
    keep = keep & ((place < 0) | (place >= 2) | (tile > 0)) & ((place < 2) | (tile < tiles - 1))
    ready = jnp.where(keep, level, 0.0).astype(BF16)
    held_one[...] = dot(order_ref[...], ready[:, :half]).reshape(held_one.shape).astype(BF16)
    copy = pltpu.make_async_copy(held_one, one_ref, sems.at[scans // 16])
    copy.start()
    copies.append(copy)

    high, low = split(dot(two_ref[...], ready))
    second = dot_parts(high, low, two_column_ref[...])
    held_second[...] = second.reshape(second_ref.shape).astype(BF16)
    copy = pltpu.make_async_copy(held_second, second_ref, sems.at[scans // 16 + 1])
    copy.start()
    copies.append(copy)

    for copy in copies:
        copy.wait()


VECTOR = pl.BlockSpec(memory_space=pltpu.VMEM)
ANYWHERE = pl.BlockSpec(memory_space=pl.ANY)
OUTSIDE = pl.BlockSpec(memory_space=pltpu.HBM)
PARAMS = pltpu.CompilerParams(vmem_limit_bytes=20 * 1024 * 1024)


def along(chunks, slabs):
    got = list(chunks)
    for step in sorted(range(1, len(chunks)), key=lambda step: (-(step & -step), step)):
        got[step] = lax.ppermute(chunks[step], "slab", [(i, i ^ (2 * step)) for i in range(slabs)])
    return got


def shifted(block, distance):
    count = lax.axis_size("tile")
    return lax.ppermute(block, "tile", [(i, (i + distance) % count) for i in range(count)])


def body(raw_stack, shear_offsets, intersection_widths):
    slabs = lax.axis_size("slab")
    planes, camera, columns = raw_stack.shape
    scans = planes * slabs
    cut = columns - LANE
    pairs = slabs // 2
    table = {name: jnp.asarray(value) for name, value in tables(scans, columns).items()}
    raw = raw_stack.reshape(planes * camera, columns)
    swap = [(i, i ^ 1) for i in range(slabs)]
    other = lax.ppermute(raw, "slab", swap)
    other_shear = lax.ppermute(shear_offsets, "slab", swap)
    outside = [pltpu.with_memory_space_constraint(each, pltpu.HBM) for each in (raw, shear_offsets, intersection_widths)]
    strip = jax.ShapeDtypeStruct((16, planes * camera), BF16)
    shift = jax.ShapeDtypeStruct((LANE, LANE), jnp.int32)
    raw, own_shift, pick, own_strip, early, *own = pl.pallas_call(
        pack_own,
        out_shape=[
            jax.ShapeDtypeStruct((planes * camera, columns), BF16),
            shift,
            jax.ShapeDtypeStruct((16, columns), BF16),
            jax.ShapeDtypeStruct((16, planes * camera), F32),
            jax.ShapeDtypeStruct((pairs, 8, cut), F32),
        ]
        + [jax.ShapeDtypeStruct((PLACED, cut), BF16)] * pairs,
        in_specs=[OUTSIDE] * 3,
        out_specs=[VECTOR] * (5 + pairs),
        scratch_shapes=[
            pltpu.SMEM(shear_offsets.shape, jnp.int32),
            pltpu.SMEM(intersection_widths.shape, jnp.int32),
            pltpu.SemaphoreType.DMA((3,)),
            pltpu.VMEM((pairs * LANE, planes * camera), BF16),
        ],
        compiler_params=PARAMS,
        name="pack_own",
    )(*outside)
    toward_right, toward_left, other_shift, *chunks = pl.pallas_call(
        pack_other,
        out_shape=[strip, strip, shift] + [jax.ShapeDtypeStruct((2 * PLACED + 8, cut), BF16)] * pairs,
        in_specs=[VECTOR, ANYWHERE] + [VECTOR] * (3 + pairs),
        out_specs=[VECTOR] * (3 + pairs),
        scratch_shapes=[
            pltpu.SMEM(shear_offsets.shape, jnp.int32),
            pltpu.SemaphoreType.DMA,
            pltpu.VMEM((pairs * LANE, planes * camera), BF16),
        ],
        compiler_params=PARAMS,
        name="pack_other",
    )(other, other_shear, pick, own_strip, early, *own)
    got_first = along(chunks, slabs)
    from_left = shifted(toward_right, 1)
    from_right = shifted(toward_left, -1)
    second = jax.ShapeDtypeStruct((2 * PLACED + 8 + 4 * STRIP, LANE), BF16)
    names = list(table)
    staged = pl.pallas_call(
        stage,
        out_shape=[jax.ShapeDtypeStruct(table[name].shape, BF16) for name in names],
        in_specs=[ANYWHERE] + [OUTSIDE] * len(names),
        out_specs=[VECTOR] * len(names),
        scratch_shapes=[pltpu.SemaphoreType.DMA((len(names),))],
        compiler_params=PARAMS,
        name="stage",
    )(toward_left, *[pltpu.with_memory_space_constraint(table[name], pltpu.HBM) for name in names])
    table = dict(zip(names, staged))
    chunks = pl.pallas_call(
        pack_second,
        out_shape=[second] * pairs,
        in_specs=[VECTOR] * 6 + [ANYWHERE],
        out_specs=[VECTOR] * pairs,
        compiler_params=PARAMS,
        name="pack_second",
    )(raw, other, own_shift, other_shift, from_left, from_right, table["two"])
    chunks, got_first[2] = lax.optimization_barrier((chunks, got_first[2]))
    got_second = along(chunks, slabs)
    partial, coarse = pl.pallas_call(
        functools.partial(first_half, pairs, scans),
        out_shape=[
            jax.ShapeDtypeStruct((scans * SLAB_ROWS, columns), F32),
            jax.ShapeDtypeStruct((scans // 8 * BLOCK, columns // 2 + LANE), F32),
        ],
        in_specs=[VECTOR] * (3 + pairs),
        out_specs=[VECTOR] * 2,
        scratch_shapes=[
            pltpu.VMEM((slabs + 2, LANE, cut), BF16),
            pltpu.VMEM((4, scans * SLAB_ROWS, cut), BF16),
            pltpu.VMEM((scans // 8 * BLOCK, cut), F32),
        ],
        compiler_params=PARAMS,
        name="first_half",
    )(table["rowscan"], table["column_first"], table["level_first"], *got_first)
    got_second, partial = lax.optimization_barrier((got_second, partial))
    return pl.pallas_call(
        functools.partial(second_half, pairs, scans),
        out_shape=[
            jax.ShapeDtypeStruct((SLAB_ROWS, scans, columns), BF16),
            jax.ShapeDtypeStruct((SLAB_ROWS // 2, scans // 2, columns // 2), BF16),
            jax.ShapeDtypeStruct((SLAB_ROWS // 4, scans // 4, columns // 4), BF16),
        ],
        in_specs=[VECTOR] * (8 + pairs),
        out_specs=[OUTSIDE] * 3,
        scratch_shapes=[
            pltpu.VMEM((slabs + 2, LANE, 2 * LANE), BF16),
            pltpu.VMEM((16, slabs * LANE), BF16),
            pltpu.VMEM((4, scans * SLAB_ROWS, 2 * LANE), BF16),
            pltpu.VMEM((scans // 8 * BLOCK, 2 * LANE), F32),
            pltpu.VMEM((SLAB_ROWS, scans, columns), BF16),
            pltpu.VMEM((SLAB_ROWS // 2, scans // 2, columns // 2), BF16),
            pltpu.VMEM((SLAB_ROWS // 4, scans // 4, columns // 4), BF16),
            pltpu.SemaphoreType.DMA((scans // 16 + 2,)),
        ],
        compiler_params=PARAMS,
        name="second_half",
    )(
        table["rowscan"],
        table["order"],
        table["column_last"],
        table["level_last"],
        table["two"],
        table["two_column"],
        partial,
        coarse,
        *got_second,
    )


def solution(mesh):
    placed = (P("slab", None, "tile"), P("slab"), P())
    return jax.shard_map(
        body,
        mesh=mesh,
        in_specs=placed,
        out_specs=(P("slab", None, "tile"), P("slab", None, "tile"), P("slab", None, "tile")),
        check_vma=False,
    )
```

```python
import functools
import math

import jax
import jax.numpy as jnp
import ml_dtypes
import numpy as np
from jax import lax
from jax.experimental import pallas as pl
from jax.experimental.pallas import tpu as pltpu
from jax.sharding import PartitionSpec as P

SLAB_ROWS = 16
STRIP = 6
RADIUS = 4
NEED = SLAB_ROWS + 2 * RADIUS
PLACED = 4 * NEED
SLOTS = PLACED + 8
LEVEL = 11
LANE = 128
BLOCK = 48
F32 = jnp.float32
BF16 = jnp.bfloat16


def gauss_taps(sigma_value):
    entries = [math.exp(-(j * j) / (2.0 * sigma_value * sigma_value)) for j in range(-RADIUS, RADIUS + 1)]
    weight_sum = sum(entries)
    return np.array([entry / weight_sum for entry in entries], np.float64)


BINOMIAL = np.array([1.0, 4.0, 6.0, 4.0, 1.0], np.float64) / 16.0


def band(weights, source, target):
    reach = len(weights) // 2
    offset = source[None, :] - target[:, None] + reach
    inside = (offset >= 0) & (offset < len(weights))
    return np.where(inside, weights[np.clip(offset, 0, len(weights) - 1)], 0.0)


def two_parts(table):
    high = table.astype(ml_dtypes.bfloat16)
    return [high, (table - high.astype(np.float64)).astype(ml_dtypes.bfloat16)]


def row_scan_table(row_band, scan_band, early=None):
    rows_out, rows_in = row_band.shape
    scans_out, groups = scan_band.shape[0], scan_band.shape[1] // 4
    scans = scan_band.reshape(scans_out, groups, 4)
    table = np.zeros((rows_out, scans_out, groups, LANE))
    table[..., :PLACED] = np.einsum("yr,sgp->ysgrp", row_band, scans).reshape(rows_out, scans_out, groups, PLACED)
    if early is not None:
        for group in range(groups):
            start = PLACED + 4 * (~group & 1)
            table[:, :, group, start : start + 4] = early[:, None, None] * scans[:, group]
    return table.reshape(rows_out * scans_out, groups * LANE)


def tables(scans, columns):
    row_in = np.arange(NEED) - RADIUS
    own = np.arange(SLAB_ROWS)
    near = np.arange(16) - 4
    block = np.arange(8)
    cut = columns - LANE
    rim = np.where(np.arange(LANE) < LANE // 2, columns, -LANE) + np.arange(LANE)
    last = np.concatenate([np.arange(cut, columns), rim])
    touched = np.concatenate([np.arange(cut, columns), np.arange(LANE // 2), np.arange(cut - LANE // 2, cut)])
    rowscan, column_first, column_last = [], [], []
    for sigma, sign in ((1.0, 1.0), (1.6, -1.0)):
        taps = gauss_taps(sigma)
        rowscan += two_parts(row_scan_table(band(taps, row_in, own), band(taps, near, block)))
        column_first += two_parts(sign * band(taps, np.arange(4 * LANE) - LANE, np.arange(2 * LANE)).T)
        column_last += two_parts(sign * band(taps, last, touched).T)
    level_rows = 2 * np.arange(LEVEL) - 4
    early = np.arange(LEVEL) == 0
    level = row_scan_table(
        band(BINOMIAL, row_in, level_rows) * ~early[:, None], band(BINOMIAL, near, 2 * np.arange(4)), early * 1.0
    )
    level = np.pad(level, ((0, BLOCK - 4 * LEVEL), (0, 0))).astype(ml_dtypes.bfloat16)
    edges = np.array([-4, -2, columns, columns + 2])
    targets = np.concatenate([2 * np.arange(columns // 2), edges])
    two = np.einsum(
        "yr,sbp->ysbrp",
        band(BINOMIAL, np.arange(LEVEL) - 2, 2 * np.arange(4)),
        band(BINOMIAL, np.arange(scans // 2), 2 * np.arange(scans // 4)).reshape(scans // 4, scans // 8, 4),
    ).reshape(scans, scans // 8, 4 * LEVEL)
    two = np.pad(two, ((0, 0), (0, 0), (0, BLOCK - 4 * LEVEL))).reshape(scans, scans // 8 * BLOCK)
    row, scan = np.divmod(np.arange(SLAB_ROWS // 2 * scans // 2), scans // 2)
    order = np.arange(scans // 8 * BLOCK)[None, :] == (scan // 4 * BLOCK + 4 * (row + 2) + scan % 4)[:, None]
    fill = ((0, 0), (0, LANE - 4))
    small = ml_dtypes.bfloat16
    return dict(
        rowscan=np.concatenate(rowscan + [level], 0),
        order=order.astype(small),
        column_first=np.stack(column_first),
        column_last=np.stack(column_last),
        level_first=np.pad(band(BINOMIAL, np.arange(cut), targets).T, fill).astype(small),
        level_last=np.pad(band(BINOMIAL, last, targets).T, fill).astype(small),
        two=two.astype(small),
        two_column=np.pad(band(BINOMIAL, targets // 2, 2 * np.arange(columns // 4)), fill).T.astype(small),
    )


def dot(left, right):
    return jnp.dot(left, right, preferred_element_type=F32)


def dot_rows(left, right):
    return lax.dot_general(left, right, (((1,), (1,)), ((), ())), preferred_element_type=F32)


def place_table(shift, slab, camera, owner):
    lanes = 4 * camera
    slot = lax.broadcasted_iota(jnp.int32, (PLACED, 1), 0)
    plane = slot & 3
    source = slab * SLAB_ROWS - RADIUS + (slot >> 2) - shift[:PLACED]
    wanted = jnp.where((source >= 0) & (source < camera), plane * camera + source, -1)
    lane = lax.broadcasted_iota(jnp.int32, (PLACED, lanes), 1)
    rows = jnp.where(lane == wanted, 1.0, 0.0).astype(BF16)
    slot = lax.broadcasted_iota(jnp.int32, (8, 1), 0)
    source = lax.broadcasted_iota(jnp.int32, (8, lanes), 1) - (slot & 3) * camera
    tap = source + shift[:8] - (slab * SLAB_ROWS - 6)
    inside = (source >= 0) & (source < camera) & ((slot >> 2) == owner) & (tap >= 0) & (tap < 5)
    weight = jnp.where(tap == 2, 6.0 / 16.0, jnp.where((tap == 1) | (tap == 3), 4.0 / 16.0, 1.0 / 16.0))
    return rows, jnp.where(inside, weight, 0.0).astype(BF16)


def place_tables(stack, pairs, shift, slab, camera, owner):
    for step in range(pairs):
        rows, early = place_table(shift, slab ^ (2 * step), camera, owner)
        stack[step * LANE : step * LANE + PLACED, :] = rows
        stack[step * LANE + PLACED : step * LANE + SLOTS, :] = early
        stack[step * LANE + SLOTS : (step + 1) * LANE, :] = jnp.zeros((LANE - SLOTS, 4 * camera), BF16)


def spread_shifts(values, slots):
    plane = lax.broadcasted_iota(jnp.int32, (slots, LANE), 0) & 3
    return jnp.where(plane < 2, jnp.where(plane == 0, values[0], values[1]), jnp.where(plane == 2, values[2], values[3]))


def strip_picks(widths, columns):
    tile = lax.axis_index("tile")
    tiles = lax.axis_size("tile")
    lane = lax.broadcasted_iota(jnp.int32, (8, columns), 1)
    line = lax.broadcasted_iota(jnp.int32, (8, columns), 0)
    right_width = widths[jnp.minimum(tile, tiles - 2)]
    left_width = widths[jnp.maximum(tile - 1, 0)]
    toward_right = jnp.where((lane == columns - right_width - 8 + line) & (line >= 2), 1.0, 0.0)
    toward_left = jnp.where((lane == left_width + line) & (line < 6), 1.0, 0.0)
    return jnp.concatenate([toward_right, toward_left], 0).astype(BF16)


def pack_own(raw_ref, shear_ref, width_ref, kept_ref, shift_ref, pick_ref, strip_ref, early_ref, *refs):
    out_refs, (shears, widths, sems, stack) = refs[:-4], refs[-4:]
    loads = [
        pltpu.make_async_copy(source, target, sems.at[index])
        for index, (source, target) in enumerate(((raw_ref, kept_ref), (shear_ref, shears), (width_ref, widths)))
    ]
    for load in loads:
        load.start()
    camera = raw_ref.shape[0] // 4
    columns = raw_ref.shape[1]
    slab = lax.axis_index("slab")
    for load in loads[1:]:
        load.wait()
    pick_ref[...] = strip_picks(widths, columns)
    shift_ref[...] = spread_shifts(shears, LANE)
    place_tables(stack, len(out_refs), shift_ref[:, :1], slab, camera, slab & 1)
    loads[0].wait()
    placed = dot(stack[...], kept_ref[:, : columns - LANE])
    for step, out_ref in enumerate(out_refs):
        out_ref[:PLACED, :] = placed[step * LANE : step * LANE + PLACED].astype(BF16)
        out_ref[PLACED:, :] = jnp.zeros((out_ref.shape[0] - PLACED, out_ref.shape[1]), BF16)
        early_ref[step] = placed[step * LANE + PLACED : step * LANE + SLOTS]
    strip_ref[...] = dot_rows(pick_ref[...], kept_ref[...])


def pack_other(other_ref, shear_ref, pick_ref, strip_ref, early_ref, *refs):
    (shears, sem, stack), refs = refs[-3:], refs[:-3]
    pairs = (len(refs) - 3) // 2
    (right_ref, left_ref, shift_ref), out_refs = refs[pairs : pairs + 3], refs[pairs + 3 :]
    load = pltpu.make_async_copy(shear_ref, shears, sem)
    load.start()
    camera = other_ref.shape[0] // 4
    columns = other_ref.shape[1]
    slab = lax.axis_index("slab")
    strips = jnp.concatenate([strip_ref[...], dot_rows(pick_ref[...], other_ref[...])], 0)
    right_ref[...] = jnp.concatenate([strips[:8], strips[16:24]], 0).astype(BF16)
    left_ref[...] = jnp.concatenate([strips[8:16], strips[24:]], 0).astype(BF16)
    load.wait()
    shift_ref[...] = spread_shifts(shears, LANE)
    place_tables(stack, pairs, shift_ref[:, :1], slab, camera, ~slab & 1)
    placed = dot(stack[...], other_ref[:, : columns - LANE])
    for step, out_ref in enumerate(out_refs):
        out_ref[PLACED : 2 * PLACED, :] = placed[step * LANE : step * LANE + PLACED].astype(BF16)
        out_ref[2 * PLACED :, :] = (early_ref[step] + placed[step * LANE + PLACED : step * LANE + SLOTS]).astype(BF16)


def stage(order_ref, *refs):
    sems, refs = refs[-1], refs[:-1]
    count = len(refs) // 2
    loads = [pltpu.make_async_copy(refs[index], refs[count + index], sems.at[index]) for index in range(count)]
    for load in loads:
        load.start()
    for load in loads:
        load.wait()


def pack_second(raw_ref, other_ref, shift_ref, other_shift_ref, from_left_ref, from_right_ref, order_ref, *out_refs):
    camera = raw_ref.shape[0] // 4
    columns = raw_ref.shape[1]
    slab = lax.axis_index("slab")
    tile = lax.axis_index("tile")
    right = jnp.where(tile < lax.axis_size("tile") - 1, from_right_ref[...].astype(F32), 0.0)
    left = jnp.where(tile > 0, from_left_ref[...].astype(F32), 0.0)
    for step, out_ref in enumerate(out_refs):
        total, placed = 0.0, []
        for owner, (planes_ref, shifts_ref) in enumerate(((raw_ref, shift_ref), (other_ref, other_shift_ref))):
            rows, early = place_table(shifts_ref[:, :1], slab ^ (2 * step), camera, (slab & 1) ^ owner)
            planes = planes_ref[:, columns - LANE :]
            out_ref[owner * PLACED : (owner + 1) * PLACED, :] = dot(rows, planes).astype(BF16)
            total = total + dot(early, planes)
            own = slice(8 * owner, 8 * owner + 8)
            strips = jnp.concatenate([right[own], left[own]], 0).astype(BF16)
            table = jnp.concatenate(
                [rows.astype(F32), early.astype(F32), jnp.zeros((LANE - SLOTS, rows.shape[1]), F32)], 0
            )
            columns_of = dot_rows(strips, table.astype(BF16))
            placed += [columns_of[:STRIP], columns_of[16 - STRIP :]]
        out_ref[2 * PLACED : 2 * PLACED + 8, :] = total.astype(BF16)
        out_ref[2 * PLACED + 8 :, :] = jnp.concatenate(placed, 0).astype(BF16)


def collect(in_refs, volume, scans):
    slab = lax.axis_index("slab")
    lanes = in_refs[0].shape[-1]
    groups = scans // 4
    outside = jnp.zeros((LANE,) + volume.shape[2:], BF16)
    volume[0] = outside
    volume[groups + 1] = outside
    for index in range(groups):
        group = (slab ^ index) + 1
        start = (index & 1) * PLACED
        volume[group, :PLACED, :lanes] = in_refs[index >> 1][start : start + PLACED, :]
        volume[group, PLACED:SLOTS, :lanes] = in_refs[index >> 1][2 * PLACED : 2 * PLACED + 8, :]
        volume[group, SLOTS:, :lanes] = jnp.zeros((LANE - SLOTS, lanes), BF16)


def split(value):
    high = value.astype(BF16)
    return high, (value - high.astype(F32)).astype(BF16)


def row_scan(rowscan_ref, volume, block, wide, rough):
    rows = 8 * SLAB_ROWS
    both = dot(rowscan_ref[...], volume[2 * block : 2 * block + 4].reshape(4 * LANE, volume.shape[-1]))
    for sigma in range(2):
        total = both[2 * sigma * rows : (2 * sigma + 1) * rows] + both[(2 * sigma + 1) * rows : (2 * sigma + 2) * rows]
        high, low = split(total)
        wide[2 * sigma, block * rows : (block + 1) * rows, :] = high
        wide[2 * sigma + 1, block * rows : (block + 1) * rows, :] = low
    rough[block * BLOCK : (block + 1) * BLOCK, :] = both[4 * rows :]


def dot_parts(high, low, right):
    both = dot(jnp.concatenate([high, low], 0), right)
    return both[: high.shape[0]] + both[high.shape[0] :]


def across(wide, rows, lanes, column_ref, taken):
    total = None
    for sigma in range(2):
        high, low = wide[2 * sigma, rows, lanes], wide[2 * sigma + 1, rows, lanes]
        table = column_ref[2 * sigma, taken]
        if rows == slice(None):
            right = jnp.concatenate([table, table, column_ref[2 * sigma + 1, taken]], 0)
            part = dot(jnp.concatenate([high, low, high], 1), right)
        else:
            part = dot(high, table) + dot(low, table) + dot(high, column_ref[2 * sigma + 1, taken])
        total = part if total is None else total + part
    return total


def level_part(rough, level_column_ref):
    high, low = split(rough[...])
    return dot_parts(high, low, level_column_ref[...])


def first_half(count, scans, rowscan_ref, column_ref, level_column_ref, *refs):
    in_refs, (partial_ref, coarse_ref, volume, wide, rough) = refs[:count], refs[count:]
    collect(in_refs, volume, scans)
    for block in range(scans // 8):
        row_scan(rowscan_ref, volume, block, wide, rough)
    cut = wide.shape[-1]
    for start in range(0, partial_ref.shape[1], 2 * LANE):
        low, high = max(start - LANE, 0), min(start + 3 * LANE, cut)
        taken = slice(low - start + LANE, high - start + LANE)
        partial_ref[:, start : start + 2 * LANE] = across(wide, slice(None), slice(low, high), column_ref, taken)
    coarse_ref[...] = level_part(rough, level_column_ref)


def second_half(count, scans, rowscan_ref, order_ref, column_ref, level_column_ref, two_ref, two_column_ref, *refs):
    partial_ref, coarse_ref, *in_refs = refs[: 2 + count]
    difference_ref, one_ref, second_ref, volume, strips, wide, rough, held, held_one, held_second, sems = refs[2 + count :]
    slab = lax.axis_index("slab")
    slabs = lax.axis_size("slab")
    tile = lax.axis_index("tile")
    tiles = lax.axis_size("tile")
    groups = scans // 4
    columns = partial_ref.shape[1]
    cut = columns - LANE
    collect(in_refs, volume, scans)
    for index in range(groups):
        place = pl.multiple_of((slab ^ index) * LANE, LANE)
        start = 2 * STRIP * (index & 1)
        both = in_refs[index >> 1][2 * PLACED + 8 :, :].astype(F32)[start : start + 2 * STRIP]
        both = jnp.concatenate([both, jnp.zeros((16 - 2 * STRIP, LANE), F32)], 0)
        strips[:, pl.ds(place, LANE)] = both.astype(BF16)
    line = lax.broadcasted_iota(jnp.int32, (16, LANE), 0)
    lane = lax.broadcasted_iota(jnp.int32, (16, LANE), 1)
    spread = jnp.where(lane == jnp.where(line < STRIP, line, line + LANE - 2 * STRIP), 1.0, 0.0).astype(BF16)
    rim = lax.dot_general(strips[...], spread, (((0,), (0,)), ((), ())), preferred_element_type=F32)
    volume[1 : groups + 1, :, LANE:] = rim.astype(BF16).reshape(groups, LANE, LANE)

    copies = []
    rows = 8 * SLAB_ROWS
    left = lax.broadcasted_iota(jnp.int32, (2 * rows, LANE), 1) < LANE // 2

    def keep(pair, start, total):
        total = total.reshape(2, SLAB_ROWS, 8, LANE)
        joined = jnp.concatenate([total[0], total[1]], 1)
        held[:, 16 * pair : 16 * pair + 16, start : start + LANE] = joined.astype(BF16)

    for pair in range(scans // 16):
        here = slice(2 * pair * rows, 2 * (pair + 1) * rows)
        for start in range(LANE, cut - LANE, LANE):
            keep(pair, start, partial_ref[here, start : start + LANE])
    for pair in range(scans // 16):
        for block in (2 * pair, 2 * pair + 1):
            row_scan(rowscan_ref, volume, block, wide, rough)
    for pair in range(scans // 16):
        here = slice(2 * pair * rows, 2 * (pair + 1) * rows)
        late = across(wide, here, slice(None), column_ref, slice(None))
        ends = late[:, LANE:]
        keep(pair, 0, partial_ref[here, :LANE] + jnp.where(left, ends, 0.0))
        keep(pair, cut - LANE, partial_ref[here, cut - LANE : cut] + jnp.where(left, 0.0, ends))
        keep(pair, cut, partial_ref[here, cut:] + late[:, :LANE])
        copy = pltpu.make_async_copy(
            held.at[:, 16 * pair : 16 * pair + 16, :], difference_ref.at[:, 16 * pair : 16 * pair + 16, :], sems.at[pair]
        )
        copy.start()
        copies.append(copy)
    level = coarse_ref[...] + level_part(rough, level_column_ref)
    half = columns // 2
    row = lax.broadcasted_iota(jnp.int32, level.shape, 0)
    within = row
    for block in range(1, scans // 8):
        within = within - jnp.where(row >= block * BLOCK, BLOCK, 0)
    row = slab * (SLAB_ROWS // 2) - 2 + (within >> 2)
    place = lax.broadcasted_iota(jnp.int32, level.shape, 1) - half
    keep = (row >= 0) & (row < slabs * (SLAB_ROWS // 2))
    keep = keep & ((place < 0) | (place >= 2) | (tile > 0)) & ((place < 2) | (tile < tiles - 1))
    ready = jnp.where(keep, level, 0.0).astype(BF16)
    held_one[...] = dot(order_ref[...], ready[:, :half]).reshape(held_one.shape).astype(BF16)
    copy = pltpu.make_async_copy(held_one, one_ref, sems.at[scans // 16])
    copy.start()
    copies.append(copy)

    high, low = split(dot(two_ref[...], ready))
    second = dot_parts(high, low, two_column_ref[...])
    held_second[...] = second.reshape(second_ref.shape).astype(BF16)
    copy = pltpu.make_async_copy(held_second, second_ref, sems.at[scans // 16 + 1])
    copy.start()
    copies.append(copy)

    for copy in copies:
        copy.wait()


VECTOR = pl.BlockSpec(memory_space=pltpu.VMEM)
ANYWHERE = pl.BlockSpec(memory_space=pl.ANY)
OUTSIDE = pl.BlockSpec(memory_space=pltpu.HBM)
PARAMS = pltpu.CompilerParams(vmem_limit_bytes=20 * 1024 * 1024)


def along(chunks, slabs):
    got = list(chunks)
    for step in sorted(range(1, len(chunks)), key=lambda step: (-(step & -step), step)):
        got[step] = lax.ppermute(chunks[step], "slab", [(i, i ^ (2 * step)) for i in range(slabs)])
    return got


def shifted(block, distance):
    count = lax.axis_size("tile")
    return lax.ppermute(block, "tile", [(i, (i + distance) % count) for i in range(count)])


def body(raw_stack, shear_offsets, intersection_widths):
    slabs = lax.axis_size("slab")
    planes, camera, columns = raw_stack.shape
    scans = planes * slabs
    cut = columns - LANE
    pairs = slabs // 2
    table = {name: jnp.asarray(value) for name, value in tables(scans, columns).items()}
    raw = raw_stack.reshape(planes * camera, columns)
    swap = [(i, i ^ 1) for i in range(slabs)]
    other = lax.ppermute(raw, "slab", swap)
    other_shear = lax.ppermute(shear_offsets, "slab", swap)
    outside = [pltpu.with_memory_space_constraint(each, pltpu.HBM) for each in (raw, shear_offsets, intersection_widths)]
    strip = jax.ShapeDtypeStruct((16, planes * camera), BF16)
    shift = jax.ShapeDtypeStruct((LANE, LANE), jnp.int32)
    raw, own_shift, pick, own_strip, early, *own = pl.pallas_call(
        pack_own,
        out_shape=[
            jax.ShapeDtypeStruct((planes * camera, columns), BF16),
            shift,
            jax.ShapeDtypeStruct((16, columns), BF16),
            jax.ShapeDtypeStruct((16, planes * camera), F32),
            jax.ShapeDtypeStruct((pairs, 8, cut), F32),
        ]
        + [jax.ShapeDtypeStruct((2 * PLACED + 8, cut), BF16)] * pairs,
        in_specs=[OUTSIDE] * 3,
        out_specs=[VECTOR] * (5 + pairs),
        scratch_shapes=[
            pltpu.SMEM(shear_offsets.shape, jnp.int32),
            pltpu.SMEM(intersection_widths.shape, jnp.int32),
            pltpu.SemaphoreType.DMA((3,)),
            pltpu.VMEM((pairs * LANE, planes * camera), BF16),
        ],
        compiler_params=PARAMS,
        name="pack_own",
    )(*outside)
    toward_right, toward_left, other_shift, *chunks = pl.pallas_call(
        pack_other,
        out_shape=[strip, strip, shift] + [jax.ShapeDtypeStruct((2 * PLACED + 8, cut), BF16)] * pairs,
        in_specs=[VECTOR, ANYWHERE] + [VECTOR] * (3 + pairs),
        out_specs=[VECTOR] * (3 + pairs),
        scratch_shapes=[
            pltpu.SMEM(shear_offsets.shape, jnp.int32),
            pltpu.SemaphoreType.DMA,
            pltpu.VMEM((pairs * LANE, planes * camera), BF16),
        ],
        input_output_aliases={5 + step: 3 + step for step in range(pairs)},
        compiler_params=PARAMS,
        name="pack_other",
    )(other, other_shear, pick, own_strip, early, *own)
    got_first = along(chunks, slabs)
    from_left = shifted(toward_right, 1)
    from_right = shifted(toward_left, -1)
    second = jax.ShapeDtypeStruct((2 * PLACED + 8 + 4 * STRIP, LANE), BF16)
    names = list(table)
    staged = pl.pallas_call(
        stage,
        out_shape=[jax.ShapeDtypeStruct(table[name].shape, BF16) for name in names],
        in_specs=[ANYWHERE] + [OUTSIDE] * len(names),
        out_specs=[VECTOR] * len(names),
        scratch_shapes=[pltpu.SemaphoreType.DMA((len(names),))],
        compiler_params=PARAMS,
        name="stage",
    )(toward_left, *[pltpu.with_memory_space_constraint(table[name], pltpu.HBM) for name in names])
    table = dict(zip(names, staged))
    chunks = pl.pallas_call(
        pack_second,
        out_shape=[second] * pairs,
        in_specs=[VECTOR] * 6 + [ANYWHERE],
        out_specs=[VECTOR] * pairs,
        compiler_params=PARAMS,
        name="pack_second",
    )(raw, other, own_shift, other_shift, from_left, from_right, table["two"])
    chunks, got_first[2] = lax.optimization_barrier((chunks, got_first[2]))
    got_second = along(chunks, slabs)
    partial, coarse = pl.pallas_call(
        functools.partial(first_half, pairs, scans),
        out_shape=[
            jax.ShapeDtypeStruct((scans * SLAB_ROWS, columns), F32),
            jax.ShapeDtypeStruct((scans // 8 * BLOCK, columns // 2 + LANE), F32),
        ],
        in_specs=[VECTOR] * (3 + pairs),
        out_specs=[VECTOR] * 2,
        scratch_shapes=[
            pltpu.VMEM((slabs + 2, LANE, cut), BF16),
            pltpu.VMEM((4, scans * SLAB_ROWS, cut), BF16),
            pltpu.VMEM((scans // 8 * BLOCK, cut), F32),
        ],
        compiler_params=PARAMS,
        name="first_half",
    )(table["rowscan"], table["column_first"], table["level_first"], *got_first)
    got_second, partial = lax.optimization_barrier((got_second, partial))
    return pl.pallas_call(
        functools.partial(second_half, pairs, scans),
        out_shape=[
            jax.ShapeDtypeStruct((SLAB_ROWS, scans, columns), BF16),
            jax.ShapeDtypeStruct((SLAB_ROWS // 2, scans // 2, columns // 2), BF16),
            jax.ShapeDtypeStruct((SLAB_ROWS // 4, scans // 4, columns // 4), BF16),
        ],
        in_specs=[VECTOR] * (8 + pairs),
        out_specs=[OUTSIDE] * 3,
        scratch_shapes=[
            pltpu.VMEM((slabs + 2, LANE, 2 * LANE), BF16),
            pltpu.VMEM((16, slabs * LANE), BF16),
            pltpu.VMEM((4, scans * SLAB_ROWS, 2 * LANE), BF16),
            pltpu.VMEM((scans // 8 * BLOCK, 2 * LANE), F32),
            pltpu.VMEM((SLAB_ROWS, scans, columns), BF16),
            pltpu.VMEM((SLAB_ROWS // 2, scans // 2, columns // 2), BF16),
            pltpu.VMEM((SLAB_ROWS // 4, scans // 4, columns // 4), BF16),
            pltpu.SemaphoreType.DMA((scans // 16 + 2,)),
        ],
        compiler_params=PARAMS,
        name="second_half",
    )(
        table["rowscan"],
        table["order"],
        table["column_last"],
        table["level_last"],
        table["two"],
        table["two_column"],
        partial,
        coarse,
        *got_second,
    )


def solution(mesh):
    placed = (P("slab", None, "tile"), P("slab"), P())
    return jax.shard_map(
        body,
        mesh=mesh,
        in_specs=placed,
        out_specs=(P("slab", None, "tile"), P("slab", None, "tile"), P("slab", None, "tile")),
        check_vma=False,
    )
```
